256 devices in a mesh: seq: 16 (over x, y), head: 16 (over z, core).
Axes of the slice: x: 4, y: 4, z: 8, core: 2. Of those that a mesh axis runs over, the one named last changes fastest.
Arguments:
- layer_input: bfloat16 [8192, 4096], P('seq', 'head'), may hold values from -40 to 40
- qk_weight: bfloat16 [4096, 4096], P('seq', 'head'), may hold values from -0.09375 to 0.09375
- value_weight: bfloat16 [4096, 4096], P('seq', 'head'), may hold values from -0.09375 to 0.09375
- groups: int32 [2, 8192, 1], P(None, 'seq'), may hold values from 0 to 15; in each aligned block of 512 rows (0 to 511, 512 to 1023, ..., all dimensions but the last counted through in order) at most 48 rows name the same one
- buckets: int32 [2, 8192], P(None, 'seq'), may hold values from 0 to 7
- out_cotangent: bfloat16 [8192, 4096], P('seq', 'head'), may hold values from -6 to 6
Outputs:
- output: bfloat16 [8192, 4096], P('seq', 'head')
- input_grad: bfloat16 [8192, 4096], P('seq', 'head')
- qk_weight_grad: float32 [4096, 4096], P('seq', 'head')
- value_weight_grad: float32 [4096, 4096], P('seq', 'head')
The draws below stay inside these ranges and needn't reach their ends.
Inputs may be any that keep to these rules, and one draw needn't show every extreme that they name: `groups`: among the 512 tokens of one device in one round no group is named more than 48 times, and in every draw some device's tokens name some group exactly 48 times.
All inputs are finite; a program needn't handle non-finite values.
Results may differ from the reference program's by a relative error of at most 0.018.
The reference program's roundings to bfloat16 on the way count: a program that leaves them out, or rounds other values in their place, can miss the bound.
Values may be sent and summed in bfloat16 or wider, within the bound.
A program may use at most 128 MiB of HBM per device.

```python
import math
import jax
import jax.numpy as jnp
import numpy as np
from jax import lax

D = 4096
HEADS = 32
HEAD_DIM = 128
ROUNDS = 2
BLOCK_LEN = 128
SUB_BUCKETS = 8
TOK_DEV = 512
TOKENS = 8192
GROUPS = 16
CAPACITY = 48
GROUP_SLOTS = 768
HEAD_SETS = 16
GROUP_HEADS = 2


def draw_layer_input(key, part):
    first = jax.random.fold_in(key, 0)
    gaussian = jax.random.normal(first, (TOKENS, D), jnp.float32)
    values = gaussian
    return jnp.clip(values, -40.0, 40.0).astype(jnp.bfloat16)


def with_ends(drawn, stream_key, low, high):
    longest = drawn.shape.index(max(drawn.shape))
    spots = []
    for shift in (0, 1):
        where = [jax.random.randint(jax.random.fold_in(stream_key, axis), (), 0, length) for axis, length in enumerate(drawn.shape)]
        where[longest] = (where[longest] + shift) % drawn.shape[longest]
        spots.append(tuple(where))
    return drawn.at[spots[0]].set(low).at[spots[1]].set(high)


def block_levels(key, dims, cuts, least, high):
    factor_of, own = 1.0, jax.random.fold_in(key, 6)
    for axis_at, shards_of in cuts:
        draws = jnp.exp(jax.random.uniform(jax.random.fold_in(own, axis_at), (shards_of,), jnp.float32, least / len(cuts), high / len(cuts)))
        factor_of = factor_of * jnp.repeat(draws, dims[axis_at] // shards_of).reshape([-1 if axis == axis_at else 1 for axis in range(len(dims))])
    return factor_of


def routed_block(own_key, own, number, rows, amount, top, limit, lean):
    order = jax.random.permutation(own_key, amount)
    packed, usual = load_shares(amount, rows * top, limit, lean, True), load_shares(amount, rows * top, limit, lean, False)
    places = jnp.arange(amount)

    def named(sizes, rotation):
        used = int((sizes > 0).sum())
        fixed = max(1, used // 4)
        moved = fixed + (places - fixed + rotation * (used - fixed)) % max(1, amount - fixed)
        return jnp.zeros((amount,), jnp.int32).at[order[jnp.where(places < fixed, places, moved)]].set(jnp.asarray(sizes, jnp.int32))

    sizes = jnp.where(number % 4 == 0, named(packed, number // 4), named(usual, number - number // 4 - 1))
    mixed = jax.random.permutation(jax.random.fold_in(own, 3), amount)
    source_of, taker = mixed[0:amount // 2 * 2:2], mixed[1:amount // 2 * 2:2]
    margin = jnp.minimum(sizes[source_of] - 1, limit - sizes[taker]) // 2
    margin = jnp.where((source_of == order[0]) | (taker == order[0]) | (sizes[taker] == 0), 0, jnp.maximum(margin, 0))
    moved = jax.random.randint(jax.random.fold_in(own, 4), (amount // 2,), 0, 1 << 20) % (margin + 1)
    sizes = sizes.at[source_of].add(-moved).at[taker].add(moved)
    labels = jnp.searchsorted(jnp.cumsum(sizes), jnp.arange(rows * top), side="right").astype(jnp.int32)
    grid = labels.reshape(top, rows).T
    grid = grid[jax.random.permutation(jax.random.fold_in(own, 1), rows)]
    rotation = jax.random.randint(jax.random.fold_in(own, 2), (rows, 1), 0, top)
    return jnp.take_along_axis(grid, (jnp.arange(top)[None, :] + rotation) % top, axis=1)


def load_shares(amount, total, reach, lean, full):
    loads = [(1 << 20) // math.isqrt(grade ** lean) + 1 for grade in range(1, amount + 1)]
    largest = reach if full else min(reach, max(-(-total // amount), total * loads[0] // sum(loads)))
    least = 1 if total - largest >= amount - 1 else 0
    given, rest = [largest] + [least] * (amount - 1), total - largest - least * (amount - 1)
    while rest > 0:
        free = [i for i in range(1, amount) if given[i] < largest] or [i for i in range(1, amount) if given[i] < reach]
        whole, remaining = sum([loads[i] for i in free]), rest
        for i in free:
            more = min(reach - given[i], max(1, remaining * loads[i] // whole), rest)
            given[i] = given[i] + more
            rest = rest - more
    return np.array(given)


def scatter_about(own_key, dims, scale, bound, shards=(), kind=jnp.bfloat16):
    drawn = jax.random.normal(own_key, dims, jnp.float32) * scale
    if len(shards) > 0:
        drawn = block_levels(own_key, dims, shards, -0.22, 0.18) * drawn
    return jnp.clip(drawn, min=-bound, max=bound).astype(kind)


def setup_inputs(seed: int = 0) -> dict:
    key_list = jax.random.split(jax.random.key(seed), 7)
    layer_input = draw_layer_input(jax.random.fold_in(key_list[6], 71), 0)
    qk_weight = scatter_about(key_list[1], (D, D), D ** -0.5, 0.09375, ((0, 16), (1, 16)))
    value_weight = scatter_about(key_list[2], (D, D), D ** -0.5, 0.09375, ((0, 16), (1, 16)))
    groups_keys = jax.random.split(jax.random.fold_in(key_list[3], 1), ROUNDS * TOKENS // TOK_DEV)
    groups_turns = jax.random.permutation(jax.random.fold_in(key_list[3], 3), ROUNDS * TOKENS // TOK_DEV)
    groups = jax.vmap(lambda own, number: routed_block(jax.random.fold_in(key_list[3], 2), own, number, TOK_DEV, GROUPS, 1, CAPACITY, 2))(groups_keys, groups_turns).reshape((ROUNDS, TOKENS, 1))
    buckets = with_ends(jax.random.randint(key_list[4], (ROUNDS, TOKENS), 0, SUB_BUCKETS), jax.random.fold_in(key_list[4], 1), 0, SUB_BUCKETS - 1).astype(jnp.int32)
    out_cotangent = scatter_about(key_list[5], (TOKENS, D), 1.0, 6.0, ((0, 16), (1, 16)))
    return dict(layer_input=layer_input, qk_weight=qk_weight, value_weight=value_weight, groups=groups, buckets=buckets, out_cotangent=out_cotangent)


EPSILON = 1e-06
SELF_SCORE = -100000.0
MASKED_SCORE = -1000000000.0

def widened(tensor):
    return lax.optimization_barrier(tensor.astype(jnp.bfloat16)).astype(jnp.float32)

def key_factor(query_f):
    return lax.rsqrt(lax.optimization_barrier(jnp.mean(query_f * query_f, axis=-1, keepdims=True)) + EPSILON) / math.sqrt(query_f.shape[-1])

def with_previous(blocked):
    return jnp.concatenate([blocked, jnp.roll(blocked, 1, axis=0)], axis=1)

def fold_previous(block_grads, block_width):
    return block_grads[:, :block_width] + jnp.roll(block_grads[:, block_width:], -1, axis=0)

def attention_rows(queries, values, live_slots):
    slot_total, heads_here, head_width = queries.shape
    blocks = slot_total // BLOCK_LEN
    query_f = queries.astype(jnp.float32)
    factor = key_factor(query_f)
    normed = widened(query_f * factor)
    query_blocks = query_f.reshape(blocks, BLOCK_LEN, heads_here, head_width)
    key_blocks = with_previous(normed.reshape(blocks, BLOCK_LEN, heads_here, head_width))
    value_blocks = with_previous(values.astype(jnp.float32).reshape(blocks, BLOCK_LEN, heads_here, head_width))
    live_keys = with_previous(live_slots.reshape(blocks, BLOCK_LEN))
    self_pairs = jnp.arange(BLOCK_LEN)[:, None] == jnp.arange(2 * BLOCK_LEN)[None, :]
    scores = jnp.einsum('nqhd,nkhd->nhqk', query_blocks, key_blocks)
    scores = jnp.where(self_pairs, SELF_SCORE, scores)
    scores = jnp.where(live_keys[:, None, None, :], scores, MASKED_SCORE)
    largest = lax.optimization_barrier(jnp.max(scores, axis=-1, keepdims=True))
    exponent = jnp.exp(scores - largest)
    row_total = lax.optimization_barrier(jnp.sum(exponent, axis=-1, keepdims=True))
    weights = exponent / row_total
    log_total = (largest + jnp.log(row_total))[..., 0]
    return (weights, log_total, query_blocks, key_blocks, value_blocks, self_pairs, factor)

def forward_rows(queries, values, live_slots):
    slot_total, heads_here, head_width = queries.shape
    weights, log_total, query_blocks, key_blocks, value_blocks, self_pairs, factor = attention_rows(queries, values, live_slots)
    mixed_rows = jnp.einsum('nhqk,nkhd->nqhd', widened(weights), value_blocks)
    return (mixed_rows.reshape(slot_total, heads_here, head_width), jnp.transpose(log_total, (0, 2, 1)).reshape(slot_total, heads_here))

def backward_rows(queries, values, live_slots, out_grads, mixes, inners):
    slot_total, heads_here, head_width = queries.shape
    blocks = slot_total // BLOCK_LEN
    weights, log_total, query_blocks, key_blocks, value_blocks, self_pairs, factor = attention_rows(queries, values, live_slots)
    mix_blocks = jnp.transpose(mixes.reshape(blocks, BLOCK_LEN, heads_here), (0, 2, 1))[..., None]
    inner_blocks = jnp.transpose(inners.reshape(blocks, BLOCK_LEN, heads_here), (0, 2, 1))[..., None]
    scaled = widened(weights * mix_blocks)
    grad_blocks = out_grads.astype(jnp.float32).reshape(blocks, BLOCK_LEN, heads_here, head_width)
    value_grads = fold_previous(jnp.einsum('nhqk,nqhd->nkhd', scaled, grad_blocks), BLOCK_LEN)
    pair_grads = jnp.einsum('nqhd,nkhd->nhqk', grad_blocks, value_blocks)
    score_grads = widened(jnp.where(self_pairs, 0.0, weights * mix_blocks * (pair_grads - inner_blocks)))
    query_part = jnp.einsum('nhqk,nkhd->nqhd', score_grads, key_blocks).reshape(slot_total, heads_here, head_width)
    key_part = fold_previous(jnp.einsum('nhqk,nqhd->nkhd', score_grads, query_blocks), BLOCK_LEN).reshape(slot_total, heads_here, head_width)
    query_f = queries.astype(jnp.float32)
    result = query_part + factor * key_part - factor * factor * factor * lax.optimization_barrier(jnp.sum(key_part * query_f, axis=-1, keepdims=True)) * query_f
    return (result.astype(jnp.bfloat16), value_grads.reshape(slot_total, heads_here, head_width).astype(jnp.bfloat16))

def layout(turn_groups, turn_buckets):
    token_total = turn_groups.shape[0]
    positions = jnp.arange(token_total, dtype=jnp.int32)
    sort_keys = turn_groups * (SUB_BUCKETS * token_total) + turn_buckets * token_total + positions
    ordering = jnp.argsort(sort_keys).astype(jnp.int32)
    one_hot = (turn_groups[:, None] == jnp.arange(GROUPS, dtype=jnp.int32)[None, :]).astype(jnp.int32)
    counts = lax.optimization_barrier(jnp.sum(one_hot, axis=0))
    starts = (jnp.cumsum(counts) - counts).astype(jnp.int32)
    sorted_groups = turn_groups[ordering]
    slot_index = (sorted_groups * GROUP_SLOTS + positions - starts[sorted_groups]).astype(jnp.int32)
    source_rows = jnp.full((GROUPS * GROUP_SLOTS,), token_total, jnp.int32).at[slot_index].set(ordering)
    token_slots = jnp.zeros((token_total,), jnp.int32).at[ordering].set(slot_index)
    return (source_rows, token_slots)

def spread(token_rows, source_rows):
    padded = jnp.concatenate([token_rows, jnp.zeros((1,) + token_rows.shape[1:], token_rows.dtype)], axis=0)
    return padded[source_rows]

def reference(layer_input, qk_weight, value_weight, groups, buckets, out_cotangent):
    token_total = layer_input.shape[0]
    queries = jnp.dot(layer_input, qk_weight, preferred_element_type=jnp.float32).astype(jnp.bfloat16).reshape(token_total, HEADS, HEAD_DIM)
    values = jnp.dot(layer_input, value_weight, preferred_element_type=jnp.float32).astype(jnp.bfloat16).reshape(token_total, HEADS, HEAD_DIM)
    layouts = [layout(groups[turn_index, :, 0], buckets[turn_index]) for turn_index in range(ROUNDS)]

    def grouped(token_rows, source_rows):
        return spread(token_rows, source_rows).reshape((GROUPS, GROUP_SLOTS) + token_rows.shape[1:])
    mixed_list = []
    log_list = []
    for turn_index in range(ROUNDS):
        source_rows, token_slots = layouts[turn_index]
        live_slots = (source_rows < token_total).reshape(GROUPS, GROUP_SLOTS)
        mixed_rows, log_total = lax.map(lambda group_item: forward_rows(group_item[0], group_item[1], group_item[2]), (grouped(queries, source_rows), grouped(values, source_rows), live_slots))
        mixed_list.append(mixed_rows.reshape(GROUPS * GROUP_SLOTS, HEADS, HEAD_DIM)[token_slots])
        log_list.append(log_total.reshape(GROUPS * GROUP_SLOTS, HEADS)[token_slots])
    turn_mixed = jnp.stack(mixed_list)
    turn_logs = jnp.stack(log_list)
    largest = lax.optimization_barrier(jnp.max(turn_logs, axis=0))
    log_all = largest + jnp.log(lax.optimization_barrier(jnp.sum(jnp.exp(turn_logs - largest), axis=0)))
    mix_weights = jnp.exp(turn_logs - log_all)
    combined = lax.optimization_barrier(jnp.sum(mix_weights[..., None] * turn_mixed, axis=0))
    output = combined.reshape(token_total, D).astype(jnp.bfloat16)
    out_grads = out_cotangent.reshape(token_total, HEADS, HEAD_DIM)
    out_inner = lax.optimization_barrier(jnp.sum(out_grads.astype(jnp.float32) * combined, axis=-1))
    query_sum = jnp.zeros((token_total, HEADS, HEAD_DIM), jnp.float32)
    value_sum = jnp.zeros((token_total, HEADS, HEAD_DIM), jnp.float32)
    for turn_index in range(ROUNDS):
        source_rows, token_slots = layouts[turn_index]
        live_slots = (source_rows < token_total).reshape(GROUPS, GROUP_SLOTS)
        inputs_here = (grouped(queries, source_rows), grouped(values, source_rows), live_slots, grouped(out_grads, source_rows), grouped(mix_weights[turn_index], source_rows), grouped(out_inner, source_rows))
        query_turn, value_turn = lax.map(lambda group_item: backward_rows(*group_item), inputs_here)
        query_sum = query_sum + query_turn.reshape(GROUPS * GROUP_SLOTS, HEADS, HEAD_DIM)[token_slots].astype(jnp.float32)
        value_sum = value_sum + value_turn.reshape(GROUPS * GROUP_SLOTS, HEADS, HEAD_DIM)[token_slots].astype(jnp.float32)
    query_grad = query_sum.reshape(token_total, D).astype(jnp.bfloat16)
    value_grad = value_sum.reshape(token_total, D).astype(jnp.bfloat16)
    set_width = GROUP_HEADS * HEAD_DIM

    def add_set(set_index, partial_sum):
        set_start = (set_index * set_width).astype(jnp.int32)
        query_cols = lax.dynamic_slice_in_dim(query_grad, set_start, set_width, 1)
        value_cols = lax.dynamic_slice_in_dim(value_grad, set_start, set_width, 1)
        qk_cols = lax.dynamic_slice_in_dim(qk_weight, set_start, set_width, 1)
        value_wcols = lax.dynamic_slice_in_dim(value_weight, set_start, set_width, 1)
        set_term = jnp.dot(query_cols, qk_cols.T, preferred_element_type=jnp.float32) + jnp.dot(value_cols, value_wcols.T, preferred_element_type=jnp.float32)
        return partial_sum + widened(set_term)
    input_sum = lax.fori_loop(0, HEAD_SETS, add_set, jnp.zeros((token_total, D), jnp.float32))
    input_grad = input_sum.astype(jnp.bfloat16)
    qk_weight_grad = jnp.dot(layer_input.T, query_grad, preferred_element_type=jnp.float32)
    value_weight_grad = jnp.dot(layer_input.T, value_grad, preferred_element_type=jnp.float32)
    return (output, input_grad, qk_weight_grad, value_weight_grad)
```

```python
import math

import jax
import jax.numpy as jnp
from jax import lax
from jax.experimental import pallas as pl
from jax.experimental.pallas import tpu as pltpu
from jax.sharding import PartitionSpec as P

HEAD_DIM = 128
ROUNDS = 2
BLOCK_LEN = 128
SUB_BUCKETS = 8


EPSILON = 1e-06
SELF_SCORE = -100000.0
MASKED_SCORE = -1000000000.0


MESH = pl.DeviceIdType.MESH
BF = jnp.bfloat16
F32 = jnp.float32


def rcopy(src, dst, ssem, rsem, dev):
    return pltpu.make_async_remote_copy(
        src_ref=src, dst_ref=dst, send_sem=ssem, recv_sem=rsem, device_id=dev, device_id_type=MESH
    )


class Sends:
    def __init__(self, sems):
        self.sems, self.used, self.open = sems, 0, []

    def start(self, src, dst, rsem, dev):
        copy = rcopy(src, dst, self.sems.at[self.used], rsem, dev)
        copy.start()
        self.used += 1
        self.open.append(copy)

    def finish(self):
        for copy in self.open:
            copy.wait_send()
        self.open = []


def arrived(ref, rsem, ssem, dev):
    rcopy(ref, ref, ssem, rsem, dev).wait_recv()


def place():
    s, h = lax.axis_index("seq"), lax.axis_index("head")
    return s, h, s // 4, s % 4, h // 2, h % 2


def enter(devices):
    barrier = pltpu.get_barrier_semaphore()
    for dev in devices:
        pl.semaphore_signal(barrier, inc=1, device_id=dev, device_id_type=MESH)
    pl.semaphore_wait(barrier, len(devices))


def ring_neighbours():
    s, h, x, y, z, c = place()
    east, west = (((x + 1) % 4) * 4 + y, h), (((x + 3) % 4) * 4 + y, h)
    north, south = (x * 4 + (y + 1) % 4, h), (x * 4 + (y + 3) % 4, h)
    up, down = (s, ((z + 1) % 8) * 2 + c), (s, ((z + 7) % 8) * 2 + c)
    twin = (s, 2 * z + 1 - c)
    return east, west, north, south, up, down, twin


def gather_kernel(x_ref, wq_ref, wv_ref, xg, wg, ssem, lsem, zsem, tsem, w1sem, w2sem):
    s, h, x, y, z, c = place()
    east, west, north, south, up, down, twin = ring_neighbours()
    local = [
        pltpu.make_async_copy(x_ref, xg.at[h], lsem.at[0]),
        pltpu.make_async_copy(wq_ref, wg.at[s, 0], lsem.at[1]),
        pltpu.make_async_copy(wv_ref, wg.at[s, 1], lsem.at[2]),
    ]
    for copy in local:
        copy.start()
    enter([east, west, north, south, up, down, twin])
    out = Sends(ssem)

    first_axis = [(north, south), (east, west)]
    second_axis = [(east, west), (north, south)]
    prim, sec = [y, x], [x, y]
    own = [wq_ref, wv_ref]

    def slot(j, p, r):
        return wg.at[r * 4 + p if j == 0 else p * 4 + r, j]

    def half(ref, k):
        return ref.at[pl.ds(128 * k, 128)]

    for j in (0, 1):
        plus, minus = first_axis[j]
        dst = slot(j, prim[j], sec[j])
        out.start(own[j], dst, w1sem.at[j, 0], plus)
        out.start(own[j], dst, w1sem.at[j, 1], minus)
    out.start(x_ref, xg.at[h], zsem.at[0, 0], up)
    out.start(x_ref, xg.at[h], zsem.at[1, 0], down)

    def second_send(j, k, p, src):
        plus, minus = second_axis[j]
        dst = slot(j, p, sec[j])
        out.start(src, dst, w2sem.at[j, k, 0], plus)
        out.start(src, dst, w2sem.at[j, k, 1], minus)

    for j in (0, 1):
        second_send(j, 0, prim[j], own[j])
    out.start(x_ref, xg.at[h], tsem.at[0, 0], twin)

    def first_arrivals(j):
        plus, minus = first_axis[j]
        for k, (step, onward) in enumerate(((3, plus), (1, minus))):
            p = (prim[j] + step) % 4
            ref = slot(j, p, sec[j])
            arrived(ref, w1sem.at[j, k], ssem.at[0], plus)
            out.start(half(ref, k), half(ref, k), w1sem.at[j, 2 + k], onward)
            second_send(j, 1 + k, p, ref)

    def first_far(j):
        p = (prim[j] + 2) % 4
        ref = slot(j, p, sec[j])
        for k in (0, 1):
            arrived(half(ref, k), w1sem.at[j, 2 + k], ssem.at[0], first_axis[j][0])
        second_send(j, 3, p, ref)

    offsets = (0, 3, 1, 2)

    def second_arrivals(j, k):
        p = (prim[j] + offsets[k]) % 4
        plus, minus = second_axis[j]
        for side, (step, onward) in enumerate(((3, plus), (1, minus))):
            ref = slot(j, p, (sec[j] + step) % 4)
            arrived(ref, w2sem.at[j, k, side], ssem.at[0], plus)
            out.start(half(ref, side), half(ref, side), w2sem.at[j, k, 2 + side], onward)

    def second_far(j, k):
        p = (prim[j] + offsets[k]) % 4
        ref = slot(j, p, (sec[j] + 2) % 4)
        for side in (0, 1):
            arrived(half(ref, side), w2sem.at[j, k, 2 + side], ssem.at[0], second_axis[j][0])

    def rows(ref, k):
        return ref.at[pl.ds(256 * k, 256)]

    def z_arrival(dist):
        for side, (step, onward) in enumerate(((8 - dist, up), (dist, down))):
            ref = xg.at[((z + step) % 8) * 2 + c]
            arrived(ref, zsem.at[side, dist - 1], ssem.at[0], up)
            if dist < 3:
                out.start(ref, ref, zsem.at[side, dist], onward)
            else:
                out.start(rows(ref, side), rows(ref, side), zsem.at[side, 3], onward)
            out.start(ref, ref, tsem.at[side, dist], twin)

    def z_far():
        ref = xg.at[((z + 4) % 8) * 2 + c]
        for side in (0, 1):
            arrived(rows(ref, side), zsem.at[side, 3], ssem.at[0], up)
            out.start(rows(ref, side), rows(ref, side), tsem.at[side, 4], twin)

    first_arrivals(0)
    first_arrivals(1)
    second_arrivals(0, 0)
    second_arrivals(1, 0)
    z_arrival(1)
    first_far(0)
    first_far(1)
    second_arrivals(0, 1)
    second_arrivals(1, 1)
    z_arrival(2)
    second_arrivals(0, 2)
    second_arrivals(1, 2)
    z_arrival(3)
    second_arrivals(0, 3)
    second_arrivals(1, 3)
    z_far()
    for k in range(4):
        second_far(0, k)
        second_far(1, k)
    arrived(xg.at[2 * z + 1 - c], tsem.at[0, 0], ssem.at[0], twin)
    for dist in (1, 2, 3):
        for side, step in enumerate((8 - dist, dist)):
            arrived(xg.at[((z + step) % 8) * 2 + 1 - c], tsem.at[side, dist], ssem.at[0], twin)
    for side in (0, 1):
        arrived(rows(xg.at[((z + 4) % 8) * 2 + 1 - c], side), tsem.at[side, 4], ssem.at[0], twin)
    for copy in local:
        copy.wait()
    out.finish()


def gather_all(layer_input, qk_weight, value_weight):
    anyspace = pl.BlockSpec(memory_space=pl.ANY)
    return pl.pallas_call(
        gather_kernel,
        out_shape=(
            jax.ShapeDtypeStruct((16, 512, 256), BF),
            jax.ShapeDtypeStruct((16, 2, 256, 256), BF),
        ),
        in_specs=[anyspace] * 3,
        out_specs=(anyspace, anyspace),
        scratch_shapes=[
            pltpu.SemaphoreType.DMA((64,)),
            pltpu.SemaphoreType.DMA((3,)),
            pltpu.SemaphoreType.DMA((2, 4)),
            pltpu.SemaphoreType.DMA((2, 5)),
            pltpu.SemaphoreType.DMA((2, 4)),
            pltpu.SemaphoreType.DMA((2, 4, 4)),
        ],
        compiler_params=pltpu.CompilerParams(collective_id=0, has_side_effects=True),
        name="gather_rings",
    )(layer_input, qk_weight, value_weight)


def mm(a, b, ca, cb):
    return lax.dot_general(a, b, (((ca,), (cb,)), ((), ())), preferred_element_type=F32)


def reduce_kernel(
    dqv, xg, wg, ig, gq, gv,
    tme, ttwin, tgot, zgot, gsum, g1far, g1near, g2far, g2near,
    ssem, tsem, zsem, s1sem, s2sem,
):
    s, h, x, y, z, c = place()
    east, west, north, south, up, down, twin = ring_neighbours()
    enter([east, west, north, south, up, down, twin])
    out = Sends(ssem)

    def term(b):
        return mm(dqv[:, 0:256], wg[b, 0], 1, 1) + mm(dqv[:, 256:512], wg[b, 1], 1, 1)

    def twin_term(k, zd):
        ttwin[zd] = term(2 * zd + 1 - c).astype(BF)
        out.start(ttwin.at[zd], tgot.at[zd], tsem.at[k], twin)

    def my_term(zd):
        tme[zd] = term(2 * zd + c).astype(BF)

    def pair(k, zd):
        arrived(tgot.at[zd], tsem.at[k], ssem.at[0], twin)
        tme[zd] = (tme[zd].astype(F32) + tgot[zd].astype(F32)).astype(BF)

    prim, sec = [x, y], [y, x]
    first_axis = [(east, west), (north, south)]
    second_axis = [(north, south), (east, west)]

    def grads(j, r):
        @pl.loop(0, 4)
        def _(p):
            b = r * 4 + p if j == 0 else p * 4 + r
            gsum[j, r, p] = mm(xg[b], dqv[:, 256 * j:256 * (j + 1)], 0, 0).astype(BF)

    order = (2, 1, 3, 0)

    def half(ref, k):
        return ref.at[pl.ds(128 * k, 128)]

    def first_far_send(j):
        r = (prim[j] + 2) % 4
        for k, off in enumerate(order):
            p = (sec[j] + off) % 4
            for side in (0, 1):
                out.start(
                    half(gsum.at[j, r, p], side), g1far.at[j, side, p], s1sem.at[j, k, side],
                    first_axis[j][side],
                )

    def first_near_send(j):
        for k, off in enumerate(order):
            p = (sec[j] + off) % 4
            for side, step in enumerate((1, 3)):
                r = (prim[j] + step) % 4
                arrived(g1far.at[j, side, p], s1sem.at[j, k, side], ssem.at[0], first_axis[j][0])
                rows = pl.ds(128 * side, 128)
                gsum[j, r, p, rows] = (
                    gsum[j, r, p, rows].astype(F32) + g1far[j, side, p].astype(F32)
                ).astype(BF)
                out.start(
                    gsum.at[j, r, p], g1near.at[j, side, p], s1sem.at[j, k, 2 + side],
                    first_axis[j][side],
                )

    def first_final(j, k):
        p = (sec[j] + order[k]) % 4
        for side in (0, 1):
            arrived(g1near.at[j, side, p], s1sem.at[j, k, 2 + side], ssem.at[0], first_axis[j][0])
        r = prim[j]
        gsum[j, r, p] = (
            gsum[j, r, p].astype(F32) + g1near[j, 0, p].astype(F32) + g1near[j, 1, p].astype(F32)
        ).astype(BF)

    def second_far_send(j):
        p = (sec[j] + 2) % 4
        for side in (0, 1):
            out.start(
                half(gsum.at[j, prim[j], p], side), g2far.at[j, side], s2sem.at[j, side],
                second_axis[j][side],
            )

    def second_near_send(j):
        for side, step in enumerate((1, 3)):
            p = (sec[j] + step) % 4
            arrived(g2far.at[j, side], s2sem.at[j, side], ssem.at[0], second_axis[j][0])
            rows = pl.ds(128 * side, 128)
            gsum[j, prim[j], p, rows] = (
                gsum[j, prim[j], p, rows].astype(F32) + g2far[j, side].astype(F32)
            ).astype(BF)
            out.start(
                gsum.at[j, prim[j], p], g2near.at[j, side], s2sem.at[j, 2 + side],
                second_axis[j][side],
            )

    def second_final(j, result):
        for side in (0, 1):
            arrived(g2near.at[j, side], s2sem.at[j, 2 + side], ssem.at[0], second_axis[j][0])
        result[...] = (
            gsum[j, prim[j], sec[j]].astype(F32)
            + g2near[j, 0].astype(F32)
            + g2near[j, 1].astype(F32)
        )

    def rows256(ref, k):
        return ref.at[pl.ds(256 * k, 256)]

    def z_send(step):
        if step == 0:
            zd = (z + 4) % 8
            for side, onward in enumerate((up, down)):
                out.start(
                    rows256(tme.at[zd], side), rows256(zgot.at[side, 0], side), zsem.at[side, 0],
                    onward,
                )
            return
        for side, (zd, onward) in enumerate((((z + 4 - step) % 8, up), ((z + 4 + step) % 8, down))):
            if step == 1:
                rows = pl.ds(256 * side, 256)
                arrived(zgot.at[side, 0, rows], zsem.at[side, 0], ssem.at[0], up)
                tme[zd, rows] = (
                    tme[zd, rows].astype(F32) + zgot[side, 0, rows].astype(F32)
                ).astype(BF)
            else:
                arrived(zgot.at[side, step - 1], zsem.at[side, step - 1], ssem.at[0], up)
                tme[zd] = (tme[zd].astype(F32) + zgot[side, step - 1].astype(F32)).astype(BF)
            out.start(tme.at[zd], zgot.at[side, step], zsem.at[side, step], onward)

    zorder = [(z + off) % 8 for off in (4, 3, 5, 2, 6, 1, 7, 0)]

    twin_term(0, zorder[0])
    for j in (0, 1):
        grads(j, (prim[j] + 2) % 4)
        first_far_send(j)
    my_term(zorder[0])
    pair(0, zorder[0])
    z_send(0)
    for k in (1, 2):
        twin_term(k, zorder[k])
        my_term(zorder[k])
    for j in (0, 1):
        grads(j, (prim[j] + 1) % 4)
        grads(j, (prim[j] + 3) % 4)
        first_near_send(j)
    pair(1, zorder[1])
    pair(2, zorder[2])
    z_send(1)
    for k in (3, 4, 5, 6, 7):
        twin_term(k, zorder[k])
        my_term(zorder[k])
    for j in (0, 1):
        grads(j, prim[j])
    pair(3, zorder[3])
    pair(4, zorder[4])
    z_send(2)
    for j in (0, 1):
        first_final(j, 0)
        second_far_send(j)
    pair(5, zorder[5])
    pair(6, zorder[6])
    z_send(3)
    for j in (0, 1):
        first_final(j, 1)
        first_final(j, 2)
        second_near_send(j)
        first_final(j, 3)
    pair(7, zorder[7])
    for side in (0, 1):
        arrived(zgot.at[side, 3], zsem.at[side, 3], ssem.at[0], up)
    ig[...] = (
        tme[z].astype(F32) + zgot[0, 3].astype(F32) + zgot[1, 3].astype(F32)
    ).astype(BF)
    second_final(0, gq)
    second_final(1, gv)
    out.finish()


def reduce_all(dqv, xg, wg):
    vm = pl.BlockSpec(memory_space=pltpu.VMEM)
    return pl.pallas_call(
        reduce_kernel,
        out_shape=(
            jax.ShapeDtypeStruct((512, 256), BF),
            jax.ShapeDtypeStruct((256, 256), F32),
            jax.ShapeDtypeStruct((256, 256), F32),
        ),
        in_specs=[vm] * 3,
        out_specs=(vm, vm, vm),
        scratch_shapes=[
            pltpu.VMEM((8, 512, 256), BF),
            pltpu.VMEM((8, 512, 256), BF),
            pltpu.VMEM((8, 512, 256), BF),
            pltpu.VMEM((2, 4, 512, 256), BF),
            pltpu.VMEM((2, 4, 4, 256, 256), BF),
            pltpu.VMEM((2, 2, 4, 128, 256), BF),
            pltpu.VMEM((2, 2, 4, 256, 256), BF),
            pltpu.VMEM((2, 2, 128, 256), BF),
            pltpu.VMEM((2, 2, 256, 256), BF),
            pltpu.SemaphoreType.DMA((64,)),
            pltpu.SemaphoreType.DMA((8,)),
            pltpu.SemaphoreType.DMA((2, 4)),
            pltpu.SemaphoreType.DMA((2, 4, 4)),
            pltpu.SemaphoreType.DMA((2, 4)),
        ],
        compiler_params=pltpu.CompilerParams(
            collective_id=1, has_side_effects=True, vmem_limit_bytes=56 * 1024 * 1024
        ),
        name="reduce_rings",
    )(dqv, xg, wg)


def key_factor(query_f):
    return lax.rsqrt(jnp.mean(query_f * query_f, axis=-1, keepdims=True) + EPSILON) / math.sqrt(
        query_f.shape[-1]
    )


def with_previous(blocked):
    return jnp.concatenate([blocked, jnp.roll(blocked, 1, axis=0)], axis=1)


def fold_previous(block_grads, block_width):
    return block_grads[:, :block_width] + jnp.roll(block_grads[:, block_width:], -1, axis=0)


def attention_rows(queries, values, live_slots):
    slot_total, heads_here, head_width = queries.shape
    blocks = slot_total // BLOCK_LEN
    query_f = queries.astype(jnp.float32)
    factor = key_factor(query_f)
    normed = (query_f * factor).astype(jnp.bfloat16)
    query_blocks = queries.reshape(blocks, BLOCK_LEN, heads_here, head_width)
    key_blocks = with_previous(normed.reshape(blocks, BLOCK_LEN, heads_here, head_width))
    value_blocks = with_previous(values.reshape(blocks, BLOCK_LEN, heads_here, head_width))
    live_keys = with_previous(live_slots.reshape(blocks, BLOCK_LEN))
    self_pairs = jnp.arange(BLOCK_LEN)[:, None] == jnp.arange(2 * BLOCK_LEN)[None, :]
    scores = jnp.einsum(
        "nqhd,nkhd->nhqk", query_blocks, key_blocks, preferred_element_type=jnp.float32
    )
    scores = jnp.where(self_pairs, SELF_SCORE, scores)
    scores = jnp.where(live_keys[:, None, None, :], scores, MASKED_SCORE)
    largest = jnp.max(scores, axis=-1, keepdims=True)
    exponent = jnp.exp(scores - largest)
    row_total = jnp.sum(exponent, axis=-1, keepdims=True)
    weights = exponent / row_total
    log_total = (largest + jnp.log(row_total))[..., 0]
    return (weights, log_total, query_blocks, key_blocks, value_blocks, self_pairs, factor)


def forward_rows(queries, values, live_slots):
    slot_total, heads_here, head_width = queries.shape
    weights, log_total, query_blocks, key_blocks, value_blocks, self_pairs, factor = attention_rows(
        queries, values, live_slots
    )
    mixed_rows = jnp.einsum(
        "nhqk,nkhd->nqhd",
        weights.astype(jnp.bfloat16),
        value_blocks,
        preferred_element_type=jnp.float32,
    )
    return (
        mixed_rows.reshape(slot_total, heads_here, head_width),
        jnp.transpose(log_total, (0, 2, 1)).reshape(slot_total, heads_here),
    )


def backward_rows(queries, values, live_slots, out_grads, mixes, inners):
    slot_total, heads_here, head_width = queries.shape
    blocks = slot_total // BLOCK_LEN
    weights, log_total, query_blocks, key_blocks, value_blocks, self_pairs, factor = attention_rows(
        queries, values, live_slots
    )
    mix_blocks = jnp.transpose(mixes.reshape(blocks, BLOCK_LEN, heads_here), (0, 2, 1))[..., None]
    inner_blocks = jnp.transpose(inners.reshape(blocks, BLOCK_LEN, heads_here), (0, 2, 1))[
        ..., None
    ]
    scaled = (weights * mix_blocks).astype(jnp.bfloat16)
    grad_blocks = out_grads.reshape(blocks, BLOCK_LEN, heads_here, head_width)
    value_grads = fold_previous(
        jnp.einsum("nhqk,nqhd->nkhd", scaled, grad_blocks, preferred_element_type=jnp.float32),
        BLOCK_LEN,
    )
    pair_grads = jnp.einsum(
        "nqhd,nkhd->nhqk", grad_blocks, value_blocks, preferred_element_type=jnp.float32
    )
    score_grads = jnp.where(
        self_pairs, 0.0, weights * mix_blocks * (pair_grads - inner_blocks)
    ).astype(jnp.bfloat16)
    query_part = jnp.einsum(
        "nhqk,nkhd->nqhd", score_grads, key_blocks, preferred_element_type=jnp.float32
    ).reshape(slot_total, heads_here, head_width)
    key_part = fold_previous(
        jnp.einsum(
            "nhqk,nqhd->nkhd", score_grads, query_blocks, preferred_element_type=jnp.float32
        ),
        BLOCK_LEN,
    ).reshape(slot_total, heads_here, head_width)
    query_f = queries.astype(jnp.float32)
    result = (
        query_part
        + factor * key_part
        - factor * factor * factor * jnp.sum(key_part * query_f, axis=-1, keepdims=True) * query_f
    )
    return (
        result.astype(jnp.bfloat16),
        value_grads.reshape(slot_total, heads_here, head_width).astype(jnp.bfloat16),
    )


def spread_rows(token_rows, source_rows):
    padded = jnp.concatenate(
        [token_rows, jnp.zeros((1,) + token_rows.shape[1:], token_rows.dtype)], axis=0
    )
    return padded[source_rows]


def per_device(layer_input, qk_weight, value_weight, groups, buckets, out_cotangent):
    tokens_here = layer_input.shape[0]
    width_here = layer_input.shape[1]
    heads_here = width_here // HEAD_DIM
    seq_count = lax.axis_size("seq")
    token_total = tokens_here * seq_count
    capacity = 3 * tokens_here // (2 * seq_count)
    slot_count = seq_count * capacity
    xg, wg = gather_all(layer_input, qk_weight, value_weight)
    projected = jnp.einsum("btd,bkdc->tkc", xg, wg, preferred_element_type=jnp.float32)
    queries = projected[:, 0].astype(jnp.bfloat16).reshape(tokens_here, heads_here, HEAD_DIM)
    values = projected[:, 1].astype(jnp.bfloat16).reshape(tokens_here, heads_here, HEAD_DIM)
    position = lax.axis_index("seq") * tokens_here + jnp.arange(tokens_here, dtype=jnp.int32)
    sentinel = SUB_BUCKETS * token_total
    source_list = []
    slot_list = []
    key_list = []
    for turn_index in range(ROUNDS):
        target = groups[turn_index, :, 0]
        one_hot = (target[:, None] == jnp.arange(seq_count, dtype=jnp.int32)[None, :]).astype(
            jnp.int32
        )
        dest_rank = jnp.sum(jnp.cumsum(one_hot, axis=0) * one_hot, axis=1) - 1
        slot_index = target * capacity + dest_rank
        source_list.append(
            jnp.full((slot_count,), tokens_here, jnp.int32)
            .at[slot_index]
            .set(jnp.arange(tokens_here, dtype=jnp.int32))
        )
        slot_list.append(slot_index)
        sort_keys = (
            jnp.full((slot_count,), sentinel, jnp.int32)
            .at[slot_index]
            .set(buckets[turn_index] * token_total + position)
        )
        key_list.append(sort_keys.reshape(seq_count, capacity))
    arrived_keys = lax.all_to_all(
        jnp.stack(key_list, axis=1), "seq", split_axis=0, concat_axis=0, tiled=True
    )
    orderings = []
    inverses = []
    live_list = []
    for turn_index in range(ROUNDS):
        received = arrived_keys[:, turn_index].reshape(slot_count)
        ordering = jnp.argsort(received, stable=True)
        orderings.append(ordering)
        inverses.append(jnp.argsort(ordering))
        live_list.append(received[ordering] < sentinel)

    def pack_rows(token_rows):
        return jnp.stack(
            [
                spread_rows(token_rows, source_list[turn_index]).reshape(
                    (seq_count, capacity) + token_rows.shape[1:]
                )
                for turn_index in range(ROUNDS)
            ],
            axis=1,
        )

    def sorted_rows(buffer, turn_index):
        return buffer[:, turn_index].reshape((slot_count,) + buffer.shape[3:])[
            orderings[turn_index]
        ]

    def unsorted(token_rows, turn_index):
        return token_rows[inverses[turn_index]].reshape(
            (seq_count, capacity) + token_rows.shape[1:]
        )

    def home_rows(buffer, turn_index):
        return buffer[:, turn_index].reshape((slot_count,) + buffer.shape[3:])[
            slot_list[turn_index]
        ]

    query_buffer = pack_rows(queries)
    value_buffer = pack_rows(values)
    got_queries, got_values = (
        lax.all_to_all(query_buffer, "seq", split_axis=0, concat_axis=0, tiled=True),
        lax.all_to_all(value_buffer, "seq", split_axis=0, concat_axis=0, tiled=True),
    )
    mixed_list = []
    log_list = []
    for turn_index in range(ROUNDS):
        mixed_rows, log_total = forward_rows(
            sorted_rows(got_queries, turn_index),
            sorted_rows(got_values, turn_index),
            live_list[turn_index],
        )
        mixed_list.append(unsorted(mixed_rows, turn_index))
        log_list.append(unsorted(log_total, turn_index))
    back_mixed, back_logs = (
        lax.all_to_all(
            jnp.stack(mixed_list, axis=1), "seq", split_axis=0, concat_axis=0, tiled=True
        ),
        lax.all_to_all(jnp.stack(log_list, axis=1), "seq", split_axis=0, concat_axis=0, tiled=True),
    )
    turn_mixed = jnp.stack([home_rows(back_mixed, turn_index) for turn_index in range(ROUNDS)])
    turn_logs = jnp.stack([home_rows(back_logs, turn_index) for turn_index in range(ROUNDS)])
    largest = jnp.max(turn_logs, axis=0)
    log_all = largest + jnp.log(jnp.sum(jnp.exp(turn_logs - largest), axis=0))
    mix_weights = jnp.exp(turn_logs - log_all)
    combined = jnp.sum(mix_weights[..., None] * turn_mixed, axis=0)
    output = combined.reshape(tokens_here, width_here).astype(jnp.bfloat16)
    out_grads = out_cotangent.reshape(tokens_here, heads_here, HEAD_DIM)
    out_inner = jnp.sum(out_grads.astype(jnp.float32) * combined, axis=-1)
    weight_buffer = jnp.stack(
        [
            spread_rows(mix_weights[turn_index], source_list[turn_index]).reshape(
                seq_count, capacity, heads_here
            )
            for turn_index in range(ROUNDS)
        ],
        axis=1,
    )
    inner_buffer = pack_rows(out_inner)
    got_mixes, got_inners = (
        lax.all_to_all(weight_buffer, "seq", split_axis=0, concat_axis=0, tiled=True),
        lax.all_to_all(inner_buffer, "seq", split_axis=0, concat_axis=0, tiled=True),
    )
    grad_buffer = pack_rows(out_grads)
    got_grads = lax.all_to_all(grad_buffer, "seq", split_axis=0, concat_axis=0, tiled=True)
    query_list = []
    value_list = []
    for turn_index in range(ROUNDS):
        query_turn, value_turn = backward_rows(
            sorted_rows(got_queries, turn_index),
            sorted_rows(got_values, turn_index),
            live_list[turn_index],
            sorted_rows(got_grads, turn_index),
            sorted_rows(got_mixes, turn_index),
            sorted_rows(got_inners, turn_index),
        )
        query_list.append(unsorted(query_turn, turn_index))
        value_list.append(unsorted(value_turn, turn_index))
    back_query, back_value = (
        lax.all_to_all(
            jnp.stack(query_list, axis=1), "seq", split_axis=0, concat_axis=0, tiled=True
        ),
        lax.all_to_all(
            jnp.stack(value_list, axis=1), "seq", split_axis=0, concat_axis=0, tiled=True
        ),
    )
    query_sum = home_rows(back_query, 0).astype(jnp.float32)
    value_sum = home_rows(back_value, 0).astype(jnp.float32)
    turn_index = 1
    query_sum = query_sum + home_rows(back_query, turn_index).astype(jnp.float32)
    value_sum = value_sum + home_rows(back_value, turn_index).astype(jnp.float32)
    query_grad = query_sum.reshape(tokens_here, width_here).astype(jnp.bfloat16)
    value_grad = value_sum.reshape(tokens_here, width_here).astype(jnp.bfloat16)
    return (output,) + reduce_all(
        jnp.concatenate((query_grad, value_grad), axis=1), xg, wg
    )


def solution(mesh):
    return jax.shard_map(
        per_device,
        mesh=mesh,
        in_specs=(
            P("seq", "head"),
            P("seq", "head"),
            P("seq", "head"),
            P(None, "seq", None),
            P(None, "seq"),
            P("seq", "head"),
        ),
        out_specs=(P("seq", "head"), P("seq", "head"), P("seq", "head"), P("seq", "head")),
        check_vma=False,
    )
```

```python
import math

import jax
import jax.numpy as jnp
from jax import lax
from jax.experimental import pallas as pl
from jax.experimental.pallas import tpu as pltpu
from jax.sharding import PartitionSpec as P

HEAD_DIM = 128
ROUNDS = 2
EPSILON = 1e-06
SELF_SCORE = -100000.0
MASKED_SCORE = -1000000000.0
MESH = pl.DeviceIdType.MESH
BF = jnp.bfloat16
F32 = jnp.float32


def rcopy(src, dst, ssem, rsem, dev):
    return pltpu.make_async_remote_copy(
        src_ref=src, dst_ref=dst, send_sem=ssem, recv_sem=rsem, device_id=dev, device_id_type=MESH
    )


class Sends:
    def __init__(self, sems):
        self.sems, self.used, self.open = sems, 0, []

    def start(self, src, dst, rsem, dev):
        copy = rcopy(src, dst, self.sems.at[self.used], rsem, dev)
        copy.start()
        self.used += 1
        self.open.append(copy)

    def finish(self):
        for copy in self.open:
            copy.wait_send()
        self.open = []


def arrived(ref, rsem, ssem, dev):
    rcopy(ref, ref, ssem, rsem, dev).wait_recv()


def place():
    s, h = lax.axis_index("seq"), lax.axis_index("head")
    return s, h, s // 4, s % 4, h // 2, h % 2


def enter(devices):
    barrier = pltpu.get_barrier_semaphore()
    for dev in devices:
        pl.semaphore_signal(barrier, inc=1, device_id=dev, device_id_type=MESH)
    pl.semaphore_wait(barrier, len(devices))


def ring_neighbours():
    s, h, x, y, z, c = place()
    east, west = (((x + 1) % 4) * 4 + y, h), (((x + 3) % 4) * 4 + y, h)
    north, south = (x * 4 + (y + 1) % 4, h), (x * 4 + (y + 3) % 4, h)
    up, down = (s, ((z + 1) % 8) * 2 + c), (s, ((z + 7) % 8) * 2 + c)
    twin = (s, 2 * z + 1 - c)
    return east, west, north, south, up, down, twin


def gather_kernel(x_ref, wq_ref, wv_ref, xg, wg, ssem, lsem, zsem, tsem, w1sem, w2sem):
    s, h, x, y, z, c = place()
    east, west, north, south, up, down, twin = ring_neighbours()
    local = [
        pltpu.make_async_copy(x_ref, xg.at[h], lsem.at[0]),
        pltpu.make_async_copy(wq_ref, wg.at[s, 0], lsem.at[1]),
        pltpu.make_async_copy(wv_ref, wg.at[s, 1], lsem.at[2]),
    ]
    for copy in local:
        copy.start()
    enter([east, west, north, south, up, down, twin])
    out = Sends(ssem)

    first_axis = [(north, south), (east, west)]
    second_axis = [(east, west), (north, south)]
    prim, sec = [y, x], [x, y]
    own = [wq_ref, wv_ref]

    def slot(j, p, r):
        return wg.at[r * 4 + p if j == 0 else p * 4 + r, j]

    def half(ref, k):
        return ref.at[pl.ds(128 * k, 128)]

    for j in (0, 1):
        plus, minus = first_axis[j]
        dst = slot(j, prim[j], sec[j])
        out.start(own[j], dst, w1sem.at[j, 0], plus)
        out.start(own[j], dst, w1sem.at[j, 1], minus)
    out.start(x_ref, xg.at[h], zsem.at[0, 0], up)
    out.start(x_ref, xg.at[h], zsem.at[1, 0], down)

    def second_send(j, k, p, src):
        plus, minus = second_axis[j]
        dst = slot(j, p, sec[j])
        out.start(src, dst, w2sem.at[j, k, 0], plus)
        out.start(src, dst, w2sem.at[j, k, 1], minus)

    for j in (0, 1):
        second_send(j, 0, prim[j], own[j])
    out.start(x_ref, xg.at[h], tsem.at[0, 0], twin)

    def first_arrivals(j):
        plus, minus = first_axis[j]
        for k, (step, onward) in enumerate(((3, plus), (1, minus))):
            p = (prim[j] + step) % 4
            ref = slot(j, p, sec[j])
            arrived(ref, w1sem.at[j, k], ssem.at[0], plus)
            out.start(half(ref, k), half(ref, k), w1sem.at[j, 2 + k], onward)
            second_send(j, 1 + k, p, ref)

    def first_far(j):
        p = (prim[j] + 2) % 4
        ref = slot(j, p, sec[j])
        for k in (0, 1):
            arrived(half(ref, k), w1sem.at[j, 2 + k], ssem.at[0], first_axis[j][0])
        second_send(j, 3, p, ref)

    offsets = (0, 3, 1, 2)

    def second_arrivals(j, k):
        p = (prim[j] + offsets[k]) % 4
        plus, minus = second_axis[j]
        for side, (step, onward) in enumerate(((3, plus), (1, minus))):
            ref = slot(j, p, (sec[j] + step) % 4)
            arrived(ref, w2sem.at[j, k, side], ssem.at[0], plus)
            out.start(half(ref, side), half(ref, side), w2sem.at[j, k, 2 + side], onward)

    def second_far(j, k):
        p = (prim[j] + offsets[k]) % 4
        ref = slot(j, p, (sec[j] + 2) % 4)
        for side in (0, 1):
            arrived(half(ref, side), w2sem.at[j, k, 2 + side], ssem.at[0], second_axis[j][0])

    def rows(ref, k):
        return ref.at[pl.ds(256 * k, 256)]

    def z_arrival(dist):
        for side, (step, onward) in enumerate(((8 - dist, up), (dist, down))):
            ref = xg.at[((z + step) % 8) * 2 + c]
            arrived(ref, zsem.at[side, dist - 1], ssem.at[0], up)
            if dist < 3:
                out.start(ref, ref, zsem.at[side, dist], onward)
            else:
                out.start(rows(ref, side), rows(ref, side), zsem.at[side, 3], onward)
            out.start(ref, ref, tsem.at[side, dist], twin)

    def z_far():
        ref = xg.at[((z + 4) % 8) * 2 + c]
        for side in (0, 1):
            arrived(rows(ref, side), zsem.at[side, 3], ssem.at[0], up)
            out.start(rows(ref, side), rows(ref, side), tsem.at[side, 4], twin)

    first_arrivals(0)
    first_arrivals(1)
    second_arrivals(0, 0)
    second_arrivals(1, 0)
    z_arrival(1)
    first_far(0)
    first_far(1)
    second_arrivals(0, 1)
    second_arrivals(1, 1)
    z_arrival(2)
    second_arrivals(0, 2)
    second_arrivals(1, 2)
    z_arrival(3)
    second_arrivals(0, 3)
    second_arrivals(1, 3)
    z_far()
    for k in range(4):
        second_far(0, k)
        second_far(1, k)
    arrived(xg.at[2 * z + 1 - c], tsem.at[0, 0], ssem.at[0], twin)
    for dist in (1, 2, 3):
        for side, step in enumerate((8 - dist, dist)):
            arrived(xg.at[((z + step) % 8) * 2 + 1 - c], tsem.at[side, dist], ssem.at[0], twin)
    for side in (0, 1):
        arrived(rows(xg.at[((z + 4) % 8) * 2 + 1 - c], side), tsem.at[side, 4], ssem.at[0], twin)
    for copy in local:
        copy.wait()
    out.finish()


def gather_all(layer_input, qk_weight, value_weight):
    anyspace = pl.BlockSpec(memory_space=pl.ANY)
    return pl.pallas_call(
        gather_kernel,
        out_shape=(
            jax.ShapeDtypeStruct((16, 512, 256), BF),
            jax.ShapeDtypeStruct((16, 2, 256, 256), BF),
        ),
        in_specs=[anyspace] * 3,
        out_specs=(anyspace, anyspace),
        scratch_shapes=[
            pltpu.SemaphoreType.DMA((64,)),
            pltpu.SemaphoreType.DMA((3,)),
            pltpu.SemaphoreType.DMA((2, 4)),
            pltpu.SemaphoreType.DMA((2, 5)),
            pltpu.SemaphoreType.DMA((2, 4)),
            pltpu.SemaphoreType.DMA((2, 4, 4)),
        ],
        compiler_params=pltpu.CompilerParams(collective_id=0, has_side_effects=True),
        name="gather_rings",
    )(layer_input, qk_weight, value_weight)


def mm(a, b, ca, cb):
    return lax.dot_general(a, b, (((ca,), (cb,)), ((), ())), preferred_element_type=F32)


def reduce_kernel(
    dqv, xg, wg, ig, gq, gv,
    tme, ttwin, tgot, zgot, gsum, g1far, g1near, g2far, g2near,
    ssem, tsem, zsem, s1sem, s2sem,
):
    s, h, x, y, z, c = place()
    east, west, north, south, up, down, twin = ring_neighbours()
    enter([east, west, north, south, up, down, twin])
    out = Sends(ssem)

    def term(b):
        return mm(dqv[:, 0:256], wg[b, 0], 1, 1) + mm(dqv[:, 256:512], wg[b, 1], 1, 1)

    def twin_term(k, zd):
        ttwin[zd] = term(2 * zd + 1 - c).astype(BF)
        out.start(ttwin.at[zd], tgot.at[zd], tsem.at[k], twin)

    def my_term(zd):
        tme[zd] = term(2 * zd + c).astype(BF)

    def pair(k, zd):
        arrived(tgot.at[zd], tsem.at[k], ssem.at[0], twin)
        tme[zd] = (tme[zd].astype(F32) + tgot[zd].astype(F32)).astype(BF)

    prim, sec = [x, y], [y, x]
    first_axis = [(east, west), (north, south)]
    second_axis = [(north, south), (east, west)]

    def grads(j, r):
        @pl.loop(0, 4)
        def _(p):
            b = r * 4 + p if j == 0 else p * 4 + r
            gsum[j, r, p] = mm(xg[b], dqv[:, 256 * j:256 * (j + 1)], 0, 0).astype(BF)

    order = (2, 1, 3, 0)

    def half(ref, k):
        return ref.at[pl.ds(128 * k, 128)]

    def first_far_send(j):
        r = (prim[j] + 2) % 4
        for k, off in enumerate(order):
            p = (sec[j] + off) % 4
            for side in (0, 1):
                out.start(
                    half(gsum.at[j, r, p], side), g1far.at[j, side, p], s1sem.at[j, k, side],
                    first_axis[j][side],
                )

    def first_near_send(j):
        for k, off in enumerate(order):
            p = (sec[j] + off) % 4
            for side, step in enumerate((1, 3)):
                r = (prim[j] + step) % 4
                arrived(g1far.at[j, side, p], s1sem.at[j, k, side], ssem.at[0], first_axis[j][0])
                rows = pl.ds(128 * side, 128)
                gsum[j, r, p, rows] = (
                    gsum[j, r, p, rows].astype(F32) + g1far[j, side, p].astype(F32)
                ).astype(BF)
                out.start(
                    gsum.at[j, r, p], g1near.at[j, side, p], s1sem.at[j, k, 2 + side],
                    first_axis[j][side],
                )

    def first_final(j, k):
        p = (sec[j] + order[k]) % 4
        for side in (0, 1):
            arrived(g1near.at[j, side, p], s1sem.at[j, k, 2 + side], ssem.at[0], first_axis[j][0])
        r = prim[j]
        gsum[j, r, p] = (
            gsum[j, r, p].astype(F32) + g1near[j, 0, p].astype(F32) + g1near[j, 1, p].astype(F32)
        ).astype(BF)

    def second_far_send(j):
        p = (sec[j] + 2) % 4
        for side in (0, 1):
            out.start(
                half(gsum.at[j, prim[j], p], side), g2far.at[j, side], s2sem.at[j, side],
                second_axis[j][side],
            )

    def second_near_send(j):
        for side, step in enumerate((1, 3)):
            p = (sec[j] + step) % 4
            arrived(g2far.at[j, side], s2sem.at[j, side], ssem.at[0], second_axis[j][0])
            rows = pl.ds(128 * side, 128)
            gsum[j, prim[j], p, rows] = (
                gsum[j, prim[j], p, rows].astype(F32) + g2far[j, side].astype(F32)
            ).astype(BF)
            out.start(
                gsum.at[j, prim[j], p], g2near.at[j, side], s2sem.at[j, 2 + side],
                second_axis[j][side],
            )

    def second_final(j, result):
        for side in (0, 1):
            arrived(g2near.at[j, side], s2sem.at[j, 2 + side], ssem.at[0], second_axis[j][0])
        result[...] = (
            gsum[j, prim[j], sec[j]].astype(F32)
            + g2near[j, 0].astype(F32)
            + g2near[j, 1].astype(F32)
        )

    def rows256(ref, k):
        return ref.at[pl.ds(256 * k, 256)]

    def z_send(step):
        if step == 0:
            zd = (z + 4) % 8
            for side, onward in enumerate((up, down)):
                out.start(
                    rows256(tme.at[zd], side), rows256(zgot.at[side, 0], side), zsem.at[side, 0],
                    onward,
                )
            return
        for side, (zd, onward) in enumerate((((z + 4 - step) % 8, up), ((z + 4 + step) % 8, down))):
            if step == 1:
                rows = pl.ds(256 * side, 256)
                arrived(zgot.at[side, 0, rows], zsem.at[side, 0], ssem.at[0], up)
                tme[zd, rows] = (
                    tme[zd, rows].astype(F32) + zgot[side, 0, rows].astype(F32)
                ).astype(BF)
            else:
                arrived(zgot.at[side, step - 1], zsem.at[side, step - 1], ssem.at[0], up)
                tme[zd] = (tme[zd].astype(F32) + zgot[side, step - 1].astype(F32)).astype(BF)
            out.start(tme.at[zd], zgot.at[side, step], zsem.at[side, step], onward)

    zorder = [(z + off) % 8 for off in (4, 3, 5, 2, 6, 1, 7, 0)]

    twin_term(0, zorder[0])
    for j in (0, 1):
        grads(j, (prim[j] + 2) % 4)
        first_far_send(j)
    my_term(zorder[0])
    pair(0, zorder[0])
    z_send(0)
    for k in (1, 2):
        twin_term(k, zorder[k])
        my_term(zorder[k])
    for j in (0, 1):
        grads(j, (prim[j] + 1) % 4)
        grads(j, (prim[j] + 3) % 4)
        first_near_send(j)
    pair(1, zorder[1])
    pair(2, zorder[2])
    z_send(1)
    for k in (3, 4, 5, 6, 7):
        twin_term(k, zorder[k])
        my_term(zorder[k])
    for j in (0, 1):
        grads(j, prim[j])
    pair(3, zorder[3])
    pair(4, zorder[4])
    z_send(2)
    for j in (0, 1):
        first_final(j, 0)
        second_far_send(j)
    pair(5, zorder[5])
    pair(6, zorder[6])
    z_send(3)
    for j in (0, 1):
        first_final(j, 1)
        first_final(j, 2)
        second_near_send(j)
        first_final(j, 3)
    pair(7, zorder[7])
    for side in (0, 1):
        arrived(zgot.at[side, 3], zsem.at[side, 3], ssem.at[0], up)
    ig[...] = (
        tme[z].astype(F32) + zgot[0, 3].astype(F32) + zgot[1, 3].astype(F32)
    ).astype(BF)
    second_final(0, gq)
    second_final(1, gv)
    out.finish()


def reduce_all(dqv, xg, wg):
    vm = pl.BlockSpec(memory_space=pltpu.VMEM)
    return pl.pallas_call(
        reduce_kernel,
        out_shape=(
            jax.ShapeDtypeStruct((512, 256), BF),
            jax.ShapeDtypeStruct((256, 256), F32),
            jax.ShapeDtypeStruct((256, 256), F32),
        ),
        in_specs=[vm] * 3,
        out_specs=(vm, vm, vm),
        scratch_shapes=[
            pltpu.VMEM((8, 512, 256), BF),
            pltpu.VMEM((8, 512, 256), BF),
            pltpu.VMEM((8, 512, 256), BF),
            pltpu.VMEM((2, 4, 512, 256), BF),
            pltpu.VMEM((2, 4, 4, 256, 256), BF),
            pltpu.VMEM((2, 2, 4, 128, 256), BF),
            pltpu.VMEM((2, 2, 4, 256, 256), BF),
            pltpu.VMEM((2, 2, 128, 256), BF),
            pltpu.VMEM((2, 2, 256, 256), BF),
            pltpu.SemaphoreType.DMA((64,)),
            pltpu.SemaphoreType.DMA((8,)),
            pltpu.SemaphoreType.DMA((2, 4)),
            pltpu.SemaphoreType.DMA((2, 4, 4)),
            pltpu.SemaphoreType.DMA((2, 4)),
        ],
        compiler_params=pltpu.CompilerParams(
            collective_id=1, has_side_effects=True, vmem_limit_bytes=56 * 1024 * 1024
        ),
        name="reduce_rings",
    )(dqv, xg, wg)


def iota(shape, axis):
    return lax.broadcasted_iota(jnp.int32, shape, axis).astype(F32)


def onehot(mask):
    return jnp.where(mask, 1.0, 0.0).astype(BF)


def split3(v):
    high = v.astype(BF).astype(F32)
    rest = v - high
    mid = rest.astype(BF).astype(F32)
    return high, mid, rest - mid


def pieces(v):
    return jnp.concatenate(split3(v), axis=0).astype(BF)


def fold3(v, n):
    return v[0:n] + v[n:2 * n] + v[2 * n:3 * n]


def middle_kernel(
    xg, wg, dout, grow, brow, dqv, output,
    proj, qv, pick, unpick, order, unorder, live, hot, rk,
    kbuf, kgot, sbuf, rbuf, dbuf, dgot, obuf, ogot, gbuf, ggot, lbuf, lgot, mbuf, mgot,
    qs, ks, vs, ds_, facs, probs, pairs, osum, vals, slots, cols, dks, dvs, mixes,
    ssem, rsem,
):
    s, h, x, y, z, c = place()
    barrier = pltpu.get_barrier_semaphore()

    @pl.loop(1, 16)
    def _(k):
        pl.semaphore_signal(barrier, inc=1, device_id=((s + k) % 16, h), device_id_type=MESH)

    pl.semaphore_wait(barrier, 15)

    def post(n, src, dst):
        @pl.loop(1, 16)
        def _(k):
            d = (s + k) % 16
            rcopy(src.at[d], dst.at[s], ssem.at[n], rsem.at[n], (d, h)).start()

        dst[s] = src[s]

    def collect(n, dst):
        part = dst.at[pl.ds(0, 15)]
        rcopy(part, part, ssem.at[n], rsem.at[n], (s, h)).wait_recv()

    def sent(n, src):
        part = src.at[pl.ds(0, 15)]
        rcopy(part, part, ssem.at[n], rsem.at[n], (s, h)).wait_send()

    kbuf[...] = jnp.zeros_like(kbuf)
    lbuf[...] = jnp.zeros_like(lbuf)
    vals[...] = jnp.zeros_like(vals)
    slots[...] = jnp.zeros_like(slots)
    upper = onehot(iota((512, 512), 0) <= iota((512, 512), 1))
    eye = iota((512, 512), 0) == iota((512, 512), 1)
    for t in (0, 1):
        g = grow[t:t + 1, :].astype(F32)
        member = jnp.where(iota((16, 512), 0) == g, 1.0, 0.0)
        count = mm(member.astype(BF), upper, 1, 0)
        rank = jnp.sum(member * count, axis=0, keepdims=True) - 1.0
        slot = g * 48.0 + rank
        slot_col = jnp.sum(jnp.where(eye, slot, 0.0), axis=1, keepdims=True)
        hot[t] = member
        rk[t] = onehot(iota((128, 512), 0) == rank)
        pick[t] = onehot(iota((768, 512), 0) == slot)
        unpick[:, 768 * t:768 * (t + 1)] = onehot(iota((512, 768), 1) == slot_col)
        named = member * (brow[t:t + 1, :].astype(F32) + 1.0)
        sent_keys = mm(named.astype(BF), rk[t], 1, 1)
        for d in range(16):
            kbuf[d, t:t + 1, :] = sent_keys[d:d + 1, :]
    post(0, kbuf, kgot)

    proj[...] = jnp.zeros_like(proj)

    @pl.loop(0, 4)
    def _(i):
        for j in (0, 1):
            total = proj[j]
            for k in range(4):
                b = 4 * i + k
                total += mm(xg[b], wg[b, j], 1, 0)
            proj[j] = total

    for j in (0, 1):
        for n in (0, 1):
            qv[n, :, 128 * j:128 * (j + 1)] = proj[j, :, 128 * n:128 * (n + 1)].astype(BF)

    for n in (0, 1):
        for t in (0, 1):
            sbuf[n, :, t] = mm(pick[t], qv[n], 1, 0).astype(BF).reshape(16, 48, 256)
        post(1 + n, sbuf.at[n], rbuf.at[n])
    for t in (0, 1):
        dbuf[:, t] = mm(pick[t], dout[...], 1, 0).astype(BF).reshape(16, 48, 256)
    post(3, dbuf, dgot)

    collect(0, kgot)
    for t in (0, 1):
        tag = jnp.concatenate([kgot[d, t:t + 1, :] for d in range(16)], axis=0)
        usable = iota((16, 128), 1) < 48.0
        kinds = [jnp.where(tag == float(k), 1.0, 0.0) for k in range(1, 9)]
        kinds.append(jnp.where(usable, jnp.where(tag == 0.0, 1.0, 0.0), 0.0))
        stack = jnp.concatenate(kinds, axis=0)
        within = mm(stack.astype(BF), onehot(iota((128, 128), 0) <= iota((128, 128), 1)), 1, 0)
        totals = jnp.broadcast_to(within[:, 127:128], (144, 128)).astype(BF)
        before = mm(onehot(iota((144, 144), 0) > iota((144, 144), 1)), totals, 1, 0)
        place_all = stack * (within + before - 1.0)
        rank = place_all[0:16]
        for k in range(1, 9):
            rank = rank + place_all[16 * k:16 * (k + 1)]
        live[t] = before[128:136, :]
        small_eye = iota((48, 128), 0) == iota((48, 128), 1)
        columns = jnp.concatenate(
            [
                jnp.sum(jnp.where(small_eye, rank[d:d + 1, :], 0.0), axis=1, keepdims=True)
                for d in range(16)
            ],
            axis=0,
        )
        unorder[t] = onehot(iota((768, 768), 1) == columns)
        row = jnp.sum(
            jnp.where(iota((768, 768), 0) == iota((768, 768), 1), columns, 0.0),
            axis=0, keepdims=True,
        )
        order[t] = onehot(iota((768, 768), 0) == row)

    def both(ref, lead, b):
        prev = (b + 5) % 6
        return jnp.concatenate(
            [ref[lead, 128 * b:128 * (b + 1)], ref[lead, 128 * prev:128 * (prev + 1)]], axis=0
        )

    self_pair = iota((128, 256), 0) == iota((128, 256), 1)

    for n in (0, 1):
        collect(1 + n, rbuf.at[n])

        @pl.loop(0, 2)
        def _(t):
            u = 2 * n + t
            rows = mm(order[t], rbuf[n, :, t].reshape(768, 256), 1, 0)
            qf = rows[:, 0:128]
            fac = lax.rsqrt(jnp.mean(qf * qf, axis=1, keepdims=True) + EPSILON) / math.sqrt(HEAD_DIM)
            facs[u] = jnp.broadcast_to(fac, (768, 128))
            qs[u] = qf.astype(BF)
            ks[u] = (qf * fac).astype(BF)
            vs[u] = rows[:, 128:256].astype(BF)
            for b in range(6):
                prev = (b + 5) % 6
                at = iota((1, 256), 1)
                at = jnp.where(at < 128.0, at + 128.0 * b, at - 128.0 + 128.0 * prev)
                used = jnp.concatenate([live[t, 0:1, :]] * 2, axis=1)
                scores = mm(qs[u, 128 * b:128 * (b + 1)], both(ks, u, b), 1, 1)
                scores = jnp.where(self_pair, SELF_SCORE, scores)
                scores = jnp.where(at < used, scores, MASKED_SCORE)
                top = jnp.max(scores, axis=1, keepdims=True)
                e = jnp.exp(scores - top)
                total = jnp.sum(e, axis=1, keepdims=True)
                weights = e * (1.0 / total)
                probs[u, b] = weights
                osum[u, 128 * b:128 * (b + 1)] = mm(weights.astype(BF), both(vs, u, b), 1, 0)
                vals[t, 128 * b:128 * (b + 1), n:n + 1] = top + jnp.log(total)

    collect(3, dgot)

    @pl.loop(0, 2)
    def _(t):
        rows = mm(order[t], dgot[:, t].reshape(768, 256), 1, 0)
        for n in (0, 1):
            u = 2 * n + t
            part = rows[:, 128 * n:128 * (n + 1)]
            ds_[u] = part.astype(BF)
            vals[t, :, 2 + n:3 + n] = jnp.sum(part * osum[u], axis=1, keepdims=True)
            for b in range(6):
                pairs[u, b] = mm(ds_[u, 128 * b:128 * (b + 1)], both(vs, u, b), 1, 1)

    for t in (0, 1):
        choose = onehot(iota((8, 128), 0) == iota((8, 128), 1))
        high, mid, low = split3(vals[t])
        lines = (
            mm(choose, high.astype(BF), 1, 1)
            + mm(choose, mid.astype(BF), 1, 1)
            + mm(choose, low.astype(BF), 1, 1)
        )
        lines = pieces(lines)
        for d in range(16):
            lbuf[d, 8 * t:8 * (t + 1), 0:48] = fold3(
                mm(lines, unorder[t, 48 * d:48 * (d + 1)], 1, 1), 8
            )
    post(4, lbuf, lgot)
    for t in (0, 1):
        wide = jnp.concatenate([osum[t], osum[2 + t]], axis=1).astype(BF)
        obuf[:, t] = mm(unorder[t], wide, 1, 0).astype(BF).reshape(16, 48, 256)
    post(5, obuf, ogot)

    collect(4, lgot)
    here = []
    for t in (0, 1):
        high, mid, low = split3(lgot[:, 8 * t:8 * (t + 1), :].reshape(128, 128))
        found = (
            mm(high.astype(BF), rk[t], 1, 0)
            + mm(mid.astype(BF), rk[t], 1, 0)
            + mm(low.astype(BF), rk[t], 1, 0)
        )
        line = found[0:8] * hot[t, 0:1, :]
        for g in range(1, 16):
            line = line + found[8 * g:8 * (g + 1)] * hot[t, g:g + 1, :]
        here.append(line)
    top = jnp.maximum(here[0], here[1])
    log_all = top + jnp.log(jnp.exp(here[0] - top) + jnp.exp(here[1] - top))
    mix = [jnp.exp(line - log_all) for line in here]
    inner = mix[0][0:2] * here[0][2:4] + mix[1][0:2] * here[1][2:4]
    for t in (0, 1):
        lines = jnp.concatenate([mix[t][0:2], inner, jnp.zeros((4, 512), F32)], axis=0)
        split = jnp.concatenate(split3(lines), axis=0)
        stack = jnp.concatenate([split * hot[t, g:g + 1, :] for g in range(16)], axis=0)
        back = mm(stack.astype(BF), rk[t], 1, 1)
        for g in range(16):
            mbuf[g, 8 * t:8 * (t + 1), :] = fold3(back[24 * g:24 * (g + 1)], 8)
        mixes[t] = mm(onehot(eye), split.astype(BF), 1, 1)
    post(6, mbuf, mgot)

    collect(6, mgot)
    lane_eye = onehot(iota((48, 128), 0) == iota((48, 128), 1))
    for t in (0, 1):
        for d in range(16):
            slots[t, 48 * d:48 * (d + 1), 0:24] = mm(
                lane_eye, pieces(mgot[d, 8 * t:8 * (t + 1), :]), 1, 1
            ).astype(BF)
        cols[t] = mm(order[t], slots[t], 1, 0)

    def column(ref, t, j):
        return ref[t, :, j:j + 1] + ref[t, :, 8 + j:9 + j] + ref[t, :, 16 + j:17 + j]

    for n in (0, 1):
        @pl.loop(0, 2)
        def _(t):
            u = 2 * n + t
            mix_col = column(cols, t, n)
            inner_col = column(cols, t, 2 + n)
            dks[...] = jnp.zeros_like(dks)
            dvs[...] = jnp.zeros_like(dvs)
            dq = []
            for b in range(6):
                prev = (b + 5) % 6
                rows = slice(128 * b, 128 * (b + 1))
                prows = slice(128 * prev, 128 * (prev + 1))
                weighted = probs[u, b] * mix_col[rows]
                grads = jnp.where(self_pair, 0.0, weighted * (pairs[u, b] - inner_col[rows]))
                grads = grads.astype(BF)
                dq.append(mm(grads, both(ks, u, b), 1, 0))
                dk = mm(grads, qs[u, rows], 0, 0)
                dv = mm(weighted.astype(BF), ds_[u, rows], 0, 0)
                dks[rows] += dk[0:128]
                dks[prows] += dk[128:256]
                dvs[rows] += dv[0:128]
                dvs[prows] += dv[128:256]
            qf = qs[u].astype(F32)
            fac = facs[u]
            dk = dks[...]
            inside = jnp.sum(dk * qf, axis=1, keepdims=True)
            result = jnp.concatenate(dq, axis=0) + fac * dk - fac * fac * fac * inside * qf
            wide = jnp.concatenate([result.astype(BF), dvs[...].astype(BF)], axis=1)
            gbuf[n, :, t] = mm(unorder[t], wide, 1, 0).astype(BF).reshape(16, 48, 256)

        post(7 + n, gbuf.at[n], ggot.at[n])

    collect(5, ogot)
    parts = [mm(unpick[:, 768 * t:768 * (t + 1)], ogot[:, t].reshape(768, 256), 1, 0) for t in (0, 1)]
    for n in (0, 1):
        lanes = slice(128 * n, 128 * (n + 1))
        output[:, lanes] = (
            column(mixes, 0, n) * parts[0][:, lanes] + column(mixes, 1, n) * parts[1][:, lanes]
        ).astype(BF)

    for n in (0, 1):
        collect(7 + n, ggot.at[n])
        rows = mm(unpick[:, 0:768], ggot[n, :, 0].reshape(768, 256), 1, 0)
        rows = rows + mm(unpick[:, 768:1536], ggot[n, :, 1].reshape(768, 256), 1, 0)
        rows = rows.astype(BF)
        dqv[:, 128 * n:128 * (n + 1)] = rows[:, 0:128]
        dqv[:, 256 + 128 * n:256 + 128 * (n + 1)] = rows[:, 128:256]

    sent(0, kbuf)
    for n in (0, 1):
        sent(1 + n, sbuf.at[n])
        sent(7 + n, gbuf.at[n])
    sent(3, dbuf)
    sent(4, lbuf)
    sent(5, obuf)
    sent(6, mbuf)


def middle(xg, wg, dout, grow, brow):
    vm = pl.BlockSpec(memory_space=pltpu.VMEM)
    V = pltpu.VMEM
    return pl.pallas_call(
        middle_kernel,
        out_shape=(
            jax.ShapeDtypeStruct((512, 512), BF),
            jax.ShapeDtypeStruct((512, 256), BF),
        ),
        in_specs=[vm] * 5,
        out_specs=(vm, vm),
        scratch_shapes=[
            V((2, 512, 256), F32),
            V((2, 512, 256), BF),
            V((2, 768, 512), BF),
            V((512, 1536), BF),
            V((2, 768, 768), BF),
            V((2, 768, 768), BF),
            V((2, 8, 128), F32),
            V((2, 16, 512), F32),
            V((2, 128, 512), BF),
            V((16, 8, 128), F32),
            V((16, 8, 128), F32),
            V((2, 16, 2, 48, 256), BF),
            V((2, 16, 2, 48, 256), BF),
            V((16, 2, 48, 256), BF),
            V((16, 2, 48, 256), BF),
            V((16, 2, 48, 256), BF),
            V((16, 2, 48, 256), BF),
            V((2, 16, 2, 48, 256), BF),
            V((2, 16, 2, 48, 256), BF),
            V((16, 16, 128), F32),
            V((16, 16, 128), F32),
            V((16, 16, 128), F32),
            V((16, 16, 128), F32),
            V((4, 768, 128), BF),
            V((4, 768, 128), BF),
            V((4, 768, 128), BF),
            V((4, 768, 128), BF),
            V((4, 768, 128), F32),
            V((4, 6, 128, 256), F32),
            V((4, 6, 128, 256), F32),
            V((4, 768, 128), F32),
            V((2, 768, 128), F32),
            V((2, 768, 128), BF),
            V((2, 768, 128), F32),
            V((768, 128), F32),
            V((768, 128), F32),
            V((2, 512, 24), F32),
            pltpu.SemaphoreType.DMA((9,)),
            pltpu.SemaphoreType.DMA((9,)),
        ],
        compiler_params=pltpu.CompilerParams(
            collective_id=2, has_side_effects=True, vmem_limit_bytes=60 * 1024 * 1024
        ),
        name="attention_exchange",
    )(xg, wg, dout, grow, brow)


def per_device(layer_input, qk_weight, value_weight, groups, buckets, out_cotangent):
    xg, wg = gather_all(layer_input, qk_weight, value_weight)
    dqv, output = middle(xg, wg, out_cotangent, groups.reshape(ROUNDS, -1), buckets)
    return (output,) + reduce_all(dqv, xg, wg)


def solution(mesh):
    return jax.shard_map(
        per_device,
        mesh=mesh,
        in_specs=(
            P("seq", "head"),
            P("seq", "head"),
            P("seq", "head"),
            P(None, "seq", None),
            P(None, "seq"),
            P("seq", "head"),
        ),
        out_specs=(P("seq", "head"), P("seq", "head"), P("seq", "head"), P("seq", "head")),
        check_vma=False,
    )
```

```python
import math

import jax
import jax.numpy as jnp
from jax import lax
from jax.experimental import pallas as pl
from jax.experimental.pallas import tpu as pltpu
from jax.sharding import PartitionSpec as P

HEAD_DIM = 128
ROUNDS = 2
EPSILON = 1e-06
SELF_SCORE = -100000.0
MASKED_SCORE = -1000000000.0


MESH = pl.DeviceIdType.MESH
BF = jnp.bfloat16
F32 = jnp.float32


def rcopy(src, dst, ssem, rsem, dev):
    return pltpu.make_async_remote_copy(
        src_ref=src, dst_ref=dst, send_sem=ssem, recv_sem=rsem, device_id=dev, device_id_type=MESH
    )


class Sends:
    def __init__(self, sems):
        self.sems, self.used, self.open = sems, 0, []

    def start(self, src, dst, rsem, dev):
        copy = rcopy(src, dst, self.sems.at[self.used], rsem, dev)
        copy.start()
        self.used += 1
        self.open.append(copy)

    def finish(self):
        for copy in self.open:
            copy.wait_send()
        self.open = []


def arrived(ref, rsem, ssem, dev):
    rcopy(ref, ref, ssem, rsem, dev).wait_recv()


def place():
    s, h = lax.axis_index("seq"), lax.axis_index("head")
    return s, h, s // 4, s % 4, h // 2, h % 2


def enter(devices):
    barrier = pltpu.get_barrier_semaphore()
    for dev in devices:
        pl.semaphore_signal(barrier, inc=1, device_id=dev, device_id_type=MESH)
    pl.semaphore_wait(barrier, len(devices))


def ring_neighbours():
    s, h, x, y, z, c = place()
    east, west = (((x + 1) % 4) * 4 + y, h), (((x + 3) % 4) * 4 + y, h)
    north, south = (x * 4 + (y + 1) % 4, h), (x * 4 + (y + 3) % 4, h)
    up, down = (s, ((z + 1) % 8) * 2 + c), (s, ((z + 7) % 8) * 2 + c)
    twin = (s, 2 * z + 1 - c)
    return east, west, north, south, up, down, twin


def mm(a, b, ca, cb):
    return lax.dot_general(a, b, (((ca,), (cb,)), ((), ())), preferred_element_type=F32)


def iota(shape, axis):
    return lax.broadcasted_iota(jnp.int32, shape, axis).astype(F32)


def onehot(mask):
    return jnp.where(mask, 1.0, 0.0).astype(BF)


def split3(v):
    high = v.astype(BF).astype(F32)
    rest = v - high
    mid = rest.astype(BF).astype(F32)
    return high, mid, rest - mid


def pieces(v):
    return jnp.concatenate(split3(v), axis=0).astype(BF)


def fold3(v, n):
    return v[0:n] + v[n:2 * n] + v[2 * n:3 * n]


def key_factor(qf):
    mean = jnp.mean(qf * qf, axis=1, keepdims=True)
    return lax.rsqrt(mean + EPSILON) * (1.0 / math.sqrt(HEAD_DIM))


def whole_kernel(
    x_ref, wq_ref, wv_ref, dout, grow, brow,
    output, ig, gq, gv,
    xg, wg, dqv, dqvt,
    qv, pick, unpick, order, unorder, live, hot, rk,
    kbuf, kgot, sbuf, rbuf, dbuf, dgot, obuf, ogot, ggot, lbuf, lgot, mbuf, mgot,
    qs, ks, vs, ds_, probs, pairs, osum, vals, slots, dks, dvs, mixes,
    tme, ttwin, tgot, zgot, gsum, g1far, g1near, g2far, g2near,
    asend, arecv, ssem, zsem, tsem, w1sem, w2sem, rtsem, rzsem, s1sem, s2sem,
):
    s, h, x, y, z, c = place()
    east, west, north, south, up, down, twin = ring_neighbours()
    barrier = pltpu.get_barrier_semaphore()

    @pl.loop(1, 16)
    def _(k):
        pl.semaphore_signal(barrier, inc=1, device_id=((s + k) % 16, h), device_id_type=MESH)

    for dev in (up, down, twin):
        pl.semaphore_signal(barrier, inc=1, device_id=dev, device_id_type=MESH)
    pl.semaphore_wait(barrier, 18)
    out = Sends(ssem)

    def rows256(ref, k):
        return ref.at[pl.ds(256 * k, 256)]

    def post(n, src, dst):
        @pl.loop(1, 16)
        def _(k):
            d = (s + k) % 16
            rcopy(src.at[d], dst.at[s], asend.at[n], arecv.at[n], (d, h)).start()

        dst[s] = src[s]

    def collect(n, dst):
        part = dst.at[pl.ds(0, 15)]
        rcopy(part, part, asend.at[n], arecv.at[n], (s, h)).wait_recv()

    def sent(n, src):
        part = src.at[pl.ds(0, 15)]
        rcopy(part, part, asend.at[n], arecv.at[n], (s, h)).wait_send()

    first_axis = [(north, south), (east, west)]
    second_axis = [(east, west), (north, south)]
    prim, sec = [y, x], [x, y]
    own = [wq_ref, wv_ref]

    def wslot(j, p, r):
        return wg.at[r * 4 + p if j == 0 else p * 4 + r, j]

    def half(ref, k):
        return ref.at[pl.ds(128 * k, 128)]

    for j in (0, 1):
        plus, minus = first_axis[j]
        dst = wslot(j, prim[j], sec[j])
        out.start(own[j], dst, w1sem.at[j, 0], plus)
        out.start(own[j], dst, w1sem.at[j, 1], minus)
    for k in (0, 1):
        rows = pl.ds(256 * k, 256)
        out.start(x_ref.at[rows], xg.at[h, rows], zsem.at[0, 0, k], up)
        out.start(x_ref.at[rows], xg.at[h, rows], zsem.at[1, 0, k], down)

    def second_send(j, k, p, src):
        plus, minus = second_axis[j]
        dst = wslot(j, p, sec[j])
        out.start(src, dst, w2sem.at[j, k, 0], plus)
        out.start(src, dst, w2sem.at[j, k, 1], minus)

    for j in (0, 1):
        second_send(j, 0, prim[j], own[j])
    out.start(x_ref, xg.at[h], tsem.at[0, 0], twin)

    def first_arrivals(j):
        plus, minus = first_axis[j]
        for k, (step, onward) in enumerate(((3, plus), (1, minus))):
            p = (prim[j] + step) % 4
            ref = wslot(j, p, sec[j])
            arrived(ref, w1sem.at[j, k], ssem.at[0], plus)
            out.start(half(ref, k), half(ref, k), w1sem.at[j, 2 + k], onward)
            second_send(j, 1 + k, p, ref)

    def first_far(j):
        p = (prim[j] + 2) % 4
        ref = wslot(j, p, sec[j])
        for k in (0, 1):
            arrived(half(ref, k), w1sem.at[j, 2 + k], ssem.at[0], first_axis[j][0])
        second_send(j, 3, p, ref)

    offsets = (0, 3, 1, 2)

    def second_arrivals(j, k):
        p = (prim[j] + offsets[k]) % 4
        plus, minus = second_axis[j]
        for side, (step, onward) in enumerate(((3, plus), (1, minus))):
            ref = wslot(j, p, (sec[j] + step) % 4)
            arrived(ref, w2sem.at[j, k, side], ssem.at[0], plus)
            out.start(half(ref, side), half(ref, side), w2sem.at[j, k, 2 + side], onward)

    def second_far(j, k):
        p = (prim[j] + offsets[k]) % 4
        ref = wslot(j, p, (sec[j] + 2) % 4)
        for side in (0, 1):
            arrived(half(ref, side), w2sem.at[j, k, 2 + side], ssem.at[0], second_axis[j][0])

    def z_arrival(dist):
        for k in (0, 1):
            for side, (step, onward) in enumerate(((8 - dist, up), (dist, down))):
                ref = rows256(xg.at[((z + step) % 8) * 2 + c], k)
                arrived(ref, zsem.at[side, dist - 1, k], ssem.at[0], up)
                if dist < 3 or k == side:
                    out.start(ref, ref, zsem.at[side, dist, k], onward)
        for side, step in enumerate((8 - dist, dist)):
            ref = xg.at[((z + step) % 8) * 2 + c]
            out.start(ref, ref, tsem.at[side, dist], twin)

    def z_far():
        ref = xg.at[((z + 4) % 8) * 2 + c]
        for side in (0, 1):
            arrived(rows256(ref, side), zsem.at[side, 3, side], ssem.at[0], up)
            out.start(rows256(ref, side), rows256(ref, side), tsem.at[side, 4], twin)

    def twin_arrivals():
        arrived(xg.at[2 * z + 1 - c], tsem.at[0, 0], ssem.at[0], twin)
        for dist in (1, 2, 3):
            for side, step in enumerate((8 - dist, dist)):
                arrived(xg.at[((z + step) % 8) * 2 + 1 - c], tsem.at[side, dist], ssem.at[0], twin)
        for side in (0, 1):
            ref = xg.at[((z + 4) % 8) * 2 + 1 - c]
            arrived(rows256(ref, side), tsem.at[side, 4], ssem.at[0], twin)

    xg[h] = x_ref[...]
    wg[s, 0] = wq_ref[...]
    wg[s, 1] = wv_ref[...]

    kbuf[...] = jnp.zeros_like(kbuf)
    lbuf[...] = jnp.zeros_like(lbuf)
    vals[...] = jnp.zeros_like(vals)
    slots[...] = jnp.zeros_like(slots)
    upper = onehot(iota((512, 512), 0) <= iota((512, 512), 1))
    eye = iota((512, 512), 0) == iota((512, 512), 1)
    slot_rows, slot_cols = [], []
    for t in (0, 1):
        g = grow[t].astype(F32)
        member = jnp.where(iota((16, 512), 0) == g, 1.0, 0.0)
        count = mm(member.astype(BF), upper, 1, 0)
        rank = jnp.sum(member * count, axis=0, keepdims=True) - 1.0
        slot = g * 48.0 + rank
        slot_col = jnp.sum(jnp.where(eye, slot, 0.0), axis=1, keepdims=True)
        hot[t] = member
        rk[t] = onehot(iota((128, 512), 0) == rank)
        slot_rows.append(slot)
        slot_cols.append(slot_col)
        named = member * (brow[t:t + 1, :].astype(F32) + 1.0)
        sent_keys = mm(named.astype(BF), rk[t], 1, 1)
        for d in range(16):
            kbuf[d, t:t + 1, :] = sent_keys[d:d + 1, :]
    post(0, kbuf, kgot)

    def slot_order(t):
        tag = jnp.concatenate([kgot[d, t:t + 1, :] for d in range(16)], axis=0)
        usable = iota((16, 128), 1) < 48.0
        kinds = [jnp.where(tag == float(k), 1.0, 0.0) for k in range(1, 9)]
        kinds.append(jnp.where(usable, jnp.where(tag == 0.0, 1.0, 0.0), 0.0))
        stack = jnp.concatenate(kinds, axis=0)
        within = mm(stack.astype(BF), onehot(iota((128, 128), 0) <= iota((128, 128), 1)), 1, 0)
        totals = jnp.broadcast_to(within[:, 127:128], (144, 128)).astype(BF)
        before = mm(onehot(iota((144, 144), 0) > iota((144, 144), 1)), totals, 1, 0)
        place_all = stack * (within + before - 1.0)
        rank = place_all[0:16]
        for k in range(1, 9):
            rank = rank + place_all[16 * k:16 * (k + 1)]
        live[t] = before[128:136, :]
        small_eye = iota((48, 128), 0) == iota((48, 128), 1)
        columns = jnp.concatenate(
            [
                jnp.sum(jnp.where(small_eye, rank[d:d + 1, :], 0.0), axis=1, keepdims=True)
                for d in range(16)
            ],
            axis=0,
        )
        unorder[t] = onehot(iota((768, 768), 1) == columns)
        row = jnp.sum(
            jnp.where(iota((768, 768), 0) == iota((768, 768), 1), columns, 0.0),
            axis=0, keepdims=True,
        )
        order[t] = onehot(iota((768, 768), 0) == row)

    for j in (0, 1):
        first_arrivals(j)
    for j in (0, 1):
        second_arrivals(j, 0)
    z_arrival(1)
    pick[0] = onehot(iota((768, 512), 0) == slot_rows[0])
    for j in (0, 1):
        first_far(j)
    for j in (0, 1):
        second_arrivals(j, 1)
    z_arrival(2)
    pick[1] = onehot(iota((768, 512), 0) == slot_rows[1])
    for t in (0, 1):
        dbuf[:, t] = mm(pick[t], dout[...], 1, 0).astype(BF).reshape(16, 48, 256)
    post(5, dbuf, dgot)

    for t in (0, 1):
        unpick[:, 768 * t:768 * (t + 1)] = onehot(iota((512, 768), 1) == slot_cols[t])
    for j in (0, 1):
        second_arrivals(j, 2)
    z_arrival(3)
    collect(0, kgot)
    slot_order(0)
    for j in (0, 1):
        second_arrivals(j, 3)
    z_far()
    slot_order(1)
    for k in range(4):
        second_far(0, k)
        second_far(1, k)
    twin_arrivals()

    for j in (0, 1):
        probs[j, 0:4] = jnp.zeros((4, 128, 256), F32)

    @pl.loop(0, 4)
    def _(i):
        for j in (0, 1):
            total = probs[j, 0:4].reshape(512, 256)
            for k in range(4):
                b = 4 * i + k
                total += mm(xg[b], wg[b, j], 1, 0)
            probs[j, 0:4] = total.reshape(4, 128, 256)

    for j in (0, 1):
        for n in (0, 1):
            part = probs[j, 0:4, :, 128 * n:128 * (n + 1)].reshape(512, 128)
            qv[n, :, 128 * j:128 * (j + 1)] = part.astype(BF)

    for n in (0, 1):
        for t in (0, 1):
            sbuf[n, t] = mm(pick[t], qv[n], 1, 0).astype(BF).reshape(16, 48, 256)
            post(1 + 2 * n + t, sbuf.at[n, t], rbuf.at[n, t])
    def both(ref, lead, b):
        prev = (b + 5) % 6
        return jnp.concatenate(
            [ref[lead, 128 * b:128 * (b + 1)], ref[lead, 128 * prev:128 * (prev + 1)]], axis=0
        )

    self_pair = iota((128, 256), 0) == iota((128, 256), 1)

    collect(5, dgot)

    @pl.loop(0, 2)
    def _(t):
        rows = mm(order[t], dgot[:, t].reshape(768, 256), 1, 0).astype(BF)
        ds_[t] = rows[:, 0:128]
        ds_[2 + t] = rows[:, 128:256]

    choose = onehot(iota((8, 128), 0) == iota((8, 128), 1))

    for n in (0, 1):

        @pl.loop(0, 2)
        def _(t):
            u = 2 * n + t
            collect(1 + u, rbuf.at[n, t])
            rows = mm(order[t], rbuf[n, t].reshape(768, 256), 1, 0)
            qf = rows[:, 0:128]
            fac = key_factor(qf)
            qs[u] = qf.astype(BF)
            ks[u] = (qf * fac).astype(BF)
            vs[u] = rows[:, 128:256].astype(BF)
            for b in range(6):
                prev = (b + 5) % 6
                at = iota((1, 256), 1)
                at = jnp.where(at < 128.0, at + 128.0 * b, at - 128.0 + 128.0 * prev)
                used = jnp.concatenate([live[t, 0:1, :]] * 2, axis=1)
                scores = mm(qs[u, 128 * b:128 * (b + 1)], both(ks, u, b), 1, 1)
                scores = jnp.where(self_pair, SELF_SCORE, scores)
                scores = jnp.where(at < used, scores, MASKED_SCORE)
                top = jnp.max(scores, axis=1, keepdims=True)
                e = jnp.exp(scores - top)
                total = jnp.sum(e, axis=1, keepdims=True)
                weights = e * (1.0 / total)
                probs[u, b] = weights
                mixed = mm(weights.astype(BF), both(vs, u, b), 1, 0)
                osum[u, 128 * b:128 * (b + 1)] = mixed
                grad = ds_[u, 128 * b:128 * (b + 1)]
                pairs[u, b] = mm(grad, both(vs, u, b), 1, 1)
                vals[t, 128 * b:128 * (b + 1), 2 + n:3 + n] = jnp.sum(
                    grad.astype(F32) * mixed, axis=1, keepdims=True
                )
                vals[t, 128 * b:128 * (b + 1), n:n + 1] = top + jnp.log(total)
            if n == 1:
                high, mid, low = split3(vals[t])
                lines = pieces(
                    mm(choose, high.astype(BF), 1, 1)
                    + mm(choose, mid.astype(BF), 1, 1)
                    + mm(choose, low.astype(BF), 1, 1)
                )
                for d in range(16):
                    lbuf[d, pl.ds(pl.multiple_of(8 * t, 8), 8), 0:48] = fold3(
                        mm(lines, unorder[t, 48 * d:48 * (d + 1)], 1, 1), 8
                    )

    post(6, lbuf, lgot)
    for t in (0, 1):
        wide = jnp.concatenate([osum[t], osum[2 + t]], axis=1).astype(BF)
        obuf[:, t] = mm(unorder[t], wide, 1, 0).astype(BF).reshape(16, 48, 256)
    post(7, obuf, ogot)

    collect(6, lgot)
    here = []
    for t in (0, 1):
        high, mid, low = split3(lgot[:, 8 * t:8 * (t + 1), :].reshape(128, 128))
        found = (
            mm(high.astype(BF), rk[t], 1, 0)
            + mm(mid.astype(BF), rk[t], 1, 0)
            + mm(low.astype(BF), rk[t], 1, 0)
        )
        line = found[0:8] * hot[t, 0:1, :]
        for g in range(1, 16):
            line = line + found[8 * g:8 * (g + 1)] * hot[t, g:g + 1, :]
        here.append(line)
    top = jnp.maximum(here[0], here[1])
    log_all = top + jnp.log(jnp.exp(here[0] - top) + jnp.exp(here[1] - top))
    mix = [jnp.exp(line - log_all) for line in here]
    inner = mix[0][0:2] * here[0][2:4] + mix[1][0:2] * here[1][2:4]
    mix_lines = []
    for t in (0, 1):
        lines = jnp.concatenate([mix[t][0:2], inner, jnp.zeros((4, 512), F32)], axis=0)
        split = jnp.concatenate(split3(lines), axis=0)
        stack = jnp.concatenate([split * hot[t, g:g + 1, :] for g in range(16)], axis=0)
        back = mm(stack.astype(BF), rk[t], 1, 1)
        for g in range(16):
            mbuf[g, 8 * t:8 * (t + 1), :] = fold3(back[24 * g:24 * (g + 1)], 8)
        mix_lines.append(split)
    post(8, mbuf, mgot)
    for t in (0, 1):
        mixes[t] = mm(onehot(eye), mix_lines[t].astype(BF), 1, 1)

    collect(8, mgot)
    lane_eye = onehot(iota((48, 128), 0) == iota((48, 128), 1))
    for t in (0, 1):
        for d in range(16):
            slots[t, 48 * d:48 * (d + 1), 0:24] = mm(
                lane_eye, pieces(mgot[d, 8 * t:8 * (t + 1), :]), 1, 1
            ).astype(BF)
        vals[t] = mm(order[t], slots[t], 1, 0)

    def column(ref, t, j):
        return ref[t, :, j:j + 1] + ref[t, :, 8 + j:9 + j] + ref[t, :, 16 + j:17 + j]

    for n in (0, 1):

        @pl.loop(0, 2)
        def _(t):
            u = 2 * n + t
            sent(1 + u, sbuf.at[n, t])
            mix_col = column(vals, t, n)
            inner_col = column(vals, t, 2 + n)
            dks[...] = jnp.zeros_like(dks)
            dvs[...] = jnp.zeros_like(dvs)
            dq = []
            for b in range(6):
                prev = (b + 5) % 6
                rows = slice(128 * b, 128 * (b + 1))
                prows = slice(128 * prev, 128 * (prev + 1))
                weighted = probs[u, b] * mix_col[rows]
                grads = jnp.where(self_pair, 0.0, weighted * (pairs[u, b] - inner_col[rows]))
                grads = grads.astype(BF)
                dq.append(mm(grads, both(ks, u, b), 1, 0))
                dk = mm(grads, qs[u, rows], 0, 0)
                dv = mm(weighted.astype(BF), ds_[u, rows], 0, 0)
                dks[rows] += dk[0:128]
                dks[prows] += dk[128:256]
                dvs[rows] += dv[0:128]
                dvs[prows] += dv[128:256]
            qf = qs[u].astype(F32)
            fac = key_factor(qf)
            dk = dks[...]
            inside = jnp.sum(dk * qf, axis=1, keepdims=True)
            result = jnp.concatenate(dq, axis=0) + fac * dk - fac * fac * fac * inside * qf
            wide = jnp.concatenate([result.astype(BF), dvs[...].astype(BF)], axis=1)
            sbuf[n, t] = mm(unorder[t], wide, 1, 0).astype(BF).reshape(16, 48, 256)
            post(9 + u, sbuf.at[n, t], ggot.at[n, t])

    collect(7, ogot)
    parts = [mm(unpick[:, 768 * t:768 * (t + 1)], ogot[:, t].reshape(768, 256), 1, 0) for t in (0, 1)]
    for n in (0, 1):
        lanes = slice(128 * n, 128 * (n + 1))
        output[:, lanes] = (
            column(mixes, 0, n) * parts[0][:, lanes] + column(mixes, 1, n) * parts[1][:, lanes]
        ).astype(BF)

    for n in (0, 1):
        collect(9 + 2 * n, ggot.at[n, 0])
        rows = mm(unpick[:, 0:768], ggot[n, 0].reshape(768, 256), 1, 0)
        collect(10 + 2 * n, ggot.at[n, 1])
        rows = rows + mm(unpick[:, 768:1536], ggot[n, 1].reshape(768, 256), 1, 0)
        rows = rows.astype(BF)
        dqv[:, 128 * n:128 * (n + 1)] = rows[:, 0:128]
        dqv[:, 256 + 128 * n:256 + 128 * (n + 1)] = rows[:, 128:256]
        dqvt[128 * n:128 * (n + 1), :] = jnp.transpose(rows[:, 0:128])
        dqvt[256 + 128 * n:256 + 128 * (n + 1), :] = jnp.transpose(rows[:, 128:256])

    def term(b):
        return mm(dqv[:, 0:256], wg[b, 0], 1, 1) + mm(dqv[:, 256:512], wg[b, 1], 1, 1)

    def twin_term(k, zd):
        ttwin[zd] = term(2 * zd + 1 - c).astype(BF)
        out.start(ttwin.at[zd], tgot.at[zd], rtsem.at[k], twin)

    def my_term(zd):
        tme[zd] = term(2 * zd + c).astype(BF)

    def pair(k, zd):
        arrived(tgot.at[zd], rtsem.at[k], ssem.at[0], twin)
        tme[zd] = (tme[zd].astype(F32) + tgot[zd].astype(F32)).astype(BF)

    prim, sec = [x, y], [y, x]
    first_axis = [(east, west), (north, south)]
    second_axis = [(north, south), (east, west)]

    def grads(j, r):
        @pl.loop(0, 4)
        def _(p):
            b = r * 4 + p if j == 0 else p * 4 + r
            gsum[j, r, p] = mm(dqvt[256 * j:256 * (j + 1), :], xg[b], 1, 0).astype(BF)

    order = (2, 1, 3, 0)

    def first_far_send(j):
        r = (prim[j] + 2) % 4
        for k, off in enumerate(order):
            p = (sec[j] + off) % 4
            for side in (0, 1):
                out.start(
                    half(gsum.at[j, r, p], side), g1far.at[j, side, p], s1sem.at[j, k, side],
                    first_axis[j][side],
                )

    def first_near_send(j):
        for k, off in enumerate(order):
            p = (sec[j] + off) % 4
            for side, step in enumerate((1, 3)):
                r = (prim[j] + step) % 4
                arrived(g1far.at[j, side, p], s1sem.at[j, k, side], ssem.at[0], first_axis[j][0])
                rows = pl.ds(128 * side, 128)
                gsum[j, r, p, rows] = (
                    gsum[j, r, p, rows].astype(F32) + g1far[j, side, p].astype(F32)
                ).astype(BF)
                out.start(
                    gsum.at[j, r, p], g1near.at[j, side, p], s1sem.at[j, k, 2 + side],
                    first_axis[j][side],
                )

    def first_final(j, k):
        p = (sec[j] + order[k]) % 4
        for side in (0, 1):
            arrived(g1near.at[j, side, p], s1sem.at[j, k, 2 + side], ssem.at[0], first_axis[j][0])
        r = prim[j]
        gsum[j, r, p] = (
            gsum[j, r, p].astype(F32) + g1near[j, 0, p].astype(F32) + g1near[j, 1, p].astype(F32)
        ).astype(BF)

    def second_far_send(j):
        p = (sec[j] + 2) % 4
        for side in (0, 1):
            out.start(
                half(gsum.at[j, prim[j], p], side), g2far.at[j, side], s2sem.at[j, side],
                second_axis[j][side],
            )

    def second_near_send(j):
        for side, step in enumerate((1, 3)):
            p = (sec[j] + step) % 4
            arrived(g2far.at[j, side], s2sem.at[j, side], ssem.at[0], second_axis[j][0])
            rows = pl.ds(128 * side, 128)
            gsum[j, prim[j], p, rows] = (
                gsum[j, prim[j], p, rows].astype(F32) + g2far[j, side].astype(F32)
            ).astype(BF)
            out.start(
                gsum.at[j, prim[j], p], g2near.at[j, side], s2sem.at[j, 2 + side],
                second_axis[j][side],
            )

    def second_final(j, result):
        for side in (0, 1):
            arrived(g2near.at[j, side], s2sem.at[j, 2 + side], ssem.at[0], second_axis[j][0])
        result[...] = jnp.transpose(
            gsum[j, prim[j], sec[j]].astype(F32)
            + g2near[j, 0].astype(F32)
            + g2near[j, 1].astype(F32)
        )

    def z_send(step):
        if step == 0:
            zd = (z + 4) % 8
            for side, onward in enumerate((up, down)):
                out.start(
                    rows256(tme.at[zd], side), rows256(zgot.at[side, 0], side), rzsem.at[side, 0],
                    onward,
                )
            return
        for side, (zd, onward) in enumerate((((z + 4 - step) % 8, up), ((z + 4 + step) % 8, down))):
            if step == 1:
                rows = pl.ds(256 * side, 256)
                arrived(zgot.at[side, 0, rows], rzsem.at[side, 0], ssem.at[0], up)
                tme[zd, rows] = (
                    tme[zd, rows].astype(F32) + zgot[side, 0, rows].astype(F32)
                ).astype(BF)
            else:
                arrived(zgot.at[side, step - 1], rzsem.at[side, step - 1], ssem.at[0], up)
                tme[zd] = (tme[zd].astype(F32) + zgot[side, step - 1].astype(F32)).astype(BF)
            out.start(tme.at[zd], zgot.at[side, step], rzsem.at[side, step], onward)

    zorder = [(z + off) % 8 for off in (4, 3, 5, 2, 6, 1, 7, 0)]

    twin_term(0, zorder[0])
    for j in (0, 1):
        grads(j, (prim[j] + 2) % 4)
        first_far_send(j)
    my_term(zorder[0])
    pair(0, zorder[0])
    z_send(0)
    for k in (1, 2):
        twin_term(k, zorder[k])
        my_term(zorder[k])
    for j in (0, 1):
        grads(j, (prim[j] + 1) % 4)
        grads(j, (prim[j] + 3) % 4)
        first_near_send(j)
    pair(1, zorder[1])
    pair(2, zorder[2])
    z_send(1)
    for k in (3, 4, 5, 6, 7):
        twin_term(k, zorder[k])
        my_term(zorder[k])
    for j in (0, 1):
        grads(j, prim[j])
    pair(3, zorder[3])
    pair(4, zorder[4])
    z_send(2)
    for j in (0, 1):
        first_final(j, 0)
        second_far_send(j)
    pair(5, zorder[5])
    pair(6, zorder[6])
    z_send(3)
    for j in (0, 1):
        first_final(j, 1)
        first_final(j, 2)
        second_near_send(j)
        first_final(j, 3)
    pair(7, zorder[7])
    for side in (0, 1):
        arrived(zgot.at[side, 3], rzsem.at[side, 3], ssem.at[0], up)
    ig[...] = (
        tme[z].astype(F32) + zgot[0, 3].astype(F32) + zgot[1, 3].astype(F32)
    ).astype(BF)
    second_final(0, gq)
    second_final(1, gv)
    out.finish()
    sent(0, kbuf)
    for u in range(4):
        sent(9 + u, sbuf.at[u // 2, u % 2])
    sent(5, dbuf)
    sent(6, lbuf)
    sent(7, obuf)
    sent(8, mbuf)


def copy_kernel(*refs):
    for source, target in zip(refs[0:4], refs[4:8]):
        target[...] = source[...]


def per_device(layer_input, qk_weight, value_weight, groups, buckets, out_cotangent):
    vm = pl.BlockSpec(memory_space=pltpu.VMEM)
    V = pltpu.VMEM
    shapes = (
        jax.ShapeDtypeStruct((512, 256), BF),
        jax.ShapeDtypeStruct((512, 256), BF),
        jax.ShapeDtypeStruct((256, 256), F32),
        jax.ShapeDtypeStruct((256, 256), F32),
    )
    results = pl.pallas_call(
        whole_kernel,
        out_shape=shapes,
        in_specs=[vm] * 6,
        out_specs=(vm,) * 4,
        scratch_shapes=[
            V((16, 512, 256), BF),
            V((16, 2, 256, 256), BF),
            V((512, 512), BF),
            V((512, 512), BF),
            V((2, 512, 256), BF),
            V((2, 768, 512), BF),
            V((512, 1536), BF),
            V((2, 768, 768), BF),
            V((2, 768, 768), BF),
            V((2, 8, 128), F32),
            V((2, 16, 512), F32),
            V((2, 128, 512), BF),
            V((16, 8, 128), F32),
            V((16, 8, 128), F32),
            V((2, 2, 16, 48, 256), BF),
            V((2, 2, 16, 48, 256), BF),
            V((16, 2, 48, 256), BF),
            V((16, 2, 48, 256), BF),
            V((16, 2, 48, 256), BF),
            V((16, 2, 48, 256), BF),
            V((2, 2, 16, 48, 256), BF),
            V((16, 16, 128), F32),
            V((16, 16, 128), F32),
            V((16, 16, 128), F32),
            V((16, 16, 128), F32),
            V((4, 768, 128), BF),
            V((4, 768, 128), BF),
            V((4, 768, 128), BF),
            V((4, 768, 128), BF),
            V((4, 6, 128, 256), F32),
            V((4, 6, 128, 256), F32),
            V((4, 768, 128), F32),
            V((2, 768, 128), F32),
            V((2, 768, 128), BF),
            V((768, 128), F32),
            V((768, 128), F32),
            V((2, 512, 24), F32),
            V((8, 512, 256), BF),
            V((8, 512, 256), BF),
            V((8, 512, 256), BF),
            V((2, 4, 512, 256), BF),
            V((2, 4, 4, 256, 256), BF),
            V((2, 2, 4, 128, 256), BF),
            V((2, 2, 4, 256, 256), BF),
            V((2, 2, 128, 256), BF),
            V((2, 2, 256, 256), BF),
            pltpu.SemaphoreType.DMA((13,)),
            pltpu.SemaphoreType.DMA((13,)),
            pltpu.SemaphoreType.DMA((160,)),
            pltpu.SemaphoreType.DMA((2, 4, 2)),
            pltpu.SemaphoreType.DMA((2, 5)),
            pltpu.SemaphoreType.DMA((2, 4)),
            pltpu.SemaphoreType.DMA((2, 4, 4)),
            pltpu.SemaphoreType.DMA((8,)),
            pltpu.SemaphoreType.DMA((2, 4)),
            pltpu.SemaphoreType.DMA((2, 4, 4)),
            pltpu.SemaphoreType.DMA((2, 4)),
        ],
        compiler_params=pltpu.CompilerParams(
            collective_id=0, has_side_effects=True, vmem_limit_bytes=63 * 1024 * 1024
        ),
        name="hashed_attention_step",
    )(layer_input, qk_weight, value_weight, out_cotangent, jnp.transpose(groups, (0, 2, 1)), buckets)
    return pl.pallas_call(
        copy_kernel,
        out_shape=shapes,
        in_specs=[vm] * 4,
        out_specs=(vm,) * 4,
        name="write_results",
    )(*results)


def solution(mesh):
    return jax.shard_map(
        per_device,
        mesh=mesh,
        in_specs=(
            P("seq", "head"),
            P("seq", "head"),
            P("seq", "head"),
            P(None, "seq", None),
            P(None, "seq"),
            P("seq", "head"),
        ),
        out_specs=(P("seq", "head"), P("seq", "head"), P("seq", "head"), P("seq", "head")),
        check_vma=False,
    )
```

```python
import math

import jax
import jax.numpy as jnp
from jax import lax
from jax.experimental import pallas as pl
from jax.experimental.pallas import tpu as pltpu
from jax.sharding import PartitionSpec as P

HEAD_DIM = 128
ROUNDS = 2
EPSILON = 1e-06
SELF_SCORE = -100000.0
MASKED_SCORE = -1000000000.0


MESH = pl.DeviceIdType.MESH
BF = jnp.bfloat16
F32 = jnp.float32


def rcopy(src, dst, ssem, rsem, dev):
    return pltpu.make_async_remote_copy(
        src_ref=src, dst_ref=dst, send_sem=ssem, recv_sem=rsem, device_id=dev, device_id_type=MESH
    )


class Sends:
    def __init__(self, sems):
        self.sems, self.used, self.open = sems, 0, []

    def start(self, src, dst, rsem, dev):
        copy = rcopy(src, dst, self.sems.at[self.used], rsem, dev)
        copy.start()
        self.used += 1
        self.open.append(copy)

    def finish(self):
        for copy in self.open:
            copy.wait_send()
        self.open = []


def arrived(ref, rsem, ssem, dev):
    rcopy(ref, ref, ssem, rsem, dev).wait_recv()


def place():
    s, h = lax.axis_index("seq"), lax.axis_index("head")
    return s, h, s // 4, s % 4, h // 2, h % 2


def enter(devices):
    barrier = pltpu.get_barrier_semaphore()
    for dev in devices:
        pl.semaphore_signal(barrier, inc=1, device_id=dev, device_id_type=MESH)
    pl.semaphore_wait(barrier, len(devices))


def ring_neighbours():
    s, h, x, y, z, c = place()
    east, west = (((x + 1) % 4) * 4 + y, h), (((x + 3) % 4) * 4 + y, h)
    north, south = (x * 4 + (y + 1) % 4, h), (x * 4 + (y + 3) % 4, h)
    up, down = (s, ((z + 1) % 8) * 2 + c), (s, ((z + 7) % 8) * 2 + c)
    twin = (s, 2 * z + 1 - c)
    return east, west, north, south, up, down, twin


def mm(a, b, ca, cb):
    return lax.dot_general(a, b, (((ca,), (cb,)), ((), ())), preferred_element_type=F32)


def iota(shape, axis):
    return lax.broadcasted_iota(jnp.int32, shape, axis).astype(F32)


def onehot(mask):
    return jnp.where(mask, 1.0, 0.0).astype(BF)


def split3(v):
    high = v.astype(BF).astype(F32)
    rest = v - high
    mid = rest.astype(BF).astype(F32)
    return high, mid, rest - mid


def pieces(v):
    return jnp.concatenate(split3(v), axis=0).astype(BF)


def fold3(v, n):
    return v[0:n] + v[n:2 * n] + v[2 * n:3 * n]


def key_factor(qf):
    mean = jnp.mean(qf * qf, axis=1, keepdims=True)
    return lax.rsqrt(mean + EPSILON) * (1.0 / math.sqrt(HEAD_DIM))


def whole_kernel(
    x_ref, wq_ref, wv_ref, dout, grow, brow,
    output, ig, gq, gv,
    xg, wg, dqv, dqvt,
    qv, pick, unpick, order, unorder, live, hot, rk,
    kbuf, kgot, sbuf, rbuf, dbuf, dgot, obuf, ogot, ggot, lbuf, lgot, mbuf, mgot,
    qs, ks, vs, ds_, probs, pairs, osum, vals, slots, dks, dvs, mixes,
    tme, ttwin, tgot, zgot, gsum, g1far, g1near, g2far, g2near,
    asend, arecv, ssem, zsem, tsem, w1sem, w2sem, rtsem, rzsem, s1sem, s2sem,
):
    s, h, x, y, z, c = place()
    east, west, north, south, up, down, twin = ring_neighbours()
    barrier = pltpu.get_barrier_semaphore()

    @pl.loop(1, 16)
    def _(k):
        pl.semaphore_signal(barrier, inc=1, device_id=((s + k) % 16, h), device_id_type=MESH)

    for dev in (up, down, twin):
        pl.semaphore_signal(barrier, inc=1, device_id=dev, device_id_type=MESH)
    pl.semaphore_wait(barrier, 18)
    out = Sends(ssem)

    def rows256(ref, k):
        return ref.at[pl.ds(256 * k, 256)]

    def post(n, src, dst):
        @pl.loop(1, 16)
        def _(k):
            d = (s + k) % 16
            rcopy(src.at[d], dst.at[s], asend.at[n], arecv.at[n], (d, h)).start()

        dst[s] = src[s]

    def collect(n, dst):
        part = dst.at[pl.ds(0, 15)]
        rcopy(part, part, asend.at[n], arecv.at[n], (s, h)).wait_recv()

    def sent(n, src):
        part = src.at[pl.ds(0, 15)]
        rcopy(part, part, asend.at[n], arecv.at[n], (s, h)).wait_send()

    first_axis = [(north, south), (east, west)]
    second_axis = [(east, west), (north, south)]
    prim, sec = [y, x], [x, y]
    own = [wq_ref, wv_ref]

    def wslot(j, p, r):
        return wg.at[r * 4 + p if j == 0 else p * 4 + r, j]

    def half(ref, k):
        return ref.at[pl.ds(128 * k, 128)]

    for j in (0, 1):
        plus, minus = first_axis[j]
        dst = wslot(j, prim[j], sec[j])
        out.start(own[j], dst, w1sem.at[j, 0], plus)
        out.start(own[j], dst, w1sem.at[j, 1], minus)
    for k in (0, 1):
        rows = pl.ds(256 * k, 256)
        out.start(x_ref.at[rows], xg.at[h, rows], zsem.at[0, 0, k], up)
        out.start(x_ref.at[rows], xg.at[h, rows], zsem.at[1, 0, k], down)

    def second_send(j, k, p, src):
        plus, minus = second_axis[j]
        dst = wslot(j, p, sec[j])
        out.start(src, dst, w2sem.at[j, k, 0], plus)
        out.start(src, dst, w2sem.at[j, k, 1], minus)

    for j in (0, 1):
        second_send(j, 0, prim[j], own[j])
    out.start(x_ref, xg.at[h], tsem.at[0, 0], twin)

    def first_arrivals(j):
        plus, minus = first_axis[j]
        for k, (step, onward) in enumerate(((3, plus), (1, minus))):
            p = (prim[j] + step) % 4
            ref = wslot(j, p, sec[j])
            arrived(ref, w1sem.at[j, k], ssem.at[0], plus)
            out.start(half(ref, k), half(ref, k), w1sem.at[j, 2 + k], onward)
            second_send(j, 1 + k, p, ref)

    def first_far(j):
        p = (prim[j] + 2) % 4
        ref = wslot(j, p, sec[j])
        for k in (0, 1):
            arrived(half(ref, k), w1sem.at[j, 2 + k], ssem.at[0], first_axis[j][0])
        second_send(j, 3, p, ref)

    offsets = (0, 3, 1, 2)

    def second_arrivals(j, k):
        p = (prim[j] + offsets[k]) % 4
        plus, minus = second_axis[j]
        for side, (step, onward) in enumerate(((3, plus), (1, minus))):
            ref = wslot(j, p, (sec[j] + step) % 4)
            arrived(ref, w2sem.at[j, k, side], ssem.at[0], plus)
            out.start(half(ref, side), half(ref, side), w2sem.at[j, k, 2 + side], onward)

    def second_far(j, k):
        p = (prim[j] + offsets[k]) % 4
        ref = wslot(j, p, (sec[j] + 2) % 4)
        for side in (0, 1):
            arrived(half(ref, side), w2sem.at[j, k, 2 + side], ssem.at[0], second_axis[j][0])

    def z_arrival(dist):
        for k in (0, 1):
            for side, (step, onward) in enumerate(((8 - dist, up), (dist, down))):
                ref = rows256(xg.at[((z + step) % 8) * 2 + c], k)
                arrived(ref, zsem.at[side, dist - 1, k], ssem.at[0], up)
                if dist < 3 or k == side:
                    out.start(ref, ref, zsem.at[side, dist, k], onward)
        for side, step in enumerate((8 - dist, dist)):
            ref = xg.at[((z + step) % 8) * 2 + c]
            out.start(ref, ref, tsem.at[side, dist], twin)

    def z_far():
        ref = xg.at[((z + 4) % 8) * 2 + c]
        for side in (0, 1):
            arrived(rows256(ref, side), zsem.at[side, 3, side], ssem.at[0], up)
            out.start(rows256(ref, side), rows256(ref, side), tsem.at[side, 4], twin)

    def twin_arrivals():
        arrived(xg.at[2 * z + 1 - c], tsem.at[0, 0], ssem.at[0], twin)
        for dist in (1, 2, 3):
            for side, step in enumerate((8 - dist, dist)):
                arrived(xg.at[((z + step) % 8) * 2 + 1 - c], tsem.at[side, dist], ssem.at[0], twin)

    def twin_far():
        for side in (0, 1):
            ref = xg.at[((z + 4) % 8) * 2 + 1 - c]
            arrived(rows256(ref, side), tsem.at[side, 4], ssem.at[0], twin)

    xg[h] = x_ref[...]
    wg[s, 0] = wq_ref[...]
    wg[s, 1] = wv_ref[...]

    kbuf[...] = jnp.zeros_like(kbuf)
    lbuf[...] = jnp.zeros_like(lbuf)
    vals[...] = jnp.zeros_like(vals)
    slots[...] = jnp.zeros_like(slots)
    upper = onehot(iota((512, 512), 0) <= iota((512, 512), 1))
    eye = iota((512, 512), 0) == iota((512, 512), 1)
    for j in (0, 1):
        probs[j, 0:4] = jnp.zeros((4, 128, 256), F32)
    slot_rows, slot_cols = [], []

    def token_layout(t):
        g = grow[t].astype(F32)
        member = jnp.where(iota((16, 512), 0) == g, 1.0, 0.0)
        count = mm(member.astype(BF), upper, 1, 0)
        rank = jnp.sum(member * count, axis=0, keepdims=True) - 1.0
        slot = g * 48.0 + rank
        slot_col = jnp.sum(jnp.where(eye, slot, 0.0), axis=1, keepdims=True)
        hot[t] = member
        rk[t] = onehot(iota((128, 512), 0) == rank)
        slot_rows.append(slot)
        slot_cols.append(slot_col)
        named = member * (brow[t:t + 1, :].astype(F32) + 1.0)
        sent_keys = mm(named.astype(BF), rk[t], 1, 1)
        for d in range(16):
            kbuf[d, t:t + 1, :] = sent_keys[d:d + 1, :]
    token_layout(0)

    def slot_order(t):
        tag = jnp.concatenate([kgot[d, t:t + 1, :] for d in range(16)], axis=0)
        usable = iota((16, 128), 1) < 48.0
        kinds = [jnp.where(tag == float(k), 1.0, 0.0) for k in range(1, 9)]
        kinds.append(jnp.where(usable, jnp.where(tag == 0.0, 1.0, 0.0), 0.0))
        stack = jnp.concatenate(kinds, axis=0)
        within = mm(stack.astype(BF), onehot(iota((128, 128), 0) <= iota((128, 128), 1)), 1, 0)
        totals = jnp.broadcast_to(within[:, 127:128], (144, 128)).astype(BF)
        before = mm(onehot(iota((144, 144), 0) > iota((144, 144), 1)), totals, 1, 0)
        place_all = stack * (within + before - 1.0)
        rank = place_all[0:16]
        for k in range(1, 9):
            rank = rank + place_all[16 * k:16 * (k + 1)]
        live[t] = before[128:136, :]
        small_eye = iota((48, 128), 0) == iota((48, 128), 1)
        columns = jnp.concatenate(
            [
                jnp.sum(jnp.where(small_eye, rank[d:d + 1, :], 0.0), axis=1, keepdims=True)
                for d in range(16)
            ],
            axis=0,
        )
        unorder[t] = onehot(iota((768, 768), 1) == columns)
        row = jnp.sum(
            jnp.where(iota((768, 768), 0) == iota((768, 768), 1), columns, 0.0),
            axis=0, keepdims=True,
        )
        order[t] = onehot(iota((768, 768), 0) == row)

    for j in (0, 1):
        first_arrivals(j)
    token_layout(1)
    post(0, kbuf, kgot)
    for j in (0, 1):
        second_arrivals(j, 0)
    z_arrival(1)
    pick[0] = onehot(iota((768, 512), 0) == slot_rows[0])
    for j in (0, 1):
        first_far(j)
    for j in (0, 1):
        second_arrivals(j, 1)
    z_arrival(2)
    pick[1] = onehot(iota((768, 512), 0) == slot_rows[1])
    for t in (0, 1):
        dbuf[:, t] = mm(pick[t], dout[...], 1, 0).astype(BF).reshape(16, 48, 256)

    for t in (0, 1):
        unpick[:, 768 * t:768 * (t + 1)] = onehot(iota((512, 768), 1) == slot_cols[t])
    for j in (0, 1):
        second_arrivals(j, 2)
    z_arrival(3)
    collect(0, kgot)
    slot_order(0)
    for j in (0, 1):
        second_arrivals(j, 3)
    post(5, dbuf, dgot)
    z_far()
    slot_order(1)
    for k in range(4):
        second_far(0, k)
        second_far(1, k)
    twin_arrivals()

    def project(q):
        chip = (z + 5 + q) % 8
        for j in (0, 1):
            total = mm(xg[2 * chip], wg[2 * chip, j], 1, 0)
            total += mm(xg[2 * chip + 1], wg[2 * chip + 1, j], 1, 0)
            probs[j, 0:4] += total.reshape(4, 128, 256)

    @pl.loop(0, 7)
    def _(q):
        project(q)

    twin_far()
    project(7)
    for j in (0, 1):
        for n in (0, 1):
            part = probs[j, 0:4, :, 128 * n:128 * (n + 1)].reshape(512, 128)
            qv[n, :, 128 * j:128 * (j + 1)] = part.astype(BF)

    for n in (0, 1):
        for t in (0, 1):
            sbuf[n, t] = mm(pick[t], qv[n], 1, 0).astype(BF).reshape(16, 48, 256)
            post(1 + 2 * n + t, sbuf.at[n, t], rbuf.at[n, t])
    def both(ref, lead, b):
        prev = (b + 5) % 6
        return jnp.concatenate(
            [ref[lead, 128 * b:128 * (b + 1)], ref[lead, 128 * prev:128 * (prev + 1)]], axis=0
        )

    self_pair = iota((128, 256), 0) == iota((128, 256), 1)

    collect(5, dgot)

    @pl.loop(0, 2)
    def _(t):
        rows = mm(order[t], dgot[:, t].reshape(768, 256), 1, 0).astype(BF)
        ds_[t] = rows[:, 0:128]
        ds_[2 + t] = rows[:, 128:256]

    choose = onehot(iota((8, 128), 0) == iota((8, 128), 1))

    for n in (0, 1):

        @pl.loop(0, 2)
        def _(t):
            u = 2 * n + t
            collect(1 + u, rbuf.at[n, t])
            rows = mm(order[t], rbuf[n, t].reshape(768, 256), 1, 0)
            qf = rows[:, 0:128]
            fac = key_factor(qf)
            qs[u] = qf.astype(BF)
            ks[u] = (qf * fac).astype(BF)
            vs[u] = rows[:, 128:256].astype(BF)
            for b in range(6):
                prev = (b + 5) % 6
                at = iota((1, 256), 1)
                at = jnp.where(at < 128.0, at + 128.0 * b, at - 128.0 + 128.0 * prev)
                used = jnp.concatenate([live[t, 0:1, :]] * 2, axis=1)
                scores = mm(qs[u, 128 * b:128 * (b + 1)], both(ks, u, b), 1, 1)
                scores = jnp.where(self_pair, SELF_SCORE, scores)
                scores = jnp.where(at < used, scores, MASKED_SCORE)
                top = jnp.max(scores, axis=1, keepdims=True)
                e = jnp.exp(scores - top)
                total = jnp.sum(e, axis=1, keepdims=True)
                weights = e * (1.0 / total)
                probs[u, b] = weights
                mixed = mm(weights.astype(BF), both(vs, u, b), 1, 0)
                osum[u, 128 * b:128 * (b + 1)] = mixed
                grad = ds_[u, 128 * b:128 * (b + 1)]
                pairs[u, b] = mm(grad, both(vs, u, b), 1, 1)
                vals[t, 128 * b:128 * (b + 1), 2 + n:3 + n] = jnp.sum(
                    grad.astype(F32) * mixed, axis=1, keepdims=True
                )
                vals[t, 128 * b:128 * (b + 1), n:n + 1] = top + jnp.log(total)
            if n == 1:
                high, mid, low = split3(vals[t])
                lines = pieces(
                    mm(choose, high.astype(BF), 1, 1)
                    + mm(choose, mid.astype(BF), 1, 1)
                    + mm(choose, low.astype(BF), 1, 1)
                )
                for d in range(16):
                    lbuf[d, pl.ds(pl.multiple_of(8 * t, 8), 8), 0:48] = fold3(
                        mm(lines, unorder[t, 48 * d:48 * (d + 1)], 1, 1), 8
                    )

    post(6, lbuf, lgot)
    for t in (0, 1):
        wide = jnp.concatenate([osum[t], osum[2 + t]], axis=1).astype(BF)
        obuf[:, t] = mm(unorder[t], wide, 1, 0).astype(BF).reshape(16, 48, 256)
    post(7, obuf, ogot)

    collect(6, lgot)
    here = []
    for t in (0, 1):
        high, mid, low = split3(lgot[:, 8 * t:8 * (t + 1), :].reshape(128, 128))
        found = (
            mm(high.astype(BF), rk[t], 1, 0)
            + mm(mid.astype(BF), rk[t], 1, 0)
            + mm(low.astype(BF), rk[t], 1, 0)
        )
        line = found[0:8] * hot[t, 0:1, :]
        for g in range(1, 16):
            line = line + found[8 * g:8 * (g + 1)] * hot[t, g:g + 1, :]
        here.append(line)
    top = jnp.maximum(here[0], here[1])
    log_all = top + jnp.log(jnp.exp(here[0] - top) + jnp.exp(here[1] - top))
    mix = [jnp.exp(line - log_all) for line in here]
    inner = mix[0][0:2] * here[0][2:4] + mix[1][0:2] * here[1][2:4]
    mix_lines = []
    for t in (0, 1):
        lines = jnp.concatenate([mix[t][0:2], inner, jnp.zeros((4, 512), F32)], axis=0)
        split = jnp.concatenate(split3(lines), axis=0)
        stack = jnp.concatenate([split * hot[t, g:g + 1, :] for g in range(16)], axis=0)
        back = mm(stack.astype(BF), rk[t], 1, 1)
        for g in range(16):
            mbuf[g, 8 * t:8 * (t + 1), :] = fold3(back[24 * g:24 * (g + 1)], 8)
        mix_lines.append(split)
    post(8, mbuf, mgot)
    for t in (0, 1):
        mixes[t] = mm(onehot(eye), mix_lines[t].astype(BF), 1, 1)

    collect(8, mgot)
    lane_eye = onehot(iota((48, 128), 0) == iota((48, 128), 1))
    for t in (0, 1):
        for d in range(16):
            slots[t, 48 * d:48 * (d + 1), 0:24] = mm(
                lane_eye, pieces(mgot[d, 8 * t:8 * (t + 1), :]), 1, 1
            ).astype(BF)
        vals[t] = mm(order[t], slots[t], 1, 0)

    def column(ref, t, j):
        return ref[t, :, j:j + 1] + ref[t, :, 8 + j:9 + j] + ref[t, :, 16 + j:17 + j]

    for n in (0, 1):

        @pl.loop(0, 2)
        def _(t):
            u = 2 * n + t
            sent(1 + u, sbuf.at[n, t])
            mix_col = column(vals, t, n)
            inner_col = column(vals, t, 2 + n)
            dks[...] = jnp.zeros_like(dks)
            dvs[...] = jnp.zeros_like(dvs)
            dq = []
            for b in range(6):
                prev = (b + 5) % 6
                rows = slice(128 * b, 128 * (b + 1))
                prows = slice(128 * prev, 128 * (prev + 1))
                weighted = probs[u, b] * mix_col[rows]
                grads = jnp.where(self_pair, 0.0, weighted * (pairs[u, b] - inner_col[rows]))
                grads = grads.astype(BF)
                dq.append(mm(grads, both(ks, u, b), 1, 0))
                dk = mm(grads, qs[u, rows], 0, 0)
                dv = mm(weighted.astype(BF), ds_[u, rows], 0, 0)
                dks[rows] += dk[0:128]
                dks[prows] += dk[128:256]
                dvs[rows] += dv[0:128]
                dvs[prows] += dv[128:256]
            qf = qs[u].astype(F32)
            fac = key_factor(qf)
            dk = dks[...]
            inside = jnp.sum(dk * qf, axis=1, keepdims=True)
            result = jnp.concatenate(dq, axis=0) + fac * dk - fac * fac * fac * inside * qf
            wide = jnp.concatenate([result.astype(BF), dvs[...].astype(BF)], axis=1)
            sbuf[n, t] = mm(unorder[t], wide, 1, 0).astype(BF).reshape(16, 48, 256)
            post(9 + u, sbuf.at[n, t], ggot.at[n, t])

    collect(7, ogot)
    parts = [mm(unpick[:, 768 * t:768 * (t + 1)], ogot[:, t].reshape(768, 256), 1, 0) for t in (0, 1)]
    for n in (0, 1):
        lanes = slice(128 * n, 128 * (n + 1))
        output[:, lanes] = (
            column(mixes, 0, n) * parts[0][:, lanes] + column(mixes, 1, n) * parts[1][:, lanes]
        ).astype(BF)

    for n in (0, 1):
        collect(9 + 2 * n, ggot.at[n, 0])
        rows = mm(unpick[:, 0:768], ggot[n, 0].reshape(768, 256), 1, 0)
        collect(10 + 2 * n, ggot.at[n, 1])
        rows = rows + mm(unpick[:, 768:1536], ggot[n, 1].reshape(768, 256), 1, 0)
        rows = rows.astype(BF)
        dqv[:, 128 * n:128 * (n + 1)] = rows[:, 0:128]
        dqv[:, 256 + 128 * n:256 + 128 * (n + 1)] = rows[:, 128:256]
        dqvt[128 * n:128 * (n + 1), :] = jnp.transpose(rows[:, 0:128])
        dqvt[256 + 128 * n:256 + 128 * (n + 1), :] = jnp.transpose(rows[:, 128:256])

    def term(b):
        return mm(dqv[:, 0:256], wg[b, 0], 1, 1) + mm(dqv[:, 256:512], wg[b, 1], 1, 1)

    def twin_term(k, zd):
        ttwin[zd] = term(2 * zd + 1 - c).astype(BF)
        out.start(ttwin.at[zd], tgot.at[zd], rtsem.at[k], twin)

    def my_term(zd):
        tme[zd] = term(2 * zd + c).astype(BF)

    def pair(k, zd):
        arrived(tgot.at[zd], rtsem.at[k], ssem.at[0], twin)
        tme[zd] = (tme[zd].astype(F32) + tgot[zd].astype(F32)).astype(BF)

    prim, sec = [x, y], [y, x]
    first_axis = [(east, west), (north, south)]
    second_axis = [(north, south), (east, west)]

    def grads(j, off):
        p = (sec[j] + off) % 4

        @pl.loop(1, 4)
        def _(i):
            r = (prim[j] + i) % 4
            b = r * 4 + p if j == 0 else p * 4 + r
            gsum[j, r, p] = mm(dqvt[256 * j:256 * (j + 1), :], xg[b], 1, 0).astype(BF)

    def own_grads(j):
        @pl.loop(0, 4)
        def _(p):
            r = prim[j]
            b = r * 4 + p if j == 0 else p * 4 + r
            gsum[j, r, p] = mm(dqvt[256 * j:256 * (j + 1), :], xg[b], 1, 0).astype(BF)

    offs = (2, 1, 3, 0)

    def add(ref, index, other):
        ref[index] = (ref[index].astype(F32) + other.astype(F32)).astype(BF)

    def first_sends(j, k):
        p = (sec[j] + offs[k]) % 4
        r = (prim[j] + 2) % 4
        for side in (0, 1):
            out.start(
                half(gsum.at[j, r, p], side), g1far.at[j, side, p], s1sem.at[j, k, side],
                first_axis[j][side],
            )
        for side, step in enumerate((1, 3)):
            r = (prim[j] + step) % 4
            out.start(
                half(gsum.at[j, r, p], 1 - side), half(g1near.at[j, side, p], 1 - side),
                s1sem.at[j, k, 2 + side], first_axis[j][side],
            )

    def first_relay(j, k):
        p = (sec[j] + offs[k]) % 4
        for side, step in enumerate((1, 3)):
            r = (prim[j] + step) % 4
            arrived(g1far.at[j, side, p], s1sem.at[j, k, side], ssem.at[0], first_axis[j][0])
            add(gsum, (j, r, p, pl.ds(128 * side, 128)), g1far[j, side, p])
            out.start(
                half(gsum.at[j, r, p], side), half(g1near.at[j, side, p], side),
                s1sem.at[j, k, 4 + side], first_axis[j][side],
            )

    def first_final(j, k):
        p = (sec[j] + offs[k]) % 4
        for side in (0, 1):
            near = g1near.at[j, side, p]
            arrived(half(near, 1 - side), s1sem.at[j, k, 2 + side], ssem.at[0], first_axis[j][0])
            arrived(half(near, side), s1sem.at[j, k, 4 + side], ssem.at[0], first_axis[j][0])
        r = prim[j]
        gsum[j, r, p] = (
            gsum[j, r, p].astype(F32) + g1near[j, 0, p].astype(F32) + g1near[j, 1, p].astype(F32)
        ).astype(BF)

    def second_far_send(j):
        p = (sec[j] + 2) % 4
        for side in (0, 1):
            out.start(
                half(gsum.at[j, prim[j], p], side), g2far.at[j, side], s2sem.at[j, side],
                second_axis[j][side],
            )

    def second_fresh(j, side):
        p = (sec[j] + (1, 3)[side]) % 4
        out.start(
            half(gsum.at[j, prim[j], p], 1 - side), half(g2near.at[j, side], 1 - side),
            s2sem.at[j, 2 + side], second_axis[j][side],
        )

    def second_relay(j, side):
        p = (sec[j] + (1, 3)[side]) % 4
        arrived(g2far.at[j, side], s2sem.at[j, side], ssem.at[0], second_axis[j][0])
        add(gsum, (j, prim[j], p, pl.ds(128 * side, 128)), g2far[j, side])
        out.start(
            half(gsum.at[j, prim[j], p], side), half(g2near.at[j, side], side),
            s2sem.at[j, 4 + side], second_axis[j][side],
        )

    def second_final(j, result):
        for side in (0, 1):
            near = g2near.at[j, side]
            arrived(half(near, 1 - side), s2sem.at[j, 2 + side], ssem.at[0], second_axis[j][0])
            arrived(half(near, side), s2sem.at[j, 4 + side], ssem.at[0], second_axis[j][0])
        result[...] = jnp.transpose(
            gsum[j, prim[j], sec[j]].astype(F32)
            + g2near[j, 0].astype(F32)
            + g2near[j, 1].astype(F32)
        )

    def z_start(side, step, k):
        zd = (z + 4 - step) % 8 if side == 0 else (z + 4 + step) % 8
        out.start(
            rows256(tme.at[zd], k), rows256(zgot.at[side, step], k), rzsem.at[side, step, k],
            (up, down)[side],
        )

    def z_relay(step, own):
        for side in (0, 1):
            k = side if own else 1 - side
            zd = (z + 4 - step) % 8 if side == 0 else (z + 4 + step) % 8
            rows = pl.ds(256 * k, 256)
            arrived(zgot.at[side, step - 1, rows], rzsem.at[side, step - 1, k], ssem.at[0], up)
            add(tme, (zd, rows), zgot[side, step - 1, rows])
            z_start(side, step, k)

    zorder = [(z + off) % 8 for off in (4, 3, 5, 2, 6, 1, 7, 0)]

    def both_terms(k):
        twin_term(k, zorder[k])
        my_term(zorder[k])

    twin_term(0, zorder[0])
    for j in (0, 1):
        grads(j, offs[0])
        first_sends(j, 0)
    my_term(zorder[0])
    both_terms(1)
    both_terms(2)
    pair(0, zorder[0])
    for side in (0, 1):
        z_start(side, 0, side)
    for j in (0, 1):
        grads(j, offs[1])
        first_sends(j, 1)
    pair(1, zorder[1])
    pair(2, zorder[2])
    for side in (0, 1):
        z_start(side, 1, 1 - side)
    for k in (2, 3):
        for j in (0, 1):
            grads(j, offs[k])
            first_sends(j, k)
    both_terms(3)
    both_terms(4)
    for j in (0, 1):
        first_relay(j, 0)
    z_relay(1, True)
    for j in (0, 1):
        first_relay(j, 1)
        own_grads(j)
    both_terms(5)
    both_terms(6)
    pair(3, zorder[3])
    pair(4, zorder[4])
    z_relay(2, False)
    for j in (0, 1):
        first_relay(j, 2)
        first_relay(j, 3)
    both_terms(7)
    z_relay(2, True)
    for j in (0, 1):
        first_final(j, 0)
        second_far_send(j)
    pair(5, zorder[5])
    pair(6, zorder[6])
    z_relay(3, False)
    for side in (0, 1):
        for j in (0, 1):
            first_final(j, 1 + side)
            second_fresh(j, side)
    z_relay(3, True)
    for j in (0, 1):
        for side in (0, 1):
            second_relay(j, side)
    pair(7, zorder[7])
    for j in (0, 1):
        first_final(j, 3)
    for side in (0, 1):
        for k in (1 - side, side):
            arrived(rows256(zgot.at[side, 3], k), rzsem.at[side, 3, k], ssem.at[0], up)
    ig[...] = (
        tme[z].astype(F32) + zgot[0, 3].astype(F32) + zgot[1, 3].astype(F32)
    ).astype(BF)
    second_final(0, gq)
    second_final(1, gv)
    out.finish()
    sent(0, kbuf)
    for u in range(4):
        sent(9 + u, sbuf.at[u // 2, u % 2])
    sent(5, dbuf)
    sent(6, lbuf)
    sent(7, obuf)
    sent(8, mbuf)


def copy_kernel(*refs):
    for source, target in zip(refs[0:4], refs[4:8]):
        target[...] = source[...]


def per_device(layer_input, qk_weight, value_weight, groups, buckets, out_cotangent):
    vm = pl.BlockSpec(memory_space=pltpu.VMEM)
    V = pltpu.VMEM
    shapes = (
        jax.ShapeDtypeStruct((512, 256), BF),
        jax.ShapeDtypeStruct((512, 256), BF),
        jax.ShapeDtypeStruct((256, 256), F32),
        jax.ShapeDtypeStruct((256, 256), F32),
    )
    results = pl.pallas_call(
        whole_kernel,
        out_shape=shapes,
        in_specs=[vm] * 6,
        out_specs=(vm,) * 4,
        scratch_shapes=[
            V((16, 512, 256), BF),
            V((16, 2, 256, 256), BF),
            V((512, 512), BF),
            V((512, 512), BF),
            V((2, 512, 256), BF),
            V((2, 768, 512), BF),
            V((512, 1536), BF),
            V((2, 768, 768), BF),
            V((2, 768, 768), BF),
            V((2, 8, 128), F32),
            V((2, 16, 512), F32),
            V((2, 128, 512), BF),
            V((16, 8, 128), F32),
            V((16, 8, 128), F32),
            V((2, 2, 16, 48, 256), BF),
            V((2, 2, 16, 48, 256), BF),
            V((16, 2, 48, 256), BF),
            V((16, 2, 48, 256), BF),
            V((16, 2, 48, 256), BF),
            V((16, 2, 48, 256), BF),
            V((2, 2, 16, 48, 256), BF),
            V((16, 16, 128), F32),
            V((16, 16, 128), F32),
            V((16, 16, 128), F32),
            V((16, 16, 128), F32),
            V((4, 768, 128), BF),
            V((4, 768, 128), BF),
            V((4, 768, 128), BF),
            V((4, 768, 128), BF),
            V((4, 6, 128, 256), F32),
            V((4, 6, 128, 256), F32),
            V((4, 768, 128), F32),
            V((2, 768, 128), F32),
            V((2, 768, 128), BF),
            V((768, 128), F32),
            V((768, 128), F32),
            V((2, 512, 24), F32),
            V((8, 512, 256), BF),
            V((8, 512, 256), BF),
            V((8, 512, 256), BF),
            V((2, 4, 512, 256), BF),
            V((2, 4, 4, 256, 256), BF),
            V((2, 2, 4, 128, 256), BF),
            V((2, 2, 4, 256, 256), BF),
            V((2, 2, 128, 256), BF),
            V((2, 2, 256, 256), BF),
            pltpu.SemaphoreType.DMA((13,)),
            pltpu.SemaphoreType.DMA((13,)),
            pltpu.SemaphoreType.DMA((176,)),
            pltpu.SemaphoreType.DMA((2, 4, 2)),
            pltpu.SemaphoreType.DMA((2, 5)),
            pltpu.SemaphoreType.DMA((2, 4)),
            pltpu.SemaphoreType.DMA((2, 4, 4)),
            pltpu.SemaphoreType.DMA((8,)),
            pltpu.SemaphoreType.DMA((2, 4, 2)),
            pltpu.SemaphoreType.DMA((2, 4, 6)),
            pltpu.SemaphoreType.DMA((2, 6)),
        ],
        compiler_params=pltpu.CompilerParams(
            collective_id=0, has_side_effects=True, vmem_limit_bytes=63 * 1024 * 1024
        ),
        name="hashed_attention_step",
    )(layer_input, qk_weight, value_weight, out_cotangent, jnp.transpose(groups, (0, 2, 1)), buckets)
    return pl.pallas_call(
        copy_kernel,
        out_shape=shapes,
        in_specs=[vm] * 4,
        out_specs=(vm,) * 4,
        name="write_results",
    )(*results)


def solution(mesh):
    return jax.shard_map(
        per_device,
        mesh=mesh,
        in_specs=(
            P("seq", "head"),
            P("seq", "head"),
            P("seq", "head"),
            P(None, "seq", None),
            P(None, "seq"),
            P("seq", "head"),
        ),
        out_specs=(P("seq", "head"), P("seq", "head"), P("seq", "head"), P("seq", "head")),
        check_vma=False,
    )
```

```python
import math

import jax
import jax.numpy as jnp
from jax import lax
from jax.experimental import pallas as pl
from jax.experimental.pallas import tpu as pltpu
from jax.sharding import PartitionSpec as P

HEAD_DIM = 128
ROUNDS = 2
EPSILON = 1e-06
SELF_SCORE = -100000.0
MASKED_SCORE = -1000000000.0


MESH = pl.DeviceIdType.MESH
BF = jnp.bfloat16
F32 = jnp.float32


def rcopy(src, dst, ssem, rsem, dev):
    return pltpu.make_async_remote_copy(
        src_ref=src, dst_ref=dst, send_sem=ssem, recv_sem=rsem, device_id=dev, device_id_type=MESH
    )


class Sends:
    def __init__(self, sems):
        self.sems, self.used, self.open = sems, 0, []

    def start(self, src, dst, rsem, dev):
        copy = rcopy(src, dst, self.sems.at[self.used], rsem, dev)
        copy.start()
        self.used += 1
        self.open.append(copy)

    def finish(self):
        for copy in self.open:
            copy.wait_send()
        self.open = []


def arrived(ref, rsem, ssem, dev):
    rcopy(ref, ref, ssem, rsem, dev).wait_recv()


def place():
    s, h = lax.axis_index("seq"), lax.axis_index("head")
    return s, h, s // 4, s % 4, h // 2, h % 2


def enter(devices):
    barrier = pltpu.get_barrier_semaphore()
    for dev in devices:
        pl.semaphore_signal(barrier, inc=1, device_id=dev, device_id_type=MESH)
    pl.semaphore_wait(barrier, len(devices))


def ring_neighbours():
    s, h, x, y, z, c = place()
    east, west = (((x + 1) % 4) * 4 + y, h), (((x + 3) % 4) * 4 + y, h)
    north, south = (x * 4 + (y + 1) % 4, h), (x * 4 + (y + 3) % 4, h)
    up, down = (s, ((z + 1) % 8) * 2 + c), (s, ((z + 7) % 8) * 2 + c)
    twin = (s, 2 * z + 1 - c)
    return east, west, north, south, up, down, twin


def mm(a, b, ca, cb):
    return lax.dot_general(a, b, (((ca,), (cb,)), ((), ())), preferred_element_type=F32)


def iota(shape, axis):
    return lax.broadcasted_iota(jnp.int32, shape, axis).astype(F32)


def onehot(mask):
    return jnp.where(mask, 1.0, 0.0).astype(BF)


def split3(v):
    high = v.astype(BF).astype(F32)
    rest = v - high
    mid = rest.astype(BF).astype(F32)
    return high, mid, rest - mid


def pieces(v):
    return jnp.concatenate(split3(v), axis=0).astype(BF)


def fold3(v, n):
    return v[0:n] + v[n:2 * n] + v[2 * n:3 * n]


def key_factor(qf):
    mean = jnp.mean(qf * qf, axis=1, keepdims=True)
    return lax.rsqrt(mean + EPSILON) * (1.0 / math.sqrt(HEAD_DIM))


def whole_kernel(
    x_ref, wq_ref, wv_ref, dout_ref, grow, brow,
    output, ig, gq, gv,
    xg, wg, dqv, dqvt, dout,
    qv, pick, unpick, order, unorder, live, hot, rk,
    kbuf, kgot, sbuf, rbuf, dbuf, dgot, obuf, ogot, ggot, lbuf, lgot, mbuf, mgot,
    qs, ks, vs, ds_, probs, pairs, osum, vals, slots, mixes,
    tme, ttwin, tgot, zgot, gsum, g1far, g1near, g2far, g2near,
    lsem, asend, arecv, ssem, zsem, tsem, w1sem, w2sem, rtsem, rzsem, s1sem, s2sem,
):
    s, h, x, y, z, c = place()
    east, west, north, south, up, down, twin = ring_neighbours()
    local = [
        pltpu.make_async_copy(x_ref, xg.at[h], lsem.at[0]),
        pltpu.make_async_copy(wq_ref, wg.at[s, 0], lsem.at[1]),
        pltpu.make_async_copy(wv_ref, wg.at[s, 1], lsem.at[2]),
        pltpu.make_async_copy(dout_ref, dout, lsem.at[3]),
    ]
    for copy in local:
        copy.start()
    barrier = pltpu.get_barrier_semaphore()

    @pl.loop(1, 16)
    def _(k):
        pl.semaphore_signal(barrier, inc=1, device_id=((s + k) % 16, h), device_id_type=MESH)

    for dev in (up, down, twin):
        pl.semaphore_signal(barrier, inc=1, device_id=dev, device_id_type=MESH)
    pl.semaphore_wait(barrier, 18)
    out = Sends(ssem)

    def rows256(ref, k):
        return ref.at[pl.ds(256 * k, 256)]

    def post(n, src, dst):
        @pl.loop(1, 16)
        def _(k):
            d = (s + k) % 16
            rcopy(src.at[d], dst.at[s], asend.at[n], arecv.at[n], (d, h)).start()

        dst[s] = src[s]

    def collect(n, dst):
        part = dst.at[pl.ds(0, 15)]
        rcopy(part, part, asend.at[n], arecv.at[n], (s, h)).wait_recv()

    def sent(n, src):
        part = src.at[pl.ds(0, 15)]
        rcopy(part, part, asend.at[n], arecv.at[n], (s, h)).wait_send()

    first_axis = [(north, south), (east, west)]
    second_axis = [(east, west), (north, south)]
    prim, sec = [y, x], [x, y]
    own = [wq_ref, wv_ref]

    def wslot(j, p, r):
        return wg.at[r * 4 + p if j == 0 else p * 4 + r, j]

    def half(ref, k):
        return ref.at[pl.ds(128 * k, 128)]

    for j in (0, 1):
        plus, minus = first_axis[j]
        dst = wslot(j, prim[j], sec[j])
        out.start(own[j], dst, w1sem.at[j, 0], plus)
        out.start(own[j], dst, w1sem.at[j, 1], minus)
    for k in (0, 1):
        rows = pl.ds(256 * k, 256)
        out.start(x_ref.at[rows], xg.at[h, rows], zsem.at[0, 0, k], up)
        out.start(x_ref.at[rows], xg.at[h, rows], zsem.at[1, 0, k], down)

    def second_send(j, k, p, src):
        plus, minus = second_axis[j]
        dst = wslot(j, p, sec[j])
        out.start(src, dst, w2sem.at[j, k, 0], plus)
        out.start(src, dst, w2sem.at[j, k, 1], minus)

    for j in (0, 1):
        second_send(j, 0, prim[j], own[j])
    out.start(x_ref, xg.at[h], tsem.at[0, 0], twin)

    def first_arrivals(j):
        plus, minus = first_axis[j]
        for k, (step, onward) in enumerate(((3, plus), (1, minus))):
            p = (prim[j] + step) % 4
            ref = wslot(j, p, sec[j])
            arrived(ref, w1sem.at[j, k], ssem.at[0], plus)
            out.start(half(ref, k), half(ref, k), w1sem.at[j, 2 + k], onward)
            second_send(j, 1 + k, p, ref)

    def first_far(j):
        p = (prim[j] + 2) % 4
        ref = wslot(j, p, sec[j])
        for k in (0, 1):
            arrived(half(ref, k), w1sem.at[j, 2 + k], ssem.at[0], first_axis[j][0])
        second_send(j, 3, p, ref)

    offsets = (0, 3, 1, 2)

    def second_arrivals(j, k):
        p = (prim[j] + offsets[k]) % 4
        plus, minus = second_axis[j]
        for side, (step, onward) in enumerate(((3, plus), (1, minus))):
            ref = wslot(j, p, (sec[j] + step) % 4)
            arrived(ref, w2sem.at[j, k, side], ssem.at[0], plus)
            out.start(half(ref, side), half(ref, side), w2sem.at[j, k, 2 + side], onward)

    def second_far(j, k):
        p = (prim[j] + offsets[k]) % 4
        ref = wslot(j, p, (sec[j] + 2) % 4)
        for side in (0, 1):
            arrived(half(ref, side), w2sem.at[j, k, 2 + side], ssem.at[0], second_axis[j][0])

    def z_arrival(dist):
        for k in (0, 1):
            for side, (step, onward) in enumerate(((8 - dist, up), (dist, down))):
                ref = rows256(xg.at[((z + step) % 8) * 2 + c], k)
                arrived(ref, zsem.at[side, dist - 1, k], ssem.at[0], up)
                if dist < 3 or k == side:
                    out.start(ref, ref, zsem.at[side, dist, k], onward)
        for side, step in enumerate((8 - dist, dist)):
            ref = xg.at[((z + step) % 8) * 2 + c]
            out.start(ref, ref, tsem.at[side, dist], twin)

    def z_far():
        ref = xg.at[((z + 4) % 8) * 2 + c]
        for side in (0, 1):
            arrived(rows256(ref, side), zsem.at[side, 3, side], ssem.at[0], up)
            out.start(rows256(ref, side), rows256(ref, side), tsem.at[side, 4], twin)

    def twin_arrivals():
        arrived(xg.at[2 * z + 1 - c], tsem.at[0, 0], ssem.at[0], twin)
        for dist in (1, 2, 3):
            for side, step in enumerate((8 - dist, dist)):
                arrived(xg.at[((z + step) % 8) * 2 + 1 - c], tsem.at[side, dist], ssem.at[0], twin)

    def twin_far():
        for side in (0, 1):
            ref = xg.at[((z + 4) % 8) * 2 + 1 - c]
            arrived(rows256(ref, side), tsem.at[side, 4], ssem.at[0], twin)


    kbuf[...] = jnp.zeros_like(kbuf)
    lbuf[...] = jnp.zeros_like(lbuf)
    vals[...] = jnp.zeros_like(vals)
    slots[...] = jnp.zeros_like(slots)
    upper = onehot(iota((512, 512), 0) <= iota((512, 512), 1))
    eye = iota((512, 512), 0) == iota((512, 512), 1)
    for j in (0, 1):
        probs[j, 0:4] = jnp.zeros((4, 128, 256), F32)
    slot_rows, slot_cols = [], []

    def token_layout(t):
        g = grow[t].astype(F32)
        member = jnp.where(iota((16, 512), 0) == g, 1.0, 0.0)
        count = mm(member.astype(BF), upper, 1, 0)
        rank = jnp.sum(member * count, axis=0, keepdims=True) - 1.0
        slot = g * 48.0 + rank
        slot_col = jnp.sum(jnp.where(eye, slot, 0.0), axis=1, keepdims=True)
        hot[t] = member
        rk[t] = onehot(iota((128, 512), 0) == rank)
        slot_rows.append(slot)
        slot_cols.append(slot_col)
        named = member * (brow[t:t + 1, :].astype(F32) + 1.0)
        sent_keys = mm(named.astype(BF), rk[t], 1, 1)
        for d in range(16):
            kbuf[d, t:t + 1, :] = sent_keys[d:d + 1, :]
    token_layout(0)

    def slot_order(t):
        tag = jnp.concatenate([kgot[d, t:t + 1, :] for d in range(16)], axis=0)
        usable = iota((16, 128), 1) < 48.0
        kinds = [jnp.where(tag == float(k), 1.0, 0.0) for k in range(1, 9)]
        kinds.append(jnp.where(usable, jnp.where(tag == 0.0, 1.0, 0.0), 0.0))
        stack = jnp.concatenate(kinds, axis=0)
        within = mm(stack.astype(BF), onehot(iota((128, 128), 0) <= iota((128, 128), 1)), 1, 0)
        totals = jnp.broadcast_to(within[:, 127:128], (144, 128)).astype(BF)
        before = mm(onehot(iota((144, 144), 0) > iota((144, 144), 1)), totals, 1, 0)
        place_all = stack * (within + before - 1.0)
        rank = place_all[0:16]
        for k in range(1, 9):
            rank = rank + place_all[16 * k:16 * (k + 1)]
        live[t] = before[128:136, :]
        small_eye = iota((48, 128), 0) == iota((48, 128), 1)
        columns = jnp.concatenate(
            [
                jnp.sum(jnp.where(small_eye, rank[d:d + 1, :], 0.0), axis=1, keepdims=True)
                for d in range(16)
            ],
            axis=0,
        )
        unorder[t] = onehot(iota((768, 768), 1) == columns)
        row = jnp.sum(
            jnp.where(iota((768, 768), 0) == iota((768, 768), 1), columns, 0.0),
            axis=0, keepdims=True,
        )
        order[t] = onehot(iota((768, 768), 0) == row)

    for j in (0, 1):
        first_arrivals(j)
    token_layout(1)
    post(0, kbuf, kgot)
    for j in (0, 1):
        second_arrivals(j, 0)
    z_arrival(1)
    pick[0] = onehot(iota((768, 512), 0) == slot_rows[0])
    for j in (0, 1):
        first_far(j)
    for j in (0, 1):
        second_arrivals(j, 1)
    z_arrival(2)
    pick[1] = onehot(iota((768, 512), 0) == slot_rows[1])
    for copy in local:
        copy.wait()
    for t in (0, 1):
        dbuf[:, t] = mm(pick[t], dout[...], 1, 0).astype(BF).reshape(16, 48, 256)

    for t in (0, 1):
        unpick[:, 768 * t:768 * (t + 1)] = onehot(iota((512, 768), 1) == slot_cols[t])
    for j in (0, 1):
        second_arrivals(j, 2)
    z_arrival(3)
    collect(0, kgot)
    slot_order(0)
    for j in (0, 1):
        second_arrivals(j, 3)
    post(5, dbuf, dgot)
    z_far()
    slot_order(1)
    for k in range(4):
        second_far(0, k)
        second_far(1, k)
    twin_arrivals()

    def project(q):
        chip = (z + 5 + q) % 8
        for j in (0, 1):
            total = mm(xg[2 * chip], wg[2 * chip, j], 1, 0)
            total += mm(xg[2 * chip + 1], wg[2 * chip + 1, j], 1, 0)
            probs[j, 0:4] += total.reshape(4, 128, 256)

    @pl.loop(0, 7)
    def _(q):
        project(q)

    twin_far()
    project(7)
    for j in (0, 1):
        for n in (0, 1):
            part = probs[j, 0:4, :, 128 * n:128 * (n + 1)].reshape(512, 128)
            qv[n, :, 128 * j:128 * (j + 1)] = part.astype(BF)

    for n in (0, 1):
        for t in (0, 1):
            sbuf[n, t] = mm(pick[t], qv[n], 1, 0).astype(BF).reshape(16, 48, 256)
            post(1 + 2 * n + t, sbuf.at[n, t], rbuf.at[n, t])
    def both(ref, lead, b):
        prev = (b + 5) % 6
        return jnp.concatenate(
            [ref[lead, 128 * b:128 * (b + 1)], ref[lead, 128 * prev:128 * (prev + 1)]], axis=0
        )

    self_pair = iota((128, 256), 0) == iota((128, 256), 1)

    collect(5, dgot)

    @pl.loop(0, 2)
    def _(t):
        rows = mm(order[t], dgot[:, t].reshape(768, 256), 1, 0).astype(BF)
        ds_[t] = rows[:, 0:128]
        ds_[2 + t] = rows[:, 128:256]

    choose = onehot(iota((8, 128), 0) == iota((8, 128), 1))

    for n in (0, 1):

        @pl.loop(0, 2)
        def _(t):
            u = 2 * n + t
            collect(1 + u, rbuf.at[n, t])
            rows = mm(order[t], rbuf[n, t].reshape(768, 256), 1, 0)
            qf = rows[:, 0:128]
            fac = key_factor(qf)
            qs[u] = qf.astype(BF)
            ks[u] = (qf * fac).astype(BF)
            vs[u] = rows[:, 128:256].astype(BF)
            used = jnp.concatenate([live[t, 0:1, :]] * 2, axis=1)
            parts = []
            for b in range(6):
                prev = (b + 5) % 6
                at = iota((1, 256), 1)
                at = jnp.where(at < 128.0, at + 128.0 * b, at - 128.0 + 128.0 * prev)
                part = mm(qs[u, 128 * b:128 * (b + 1)], both(ks, u, b), 1, 1)
                part = jnp.where(self_pair, SELF_SCORE, part)
                parts.append(jnp.where(at < used, part, MASKED_SCORE))
                pairs[u, b] = mm(ds_[u, 128 * b:128 * (b + 1)], both(vs, u, b), 1, 1)
            scores = jnp.concatenate(parts, axis=0)
            top = jnp.max(scores, axis=1, keepdims=True)
            e = jnp.exp(scores - top)
            total = jnp.sum(e, axis=1, keepdims=True)
            weights = e * (1.0 / total)
            probs[u] = weights.reshape(6, 128, 256)
            packed = weights.astype(BF)
            mixed = jnp.concatenate(
                [mm(packed[128 * b:128 * (b + 1)], both(vs, u, b), 1, 0) for b in range(6)], axis=0
            )
            osum[u] = mixed
            vals[t, :, n:n + 1] = top + jnp.log(total)
            vals[t, :, 2 + n:3 + n] = jnp.sum(ds_[u].astype(F32) * mixed, axis=1, keepdims=True)
            if n == 1:
                high, mid, low = split3(vals[t])
                lines = pieces(
                    mm(choose, high.astype(BF), 1, 1)
                    + mm(choose, mid.astype(BF), 1, 1)
                    + mm(choose, low.astype(BF), 1, 1)
                )
                for d in range(16):
                    lbuf[d, pl.ds(pl.multiple_of(8 * t, 8), 8), 0:48] = fold3(
                        mm(lines, unorder[t, 48 * d:48 * (d + 1)], 1, 1), 8
                    )

    post(6, lbuf, lgot)
    for t in (0, 1):
        wide = jnp.concatenate([osum[t], osum[2 + t]], axis=1).astype(BF)
        obuf[:, t] = mm(unorder[t], wide, 1, 0).astype(BF).reshape(16, 48, 256)
    collect(6, lgot)
    here = []
    for t in (0, 1):
        high, mid, low = split3(lgot[:, 8 * t:8 * (t + 1), :].reshape(128, 128))
        found = (
            mm(high.astype(BF), rk[t], 1, 0)
            + mm(mid.astype(BF), rk[t], 1, 0)
            + mm(low.astype(BF), rk[t], 1, 0)
        )
        line = found[0:8] * hot[t, 0:1, :]
        for g in range(1, 16):
            line = line + found[8 * g:8 * (g + 1)] * hot[t, g:g + 1, :]
        here.append(line)
    top = jnp.maximum(here[0], here[1])
    log_all = top + jnp.log(jnp.exp(here[0] - top) + jnp.exp(here[1] - top))
    mix = [jnp.exp(line - log_all) for line in here]
    inner = mix[0][0:2] * here[0][2:4] + mix[1][0:2] * here[1][2:4]
    mix_lines = []
    for t in (0, 1):
        lines = jnp.concatenate([mix[t][0:2], inner, jnp.zeros((4, 512), F32)], axis=0)
        split = jnp.concatenate(split3(lines), axis=0)
        stack = jnp.concatenate([split * hot[t, g:g + 1, :] for g in range(16)], axis=0)
        back = mm(stack.astype(BF), rk[t], 1, 1)
        for g in range(16):
            mbuf[g, 8 * t:8 * (t + 1), :] = fold3(back[24 * g:24 * (g + 1)], 8)
        mix_lines.append(split)
    post(8, mbuf, mgot)
    post(7, obuf, ogot)
    for t in (0, 1):
        mixes[t] = mm(onehot(eye), mix_lines[t].astype(BF), 1, 1)

    collect(8, mgot)
    lane_eye = onehot(iota((48, 128), 0) == iota((48, 128), 1))
    for t in (0, 1):
        for d in range(16):
            slots[t, 48 * d:48 * (d + 1), 0:24] = mm(
                lane_eye, pieces(mgot[d, 8 * t:8 * (t + 1), :]), 1, 1
            ).astype(BF)
        vals[t] = mm(order[t], slots[t], 1, 0)

    def column(ref, t, j):
        return ref[t, :, j:j + 1] + ref[t, :, 8 + j:9 + j] + ref[t, :, 16 + j:17 + j]

    for n in (0, 1):

        @pl.loop(0, 2)
        def _(t):
            u = 2 * n + t
            sent(1 + u, sbuf.at[n, t])
            mix_col = column(vals, t, n)
            inner_col = column(vals, t, 2 + n)
            weighted = probs[u].reshape(768, 256) * mix_col
            grads = weighted * (pairs[u].reshape(768, 256) - inner_col)
            self_all = jnp.concatenate([jnp.where(self_pair, 0.0, 1.0)] * 6, axis=0)
            grads = jnp.where(self_all == 0.0, 0.0, grads).astype(BF)
            weighted = weighted.astype(BF)
            blocks = [slice(128 * b, 128 * (b + 1)) for b in range(6)]
            dq = [mm(grads[blocks[b]], both(ks, u, b), 1, 0) for b in range(6)]
            dk = [mm(grads[blocks[b]], qs[u, blocks[b]], 0, 0) for b in range(6)]
            dv = [mm(weighted[blocks[b]], ds_[u, blocks[b]], 0, 0) for b in range(6)]

            def folded(grad):
                return jnp.concatenate(
                    [grad[b][0:128] + grad[(b + 1) % 6][128:256] for b in range(6)], axis=0
                )

            qf = qs[u].astype(F32)
            fac = key_factor(qf)
            dk = folded(dk)
            inside = jnp.sum(dk * qf, axis=1, keepdims=True)
            result = jnp.concatenate(dq, axis=0) + fac * dk - fac * fac * fac * inside * qf
            wide = jnp.concatenate([result.astype(BF), folded(dv).astype(BF)], axis=1)
            sbuf[n, t] = mm(unorder[t], wide, 1, 0).astype(BF).reshape(16, 48, 256)
            post(9 + u, sbuf.at[n, t], ggot.at[n, t])

    collect(7, ogot)
    parts = [mm(unpick[:, 768 * t:768 * (t + 1)], ogot[:, t].reshape(768, 256), 1, 0) for t in (0, 1)]
    for n in (0, 1):
        lanes = slice(128 * n, 128 * (n + 1))
        output[:, lanes] = (
            column(mixes, 0, n) * parts[0][:, lanes] + column(mixes, 1, n) * parts[1][:, lanes]
        ).astype(BF)

    for n in (0, 1):
        collect(9 + 2 * n, ggot.at[n, 0])
        rows = mm(unpick[:, 0:768], ggot[n, 0].reshape(768, 256), 1, 0)
        collect(10 + 2 * n, ggot.at[n, 1])
        rows = rows + mm(unpick[:, 768:1536], ggot[n, 1].reshape(768, 256), 1, 0)
        rows = rows.astype(BF)
        dqv[:, 128 * n:128 * (n + 1)] = rows[:, 0:128]
        dqv[:, 256 + 128 * n:256 + 128 * (n + 1)] = rows[:, 128:256]
        dqvt[128 * n:128 * (n + 1), :] = jnp.transpose(rows[:, 0:128])
        dqvt[256 + 128 * n:256 + 128 * (n + 1), :] = jnp.transpose(rows[:, 128:256])

    def term(b):
        return mm(dqv[:, 0:256], wg[b, 0], 1, 1) + mm(dqv[:, 256:512], wg[b, 1], 1, 1)

    def twin_term(k, zd):
        ttwin[zd] = term(2 * zd + 1 - c).astype(BF)
        out.start(ttwin.at[zd], tgot.at[zd], rtsem.at[k], twin)

    def my_term(zd):
        tme[zd] = term(2 * zd + c).astype(BF)

    def pair(k, zd):
        arrived(tgot.at[zd], rtsem.at[k], ssem.at[0], twin)
        tme[zd] = (tme[zd].astype(F32) + tgot[zd].astype(F32)).astype(BF)

    prim, sec = [x, y], [y, x]
    first_axis = [(east, west), (north, south)]
    second_axis = [(north, south), (east, west)]

    def grads(j, off):
        p = (sec[j] + off) % 4

        @pl.loop(0, 2)
        def _(i):
            r = (prim[j] + 2 * i + 1) % 4
            b = r * 4 + p if j == 0 else p * 4 + r
            gsum[j, r, p] = mm(dqvt[256 * j:256 * (j + 1), :], xg[b], 1, 0).astype(BF)

    def own_grads(j):
        @pl.loop(0, 4)
        def _(p):
            r = prim[j]
            b = r * 4 + p if j == 0 else p * 4 + r
            gsum[j, r, p] = mm(dqvt[256 * j:256 * (j + 1), :], xg[b], 1, 0).astype(BF)

    offs = (2, 1, 3, 0)

    def add(ref, index, other):
        ref[index] = (ref[index].astype(F32) + other.astype(F32)).astype(BF)

    def first_far_sends(j, k):
        p = (sec[j] + offs[k]) % 4
        r = (prim[j] + 2) % 4
        b = r * 4 + p if j == 0 else p * 4 + r
        gsum[j, r, p] = mm(dqvt[256 * j:256 * (j + 1), :], xg[b], 1, 0).astype(BF)
        for side in (0, 1):
            out.start(
                half(gsum.at[j, r, p], side), g1far.at[j, side, p], s1sem.at[j, k, side],
                first_axis[j][side],
            )

    def first_sends(j, k):
        p = (sec[j] + offs[k]) % 4
        for side, step in enumerate((1, 3)):
            r = (prim[j] + step) % 4
            out.start(
                half(gsum.at[j, r, p], 1 - side), half(g1near.at[j, side, p], 1 - side),
                s1sem.at[j, k, 2 + side], first_axis[j][side],
            )

    def first_relay(j, k):
        p = (sec[j] + offs[k]) % 4
        for side, step in enumerate((1, 3)):
            r = (prim[j] + step) % 4
            arrived(g1far.at[j, side, p], s1sem.at[j, k, side], ssem.at[0], first_axis[j][0])
            add(gsum, (j, r, p, pl.ds(128 * side, 128)), g1far[j, side, p])
            out.start(
                half(gsum.at[j, r, p], side), half(g1near.at[j, side, p], side),
                s1sem.at[j, k, 4 + side], first_axis[j][side],
            )

    def first_final(j, k):
        p = (sec[j] + offs[k]) % 4
        for side in (0, 1):
            near = g1near.at[j, side, p]
            arrived(half(near, 1 - side), s1sem.at[j, k, 2 + side], ssem.at[0], first_axis[j][0])
            arrived(half(near, side), s1sem.at[j, k, 4 + side], ssem.at[0], first_axis[j][0])
        r = prim[j]
        gsum[j, r, p] = (
            gsum[j, r, p].astype(F32) + g1near[j, 0, p].astype(F32) + g1near[j, 1, p].astype(F32)
        ).astype(BF)

    def second_far_send(j):
        p = (sec[j] + 2) % 4
        for side in (0, 1):
            out.start(
                half(gsum.at[j, prim[j], p], side), g2far.at[j, side], s2sem.at[j, side],
                second_axis[j][side],
            )

    def second_fresh(j, side):
        p = (sec[j] + (1, 3)[side]) % 4
        out.start(
            half(gsum.at[j, prim[j], p], 1 - side), half(g2near.at[j, side], 1 - side),
            s2sem.at[j, 2 + side], second_axis[j][side],
        )

    def second_relay(j, side):
        p = (sec[j] + (1, 3)[side]) % 4
        arrived(g2far.at[j, side], s2sem.at[j, side], ssem.at[0], second_axis[j][0])
        add(gsum, (j, prim[j], p, pl.ds(128 * side, 128)), g2far[j, side])
        out.start(
            half(gsum.at[j, prim[j], p], side), half(g2near.at[j, side], side),
            s2sem.at[j, 4 + side], second_axis[j][side],
        )

    def second_final(j, result):
        for side in (0, 1):
            near = g2near.at[j, side]
            arrived(half(near, 1 - side), s2sem.at[j, 2 + side], ssem.at[0], second_axis[j][0])
            arrived(half(near, side), s2sem.at[j, 4 + side], ssem.at[0], second_axis[j][0])
        result[...] = jnp.transpose(
            gsum[j, prim[j], sec[j]].astype(F32)
            + g2near[j, 0].astype(F32)
            + g2near[j, 1].astype(F32)
        )

    def z_start(side, step, k):
        zd = (z + 4 - step) % 8 if side == 0 else (z + 4 + step) % 8
        out.start(
            rows256(tme.at[zd], k), rows256(zgot.at[side, step], k), rzsem.at[side, step, k],
            (up, down)[side],
        )

    def z_relay(step, own):
        for side in (0, 1):
            k = side if own else 1 - side
            zd = (z + 4 - step) % 8 if side == 0 else (z + 4 + step) % 8
            rows = pl.ds(256 * k, 256)
            arrived(zgot.at[side, step - 1, rows], rzsem.at[side, step - 1, k], ssem.at[0], up)
            add(tme, (zd, rows), zgot[side, step - 1, rows])
            z_start(side, step, k)

    zorder = [(z + off) % 8 for off in (4, 3, 5, 2, 6, 1, 7, 0)]

    def both_terms(k):
        twin_term(k, zorder[k])
        my_term(zorder[k])

    twin_term(0, zorder[0])
    for j in (0, 1):
        first_far_sends(j, 0)
    for j in (0, 1):
        grads(j, offs[0])
        first_sends(j, 0)
    my_term(zorder[0])
    both_terms(1)
    both_terms(2)
    pair(0, zorder[0])
    for side in (0, 1):
        z_start(side, 0, side)
    for j in (0, 1):
        first_far_sends(j, 1)
        grads(j, offs[1])
        first_sends(j, 1)
    pair(1, zorder[1])
    pair(2, zorder[2])
    for side in (0, 1):
        z_start(side, 1, 1 - side)
    for k in (2, 3):
        for j in (0, 1):
            first_far_sends(j, k)
            grads(j, offs[k])
            first_sends(j, k)
    both_terms(3)
    both_terms(4)
    for j in (0, 1):
        first_relay(j, 0)
    z_relay(1, True)
    for j in (0, 1):
        first_relay(j, 1)
        own_grads(j)
    both_terms(5)
    both_terms(6)
    pair(3, zorder[3])
    pair(4, zorder[4])
    z_relay(2, False)
    for j in (0, 1):
        first_relay(j, 2)
        first_relay(j, 3)
    both_terms(7)
    z_relay(2, True)
    for j in (0, 1):
        first_final(j, 0)
        second_far_send(j)
    pair(5, zorder[5])
    pair(6, zorder[6])
    z_relay(3, False)
    for side in (0, 1):
        for j in (0, 1):
            first_final(j, 1 + side)
            second_fresh(j, side)
    z_relay(3, True)
    for j in (0, 1):
        for side in (0, 1):
            second_relay(j, side)
    pair(7, zorder[7])
    for j in (0, 1):
        first_final(j, 3)
    for side in (0, 1):
        for k in (1 - side, side):
            arrived(rows256(zgot.at[side, 3], k), rzsem.at[side, 3, k], ssem.at[0], up)
    ig[...] = (
        tme[z].astype(F32) + zgot[0, 3].astype(F32) + zgot[1, 3].astype(F32)
    ).astype(BF)
    second_final(0, gq)
    second_final(1, gv)
    out.finish()
    sent(0, kbuf)
    for u in range(4):
        sent(9 + u, sbuf.at[u // 2, u % 2])
    sent(5, dbuf)
    sent(6, lbuf)
    sent(7, obuf)
    sent(8, mbuf)


def copy_kernel(*refs):
    for source, target in zip(refs[0:4], refs[4:8]):
        target[...] = source[...]


def per_device(layer_input, qk_weight, value_weight, groups, buckets, out_cotangent):
    vm = pl.BlockSpec(memory_space=pltpu.VMEM)
    V = pltpu.VMEM
    shapes = (
        jax.ShapeDtypeStruct((512, 256), BF),
        jax.ShapeDtypeStruct((512, 256), BF),
        jax.ShapeDtypeStruct((256, 256), F32),
        jax.ShapeDtypeStruct((256, 256), F32),
    )
    results = pl.pallas_call(
        whole_kernel,
        out_shape=shapes,
        in_specs=[pl.BlockSpec(memory_space=pl.ANY)] * 4 + [vm] * 2,
        out_specs=(vm,) * 4,
        scratch_shapes=[
            V((16, 512, 256), BF),
            V((16, 2, 256, 256), BF),
            V((512, 512), BF),
            V((512, 512), BF),
            V((512, 256), BF),
            V((2, 512, 256), BF),
            V((2, 768, 512), BF),
            V((512, 1536), BF),
            V((2, 768, 768), BF),
            V((2, 768, 768), BF),
            V((2, 8, 128), F32),
            V((2, 16, 512), F32),
            V((2, 128, 512), BF),
            V((16, 8, 128), F32),
            V((16, 8, 128), F32),
            V((2, 2, 16, 48, 256), BF),
            V((2, 2, 16, 48, 256), BF),
            V((16, 2, 48, 256), BF),
            V((16, 2, 48, 256), BF),
            V((16, 2, 48, 256), BF),
            V((16, 2, 48, 256), BF),
            V((2, 2, 16, 48, 256), BF),
            V((16, 16, 128), F32),
            V((16, 16, 128), F32),
            V((16, 16, 128), F32),
            V((16, 16, 128), F32),
            V((4, 768, 128), BF),
            V((4, 768, 128), BF),
            V((4, 768, 128), BF),
            V((4, 768, 128), BF),
            V((4, 6, 128, 256), F32),
            V((4, 6, 128, 256), F32),
            V((4, 768, 128), F32),
            V((2, 768, 128), F32),
            V((2, 768, 128), BF),
            V((2, 512, 24), F32),
            V((8, 512, 256), BF),
            V((8, 512, 256), BF),
            V((8, 512, 256), BF),
            V((2, 4, 512, 256), BF),
            V((2, 4, 4, 256, 256), BF),
            V((2, 2, 4, 128, 256), BF),
            V((2, 2, 4, 256, 256), BF),
            V((2, 2, 128, 256), BF),
            V((2, 2, 256, 256), BF),
            pltpu.SemaphoreType.DMA((4,)),
            pltpu.SemaphoreType.DMA((13,)),
            pltpu.SemaphoreType.DMA((13,)),
            pltpu.SemaphoreType.DMA((176,)),
            pltpu.SemaphoreType.DMA((2, 4, 2)),
            pltpu.SemaphoreType.DMA((2, 5)),
            pltpu.SemaphoreType.DMA((2, 4)),
            pltpu.SemaphoreType.DMA((2, 4, 4)),
            pltpu.SemaphoreType.DMA((8,)),
            pltpu.SemaphoreType.DMA((2, 4, 2)),
            pltpu.SemaphoreType.DMA((2, 4, 6)),
            pltpu.SemaphoreType.DMA((2, 6)),
        ],
        compiler_params=pltpu.CompilerParams(
            collective_id=0, has_side_effects=True, vmem_limit_bytes=63 * 1024 * 1024
        ),
        name="hashed_attention_step",
    )(layer_input, qk_weight, value_weight, out_cotangent, jnp.transpose(groups, (0, 2, 1)), buckets)
    return pl.pallas_call(
        copy_kernel,
        out_shape=shapes,
        in_specs=[vm] * 4,
        out_specs=(vm,) * 4,
        name="write_results",
    )(*results)


def solution(mesh):
    return jax.shard_map(
        per_device,
        mesh=mesh,
        in_specs=(
            P("seq", "head"),
            P("seq", "head"),
            P("seq", "head"),
            P(None, "seq", None),
            P(None, "seq"),
            P("seq", "head"),
        ),
        out_specs=(P("seq", "head"), P("seq", "head"), P("seq", "head"), P("seq", "head")),
        check_vma=False,
    )
```

```python
import math

import jax
import jax.numpy as jnp
from jax import lax
from jax.experimental import pallas as pl
from jax.experimental.pallas import tpu as pltpu
from jax.sharding import PartitionSpec as P

HEAD_DIM = 128
ROUNDS = 2
EPSILON = 1e-06
SELF_SCORE = -100000.0
MASKED_SCORE = -1000000000.0


MESH = pl.DeviceIdType.MESH
BF = jnp.bfloat16
F32 = jnp.float32


def rcopy(src, dst, ssem, rsem, dev):
    return pltpu.make_async_remote_copy(
        src_ref=src, dst_ref=dst, send_sem=ssem, recv_sem=rsem, device_id=dev, device_id_type=MESH
    )


class Sends:
    def __init__(self, sems):
        self.sems, self.used, self.open = sems, 0, []

    def start(self, src, dst, rsem, dev):
        copy = rcopy(src, dst, self.sems.at[self.used], rsem, dev)
        copy.start()
        self.used += 1
        self.open.append(copy)

    def finish(self):
        for copy in self.open:
            copy.wait_send()
        self.open = []


def arrived(ref, rsem, ssem, dev):
    rcopy(ref, ref, ssem, rsem, dev).wait_recv()


def place():
    s, h = lax.axis_index("seq"), lax.axis_index("head")
    return s, h, s // 4, s % 4, h // 2, h % 2


def enter(devices):
    barrier = pltpu.get_barrier_semaphore()
    for dev in devices:
        pl.semaphore_signal(barrier, inc=1, device_id=dev, device_id_type=MESH)
    pl.semaphore_wait(barrier, len(devices))


def ring_neighbours():
    s, h, x, y, z, c = place()
    east, west = (((x + 1) % 4) * 4 + y, h), (((x + 3) % 4) * 4 + y, h)
    north, south = (x * 4 + (y + 1) % 4, h), (x * 4 + (y + 3) % 4, h)
    up, down = (s, ((z + 1) % 8) * 2 + c), (s, ((z + 7) % 8) * 2 + c)
    twin = (s, 2 * z + 1 - c)
    return east, west, north, south, up, down, twin


def mm(a, b, ca, cb):
    return lax.dot_general(a, b, (((ca,), (cb,)), ((), ())), preferred_element_type=F32)


def iota(shape, axis):
    return lax.broadcasted_iota(jnp.int32, shape, axis).astype(F32)


def onehot(mask):
    return jnp.where(mask, 1.0, 0.0).astype(BF)


def split3(v):
    high = v.astype(BF).astype(F32)
    rest = v - high
    mid = rest.astype(BF).astype(F32)
    return high, mid, rest - mid


def pieces(v):
    return jnp.concatenate(split3(v), axis=0).astype(BF)


def fold3(v, n):
    return v[0:n] + v[n:2 * n] + v[2 * n:3 * n]


def key_factor(qf):
    mean = jnp.mean(qf * qf, axis=1, keepdims=True)
    return lax.rsqrt(mean + EPSILON) * (1.0 / math.sqrt(HEAD_DIM))


def whole_kernel(
    x_ref, wq_ref, wv_ref, dout_ref, grow, brow,
    output, ig, gq, gv,
    xg, wg, dqv, dqvt, dout,
    qv, pick, unpick, order, unorder, live, hot, rk,
    kbuf, kgot, sbuf, rbuf, dbuf, dgot, obuf, ogot, ggot, lbuf, lgot, mbuf, mgot,
    qs, ks, vs, ds_, probs, pairs, osum, vals, slots, mixes,
    tme, ttwin, tgot, zgot, gsum, g1far, g1near, g2far, g2near,
    lsem, asend, arecv, ssem, zsem, tsem, w1sem, w2sem, rtsem, rzsem, s1sem, s2sem,
):
    s, h, x, y, z, c = place()
    east, west, north, south, up, down, twin = ring_neighbours()
    local = [
        pltpu.make_async_copy(x_ref, xg.at[h], lsem.at[0]),
        pltpu.make_async_copy(wq_ref, wg.at[s, 0], lsem.at[1]),
        pltpu.make_async_copy(wv_ref, wg.at[s, 1], lsem.at[2]),
        pltpu.make_async_copy(dout_ref, dout, lsem.at[3]),
    ]
    for copy in local:
        copy.start()
    barrier = pltpu.get_barrier_semaphore()

    @pl.loop(1, 16)
    def _(k):
        pl.semaphore_signal(barrier, inc=1, device_id=((s + k) % 16, h), device_id_type=MESH)

    for dev in (up, down, twin):
        pl.semaphore_signal(barrier, inc=1, device_id=dev, device_id_type=MESH)
    pl.semaphore_wait(barrier, 18)
    out = Sends(ssem)

    def rows256(ref, k):
        return ref.at[pl.ds(256 * k, 256)]

    def post(n, src, dst):
        @pl.loop(1, 16)
        def _(k):
            d = (s + k) % 16
            rcopy(src.at[d], dst.at[s], asend.at[n], arecv.at[n], (d, h)).start()

        dst[s] = src[s]

    def collect(n, dst):
        part = dst.at[pl.ds(0, 15)]
        rcopy(part, part, asend.at[n], arecv.at[n], (s, h)).wait_recv()

    def sent(n, src):
        part = src.at[pl.ds(0, 15)]
        rcopy(part, part, asend.at[n], arecv.at[n], (s, h)).wait_send()

    first_axis = [(north, south), (east, west)]
    second_axis = [(east, west), (north, south)]
    prim, sec = [y, x], [x, y]
    own = [wq_ref, wv_ref]

    def wslot(j, p, r):
        return wg.at[r * 4 + p if j == 0 else p * 4 + r, j]

    def half(ref, k):
        return ref.at[pl.ds(128 * k, 128)]

    for j in (0, 1):
        plus, minus = first_axis[j]
        dst = wslot(j, prim[j], sec[j])
        out.start(own[j], dst, w1sem.at[j, 0], plus)
        out.start(own[j], dst, w1sem.at[j, 1], minus)
    for k in (0, 1):
        rows = pl.ds(256 * k, 256)
        out.start(x_ref.at[rows], xg.at[h, rows], zsem.at[0, 0, k], up)
        out.start(x_ref.at[rows], xg.at[h, rows], zsem.at[1, 0, k], down)

    def second_send(j, k, p, src):
        plus, minus = second_axis[j]
        dst = wslot(j, p, sec[j])
        out.start(src, dst, w2sem.at[j, k, 0], plus)
        out.start(src, dst, w2sem.at[j, k, 1], minus)

    for j in (0, 1):
        second_send(j, 0, prim[j], own[j])
    out.start(x_ref, xg.at[h], tsem.at[0, 0], twin)

    def first_arrivals(j):
        plus, minus = first_axis[j]
        for k, (step, onward) in enumerate(((3, plus), (1, minus))):
            p = (prim[j] + step) % 4
            ref = wslot(j, p, sec[j])
            arrived(ref, w1sem.at[j, k], ssem.at[0], plus)
            out.start(half(ref, k), half(ref, k), w1sem.at[j, 2 + k], onward)
            second_send(j, 1 + k, p, ref)

    def first_far(j):
        p = (prim[j] + 2) % 4
        ref = wslot(j, p, sec[j])
        for k in (0, 1):
            arrived(half(ref, k), w1sem.at[j, 2 + k], ssem.at[0], first_axis[j][0])
        second_send(j, 3, p, ref)

    offsets = (0, 3, 1, 2)

    def second_arrivals(j, k):
        p = (prim[j] + offsets[k]) % 4
        plus, minus = second_axis[j]
        for side, (step, onward) in enumerate(((3, plus), (1, minus))):
            ref = wslot(j, p, (sec[j] + step) % 4)
            arrived(ref, w2sem.at[j, k, side], ssem.at[0], plus)
            out.start(half(ref, side), half(ref, side), w2sem.at[j, k, 2 + side], onward)

    def second_far(j, k):
        p = (prim[j] + offsets[k]) % 4
        ref = wslot(j, p, (sec[j] + 2) % 4)
        for side in (0, 1):
            arrived(half(ref, side), w2sem.at[j, k, 2 + side], ssem.at[0], second_axis[j][0])

    def z_arrival(dist):
        for k in (0, 1):
            for side, (step, onward) in enumerate(((8 - dist, up), (dist, down))):
                ref = rows256(xg.at[((z + step) % 8) * 2 + c], k)
                arrived(ref, zsem.at[side, dist - 1, k], ssem.at[0], up)
                if dist < 3 or k == side:
                    out.start(ref, ref, zsem.at[side, dist, k], onward)
        for side, step in enumerate((8 - dist, dist)):
            ref = xg.at[((z + step) % 8) * 2 + c]
            out.start(ref, ref, tsem.at[side, dist], twin)

    def z_far():
        ref = xg.at[((z + 4) % 8) * 2 + c]
        for side in (0, 1):
            arrived(rows256(ref, side), zsem.at[side, 3, side], ssem.at[0], up)
            out.start(rows256(ref, side), rows256(ref, side), tsem.at[side, 4], twin)

    def twin_arrivals():
        arrived(xg.at[2 * z + 1 - c], tsem.at[0, 0], ssem.at[0], twin)
        for dist in (1, 2, 3):
            for side, step in enumerate((8 - dist, dist)):
                arrived(xg.at[((z + step) % 8) * 2 + 1 - c], tsem.at[side, dist], ssem.at[0], twin)

    def twin_far():
        for side in (0, 1):
            ref = xg.at[((z + 4) % 8) * 2 + 1 - c]
            arrived(rows256(ref, side), tsem.at[side, 4], ssem.at[0], twin)


    kbuf[...] = jnp.zeros_like(kbuf)
    lbuf[...] = jnp.zeros_like(lbuf)
    vals[...] = jnp.zeros_like(vals)
    slots[...] = jnp.zeros_like(slots)
    upper = onehot(iota((512, 512), 0) <= iota((512, 512), 1))
    eye = iota((512, 512), 0) == iota((512, 512), 1)
    for j in (0, 1):
        probs[j, 0:4] = jnp.zeros((4, 128, 256), F32)
    slot_rows, slot_cols = [], []

    def token_layout(t):
        g = grow[t].astype(F32)
        member = jnp.where(iota((16, 512), 0) == g, 1.0, 0.0)
        count = mm(member.astype(BF), upper, 1, 0)
        rank = jnp.sum(member * count, axis=0, keepdims=True) - 1.0
        slot = g * 48.0 + rank
        slot_col = jnp.sum(jnp.where(eye, slot, 0.0), axis=1, keepdims=True)
        hot[t] = member
        rk[t] = onehot(iota((128, 512), 0) == rank)
        slot_rows.append(slot)
        slot_cols.append(slot_col)
        named = member * (brow[t:t + 1, :].astype(F32) + 1.0)
        sent_keys = mm(named.astype(BF), rk[t], 1, 1)
        for d in range(16):
            kbuf[d, t:t + 1, :] = sent_keys[d:d + 1, :]
    token_layout(0)

    def slot_order(t):
        tag = jnp.concatenate([kgot[d, t:t + 1, :] for d in range(16)], axis=0)
        usable = iota((16, 128), 1) < 48.0
        kinds = [jnp.where(tag == float(k), 1.0, 0.0) for k in range(1, 9)]
        kinds.append(jnp.where(usable, jnp.where(tag == 0.0, 1.0, 0.0), 0.0))
        stack = jnp.concatenate(kinds, axis=0)
        within = mm(stack.astype(BF), onehot(iota((128, 128), 0) <= iota((128, 128), 1)), 1, 0)
        totals = jnp.broadcast_to(within[:, 127:128], (144, 128)).astype(BF)
        before = mm(onehot(iota((144, 144), 0) > iota((144, 144), 1)), totals, 1, 0)
        place_all = stack * (within + before - 1.0)
        rank = place_all[0:16]
        for k in range(1, 9):
            rank = rank + place_all[16 * k:16 * (k + 1)]
        live[t] = before[128:136, :]
        small_eye = iota((48, 128), 0) == iota((48, 128), 1)
        columns = jnp.concatenate(
            [
                jnp.sum(jnp.where(small_eye, rank[d:d + 1, :], 0.0), axis=1, keepdims=True)
                for d in range(16)
            ],
            axis=0,
        )
        unorder[t] = onehot(iota((768, 768), 1) == columns)
        row = jnp.sum(
            jnp.where(iota((768, 768), 0) == iota((768, 768), 1), columns, 0.0),
            axis=0, keepdims=True,
        )
        order[t] = onehot(iota((768, 768), 0) == row)

    for j in (0, 1):
        first_arrivals(j)
    token_layout(1)
    post(0, kbuf, kgot)
    for j in (0, 1):
        second_arrivals(j, 0)
    z_arrival(1)
    pick[0] = onehot(iota((768, 512), 0) == slot_rows[0])
    for j in (0, 1):
        first_far(j)
    for j in (0, 1):
        second_arrivals(j, 1)
    z_arrival(2)
    pick[1] = onehot(iota((768, 512), 0) == slot_rows[1])
    for copy in local:
        copy.wait()
    for t in (0, 1):
        dbuf[:, t] = mm(pick[t], dout[...], 1, 0).astype(BF).reshape(16, 48, 256)

    for t in (0, 1):
        unpick[:, 768 * t:768 * (t + 1)] = onehot(iota((512, 768), 1) == slot_cols[t])
    for j in (0, 1):
        second_arrivals(j, 2)
    z_arrival(3)
    collect(0, kgot)
    slot_order(0)
    for j in (0, 1):
        second_arrivals(j, 3)
    post(5, dbuf, dgot)
    z_far()
    slot_order(1)
    for k in range(4):
        second_far(0, k)
        second_far(1, k)
    twin_arrivals()

    def project(q):
        chip = (z + 5 + q) % 8
        for j in (0, 1):
            total = mm(xg[2 * chip], wg[2 * chip, j], 1, 0)
            total += mm(xg[2 * chip + 1], wg[2 * chip + 1, j], 1, 0)
            probs[j, 0:4] += total.reshape(4, 128, 256)

    @pl.loop(0, 7)
    def _(q):
        project(q)

    twin_far()
    project(7)
    for j in (0, 1):
        for n in (0, 1):
            part = probs[j, 0:4, :, 128 * n:128 * (n + 1)].reshape(512, 128)
            qv[n, :, 128 * j:128 * (j + 1)] = part.astype(BF)

    for n in (0, 1):
        for t in (0, 1):
            sbuf[n, t] = mm(pick[t], qv[n], 1, 0).astype(BF).reshape(16, 48, 256)
            post(1 + 2 * n + t, sbuf.at[n, t], rbuf.at[n, t])
    def both(ref, lead, b):
        prev = (b + 5) % 6
        return jnp.concatenate(
            [ref[lead, 128 * b:128 * (b + 1)], ref[lead, 128 * prev:128 * (prev + 1)]], axis=0
        )

    self_pair = iota((128, 256), 0) == iota((128, 256), 1)

    collect(5, dgot)

    @pl.loop(0, 2)
    def _(t):
        rows = mm(order[t], dgot[:, t].reshape(768, 256), 1, 0).astype(BF)
        ds_[t] = rows[:, 0:128]
        ds_[2 + t] = rows[:, 128:256]

    choose = onehot(iota((8, 128), 0) == iota((8, 128), 1))

    for n in (0, 1):

        @pl.loop(0, 2)
        def _(t):
            u = 2 * n + t
            collect(1 + u, rbuf.at[n, t])
            rows = mm(order[t], rbuf[n, t].reshape(768, 256), 1, 0)
            qf = rows[:, 0:128]
            fac = key_factor(qf)
            qs[u] = qf.astype(BF)
            ks[u] = (qf * fac).astype(BF)
            vs[u] = rows[:, 128:256].astype(BF)
            used = jnp.concatenate([live[t, 0:1, :]] * 2, axis=1)
            parts = []
            for b in range(6):
                prev = (b + 5) % 6
                at = iota((1, 256), 1)
                at = jnp.where(at < 128.0, at + 128.0 * b, at - 128.0 + 128.0 * prev)
                part = mm(qs[u, 128 * b:128 * (b + 1)], both(ks, u, b), 1, 1)
                part = jnp.where(self_pair, SELF_SCORE, part)
                parts.append(jnp.where(at < used, part, MASKED_SCORE))
                pairs[u, b] = mm(ds_[u, 128 * b:128 * (b + 1)], both(vs, u, b), 1, 1)
            scores = jnp.concatenate(parts, axis=0)
            top = jnp.max(scores, axis=1, keepdims=True)
            e = jnp.exp(scores - top)
            total = jnp.sum(e, axis=1, keepdims=True)
            weights = e * (1.0 / total)
            probs[u] = weights.reshape(6, 128, 256)
            packed = weights.astype(BF)
            mixed = jnp.concatenate(
                [mm(packed[128 * b:128 * (b + 1)], both(vs, u, b), 1, 0) for b in range(6)], axis=0
            )
            osum[u] = mixed
            vals[t, :, n:n + 1] = top + jnp.log(total)
            vals[t, :, 2 + n:3 + n] = jnp.sum(ds_[u].astype(F32) * mixed, axis=1, keepdims=True)
            if n == 1:
                high, mid, low = split3(vals[t])
                lines = pieces(
                    mm(choose, high.astype(BF), 1, 1)
                    + mm(choose, mid.astype(BF), 1, 1)
                    + mm(choose, low.astype(BF), 1, 1)
                )
                placed = fold3(mm(lines, order[t], 1, 0), 8)
                for d in range(16):
                    lbuf[d, pl.ds(pl.multiple_of(8 * t, 8), 8), 0:48] = placed[
                        :, 48 * d:48 * (d + 1)
                    ]

    post(6, lbuf, lgot)
    for t in (0, 1):
        wide = jnp.concatenate([osum[t], osum[2 + t]], axis=1).astype(BF)
        obuf[:, t] = mm(unorder[t], wide, 1, 0).astype(BF).reshape(16, 48, 256)
    collect(6, lgot)
    here = []
    for t in (0, 1):
        high, mid, low = split3(lgot[:, 8 * t:8 * (t + 1), :].reshape(128, 128))
        found = (
            mm(high.astype(BF), rk[t], 1, 0)
            + mm(mid.astype(BF), rk[t], 1, 0)
            + mm(low.astype(BF), rk[t], 1, 0)
        )
        line = found[0:8] * hot[t, 0:1, :]
        for g in range(1, 16):
            line = line + found[8 * g:8 * (g + 1)] * hot[t, g:g + 1, :]
        here.append(line)
    top = jnp.maximum(here[0], here[1])
    log_all = top + jnp.log(jnp.exp(here[0] - top) + jnp.exp(here[1] - top))
    mix = [jnp.exp(line - log_all) for line in here]
    inner = mix[0][0:2] * here[0][2:4] + mix[1][0:2] * here[1][2:4]
    mix_lines = []
    for t in (0, 1):
        lines = jnp.concatenate([mix[t][0:2], inner, jnp.zeros((4, 512), F32)], axis=0)
        split = jnp.concatenate(split3(lines), axis=0)
        stack = jnp.concatenate([split * hot[t, g:g + 1, :] for g in range(16)], axis=0)
        back = mm(stack.astype(BF), rk[t], 1, 1)
        for g in range(16):
            mbuf[g, 8 * t:8 * (t + 1), :] = fold3(back[24 * g:24 * (g + 1)], 8)
        mix_lines.append(split)
    post(8, mbuf, mgot)
    post(7, obuf, ogot)
    for t in (0, 1):
        mixes[t] = mm(onehot(eye), mix_lines[t].astype(BF), 1, 1)

    collect(8, mgot)
    lane_eye = onehot(iota((48, 128), 0) == iota((48, 128), 1))
    for t in (0, 1):
        for d in range(16):
            slots[t, 48 * d:48 * (d + 1), 0:24] = mm(
                lane_eye, pieces(mgot[d, 8 * t:8 * (t + 1), :]), 1, 1
            ).astype(BF)
        vals[t] = mm(order[t], slots[t], 1, 0)

    def column(ref, t, j):
        return ref[t, :, j:j + 1] + ref[t, :, 8 + j:9 + j] + ref[t, :, 16 + j:17 + j]

    for n in (0, 1):

        @pl.loop(0, 2)
        def _(t):
            u = 2 * n + t
            sent(1 + u, sbuf.at[n, t])
            mix_col = column(vals, t, n)
            inner_col = column(vals, t, 2 + n)
            weighted = probs[u].reshape(768, 256) * mix_col
            grads = weighted * (pairs[u].reshape(768, 256) - inner_col)
            self_all = jnp.concatenate([jnp.where(self_pair, 0.0, 1.0)] * 6, axis=0)
            grads = jnp.where(self_all == 0.0, 0.0, grads).astype(BF)
            weighted = weighted.astype(BF)
            blocks = [slice(128 * b, 128 * (b + 1)) for b in range(6)]
            dq = [mm(grads[blocks[b]], both(ks, u, b), 1, 0) for b in range(6)]
            dk = [mm(grads[blocks[b]], qs[u, blocks[b]], 0, 0) for b in range(6)]
            dv = [mm(weighted[blocks[b]], ds_[u, blocks[b]], 0, 0) for b in range(6)]

            def folded(grad):
                return jnp.concatenate(
                    [grad[b][0:128] + grad[(b + 1) % 6][128:256] for b in range(6)], axis=0
                )

            qf = qs[u].astype(F32)
            fac = key_factor(qf)
            dk = folded(dk)
            inside = jnp.sum(dk * qf, axis=1, keepdims=True)
            result = jnp.concatenate(dq, axis=0) + fac * dk - fac * fac * fac * inside * qf
            wide = jnp.concatenate([result.astype(BF), folded(dv).astype(BF)], axis=1)
            sbuf[n, t] = mm(unorder[t], wide, 1, 0).astype(BF).reshape(16, 48, 256)
            post(9 + u, sbuf.at[n, t], ggot.at[n, t])

    collect(7, ogot)
    parts = [mm(unpick[:, 768 * t:768 * (t + 1)], ogot[:, t].reshape(768, 256), 1, 0) for t in (0, 1)]
    for n in (0, 1):
        lanes = slice(128 * n, 128 * (n + 1))
        output[:, lanes] = (
            column(mixes, 0, n) * parts[0][:, lanes] + column(mixes, 1, n) * parts[1][:, lanes]
        ).astype(BF)

    for n in (0, 1):
        collect(9 + 2 * n, ggot.at[n, 0])
        rows = mm(unpick[:, 0:768], ggot[n, 0].reshape(768, 256), 1, 0)
        collect(10 + 2 * n, ggot.at[n, 1])
        rows = rows + mm(unpick[:, 768:1536], ggot[n, 1].reshape(768, 256), 1, 0)
        rows = rows.astype(BF)
        dqv[:, 128 * n:128 * (n + 1)] = rows[:, 0:128]
        dqv[:, 256 + 128 * n:256 + 128 * (n + 1)] = rows[:, 128:256]
        dqvt[128 * n:128 * (n + 1), :] = jnp.transpose(rows[:, 0:128])
        dqvt[256 + 128 * n:256 + 128 * (n + 1), :] = jnp.transpose(rows[:, 128:256])

    def term(b):
        return mm(dqv[:, 0:256], wg[b, 0], 1, 1) + mm(dqv[:, 256:512], wg[b, 1], 1, 1)

    def twin_term(k, zd):
        ttwin[zd] = term(2 * zd + 1 - c).astype(BF)
        out.start(ttwin.at[zd], tgot.at[zd], rtsem.at[k], twin)

    def my_term(zd):
        tme[zd] = term(2 * zd + c).astype(BF)

    def pair(k, zd):
        arrived(tgot.at[zd], rtsem.at[k], ssem.at[0], twin)
        tme[zd] = (tme[zd].astype(F32) + tgot[zd].astype(F32)).astype(BF)

    prim, sec = [x, y], [y, x]
    first_axis = [(east, west), (north, south)]
    second_axis = [(north, south), (east, west)]

    def grads(j, off):
        p = (sec[j] + off) % 4

        @pl.loop(0, 2)
        def _(i):
            r = (prim[j] + 2 * i + 1) % 4
            b = r * 4 + p if j == 0 else p * 4 + r
            gsum[j, r, p] = mm(dqvt[256 * j:256 * (j + 1), :], xg[b], 1, 0).astype(BF)

    def own_grads(j):
        @pl.loop(0, 4)
        def _(p):
            r = prim[j]
            b = r * 4 + p if j == 0 else p * 4 + r
            gsum[j, r, p] = mm(dqvt[256 * j:256 * (j + 1), :], xg[b], 1, 0).astype(BF)

    offs = (2, 1, 3, 0)

    def add(ref, index, other):
        ref[index] = (ref[index].astype(F32) + other.astype(F32)).astype(BF)

    def first_far_sends(j, k):
        p = (sec[j] + offs[k]) % 4
        r = (prim[j] + 2) % 4
        b = r * 4 + p if j == 0 else p * 4 + r
        gsum[j, r, p] = mm(dqvt[256 * j:256 * (j + 1), :], xg[b], 1, 0).astype(BF)
        for side in (0, 1):
            out.start(
                half(gsum.at[j, r, p], side), g1far.at[j, side, p], s1sem.at[j, k, side],
                first_axis[j][side],
            )

    def first_sends(j, k):
        p = (sec[j] + offs[k]) % 4
        for side, step in enumerate((1, 3)):
            r = (prim[j] + step) % 4
            out.start(
                half(gsum.at[j, r, p], 1 - side), half(g1near.at[j, side, p], 1 - side),
                s1sem.at[j, k, 2 + side], first_axis[j][side],
            )

    def first_relay(j, k):
        p = (sec[j] + offs[k]) % 4
        for side, step in enumerate((1, 3)):
            r = (prim[j] + step) % 4
            arrived(g1far.at[j, side, p], s1sem.at[j, k, side], ssem.at[0], first_axis[j][0])
            add(gsum, (j, r, p, pl.ds(128 * side, 128)), g1far[j, side, p])
            out.start(
                half(gsum.at[j, r, p], side), half(g1near.at[j, side, p], side),
                s1sem.at[j, k, 4 + side], first_axis[j][side],
            )

    def first_final(j, k):
        p = (sec[j] + offs[k]) % 4
        for side in (0, 1):
            near = g1near.at[j, side, p]
            arrived(half(near, 1 - side), s1sem.at[j, k, 2 + side], ssem.at[0], first_axis[j][0])
            arrived(half(near, side), s1sem.at[j, k, 4 + side], ssem.at[0], first_axis[j][0])
        r = prim[j]
        gsum[j, r, p] = (
            gsum[j, r, p].astype(F32) + g1near[j, 0, p].astype(F32) + g1near[j, 1, p].astype(F32)
        ).astype(BF)

    def second_far_send(j):
        p = (sec[j] + 2) % 4
        for side in (0, 1):
            out.start(
                half(gsum.at[j, prim[j], p], side), g2far.at[j, side], s2sem.at[j, side],
                second_axis[j][side],
            )

    def second_fresh(j, side):
        p = (sec[j] + (1, 3)[side]) % 4
        out.start(
            half(gsum.at[j, prim[j], p], 1 - side), half(g2near.at[j, side], 1 - side),
            s2sem.at[j, 2 + side], second_axis[j][side],
        )

    def second_relay(j, side):
        p = (sec[j] + (1, 3)[side]) % 4
        arrived(g2far.at[j, side], s2sem.at[j, side], ssem.at[0], second_axis[j][0])
        add(gsum, (j, prim[j], p, pl.ds(128 * side, 128)), g2far[j, side])
        out.start(
            half(gsum.at[j, prim[j], p], side), half(g2near.at[j, side], side),
            s2sem.at[j, 4 + side], second_axis[j][side],
        )

    def second_final(j, result):
        for side in (0, 1):
            near = g2near.at[j, side]
            arrived(half(near, 1 - side), s2sem.at[j, 2 + side], ssem.at[0], second_axis[j][0])
            arrived(half(near, side), s2sem.at[j, 4 + side], ssem.at[0], second_axis[j][0])
        result[...] = jnp.transpose(
            gsum[j, prim[j], sec[j]].astype(F32)
            + g2near[j, 0].astype(F32)
            + g2near[j, 1].astype(F32)
        )

    def z_start(side, step, k):
        zd = (z + 4 - step) % 8 if side == 0 else (z + 4 + step) % 8
        out.start(
            rows256(tme.at[zd], k), rows256(zgot.at[side, step], k), rzsem.at[side, step, k],
            (up, down)[side],
        )

    def z_relay(step, own):
        for side in (0, 1):
            k = side if own else 1 - side
            zd = (z + 4 - step) % 8 if side == 0 else (z + 4 + step) % 8
            rows = pl.ds(256 * k, 256)
            arrived(zgot.at[side, step - 1, rows], rzsem.at[side, step - 1, k], ssem.at[0], up)
            add(tme, (zd, rows), zgot[side, step - 1, rows])
            z_start(side, step, k)

    zorder = [(z + off) % 8 for off in (4, 3, 5, 2, 6, 1, 7, 0)]

    def both_terms(k):
        twin_term(k, zorder[k])
        my_term(zorder[k])

    twin_term(0, zorder[0])
    for j in (0, 1):
        first_far_sends(j, 0)
    for j in (0, 1):
        grads(j, offs[0])
        first_sends(j, 0)
    my_term(zorder[0])
    both_terms(1)
    both_terms(2)
    pair(0, zorder[0])
    for side in (0, 1):
        z_start(side, 0, side)
    for j in (0, 1):
        first_far_sends(j, 1)
        grads(j, offs[1])
        first_sends(j, 1)
    pair(1, zorder[1])
    pair(2, zorder[2])
    for side in (0, 1):
        z_start(side, 1, 1 - side)
    for k in (2, 3):
        for j in (0, 1):
            first_far_sends(j, k)
            grads(j, offs[k])
            first_sends(j, k)
    both_terms(3)
    both_terms(4)
    for j in (0, 1):
        first_relay(j, 0)
    z_relay(1, True)
    for j in (0, 1):
        first_relay(j, 1)
        own_grads(j)
    both_terms(5)
    both_terms(6)
    pair(3, zorder[3])
    pair(4, zorder[4])
    z_relay(2, False)
    for j in (0, 1):
        first_relay(j, 2)
        first_relay(j, 3)
    both_terms(7)
    z_relay(2, True)
    for j in (0, 1):
        first_final(j, 0)
        second_far_send(j)
    pair(5, zorder[5])
    pair(6, zorder[6])
    z_relay(3, False)
    for side in (0, 1):
        for j in (0, 1):
            first_final(j, 1 + side)
            second_fresh(j, side)
    z_relay(3, True)
    for j in (0, 1):
        for side in (0, 1):
            second_relay(j, side)
    pair(7, zorder[7])
    for j in (0, 1):
        first_final(j, 3)
    for side in (0, 1):
        for k in (1 - side, side):
            arrived(rows256(zgot.at[side, 3], k), rzsem.at[side, 3, k], ssem.at[0], up)
    ig[...] = (
        tme[z].astype(F32) + zgot[0, 3].astype(F32) + zgot[1, 3].astype(F32)
    ).astype(BF)
    second_final(0, gq)
    second_final(1, gv)
    out.finish()
    sent(0, kbuf)
    for u in range(4):
        sent(9 + u, sbuf.at[u // 2, u % 2])
    sent(5, dbuf)
    sent(6, lbuf)
    sent(7, obuf)
    sent(8, mbuf)


def copy_kernel(*refs):
    for source, target in zip(refs[0:4], refs[4:8]):
        target[...] = source[...]


def per_device(layer_input, qk_weight, value_weight, groups, buckets, out_cotangent):
    vm = pl.BlockSpec(memory_space=pltpu.VMEM)
    V = pltpu.VMEM
    shapes = (
        jax.ShapeDtypeStruct((512, 256), BF),
        jax.ShapeDtypeStruct((512, 256), BF),
        jax.ShapeDtypeStruct((256, 256), F32),
        jax.ShapeDtypeStruct((256, 256), F32),
    )
    results = pl.pallas_call(
        whole_kernel,
        out_shape=shapes,
        in_specs=[pl.BlockSpec(memory_space=pl.ANY)] * 4 + [vm] * 2,
        out_specs=(vm,) * 4,
        scratch_shapes=[
            V((16, 512, 256), BF),
            V((16, 2, 256, 256), BF),
            V((512, 512), BF),
            V((512, 512), BF),
            V((512, 256), BF),
            V((2, 512, 256), BF),
            V((2, 768, 512), BF),
            V((512, 1536), BF),
            V((2, 768, 768), BF),
            V((2, 768, 768), BF),
            V((2, 8, 128), F32),
            V((2, 16, 512), F32),
            V((2, 128, 512), BF),
            V((16, 8, 128), F32),
            V((16, 8, 128), F32),
            V((2, 2, 16, 48, 256), BF),
            V((2, 2, 16, 48, 256), BF),
            V((16, 2, 48, 256), BF),
            V((16, 2, 48, 256), BF),
            V((16, 2, 48, 256), BF),
            V((16, 2, 48, 256), BF),
            V((2, 2, 16, 48, 256), BF),
            V((16, 16, 128), F32),
            V((16, 16, 128), F32),
            V((16, 16, 128), F32),
            V((16, 16, 128), F32),
            V((4, 768, 128), BF),
            V((4, 768, 128), BF),
            V((4, 768, 128), BF),
            V((4, 768, 128), BF),
            V((4, 6, 128, 256), F32),
            V((4, 6, 128, 256), F32),
            V((4, 768, 128), F32),
            V((2, 768, 128), F32),
            V((2, 768, 128), BF),
            V((2, 512, 24), F32),
            V((8, 512, 256), BF),
            V((8, 512, 256), BF),
            V((8, 512, 256), BF),
            V((2, 4, 512, 256), BF),
            V((2, 4, 4, 256, 256), BF),
            V((2, 2, 4, 128, 256), BF),
            V((2, 2, 4, 256, 256), BF),
            V((2, 2, 128, 256), BF),
            V((2, 2, 256, 256), BF),
            pltpu.SemaphoreType.DMA((4,)),
            pltpu.SemaphoreType.DMA((13,)),
            pltpu.SemaphoreType.DMA((13,)),
            pltpu.SemaphoreType.DMA((176,)),
            pltpu.SemaphoreType.DMA((2, 4, 2)),
            pltpu.SemaphoreType.DMA((2, 5)),
            pltpu.SemaphoreType.DMA((2, 4)),
            pltpu.SemaphoreType.DMA((2, 4, 4)),
            pltpu.SemaphoreType.DMA((8,)),
            pltpu.SemaphoreType.DMA((2, 4, 2)),
            pltpu.SemaphoreType.DMA((2, 4, 6)),
            pltpu.SemaphoreType.DMA((2, 6)),
        ],
        compiler_params=pltpu.CompilerParams(
            collective_id=0, has_side_effects=True, vmem_limit_bytes=63 * 1024 * 1024
        ),
        name="hashed_attention_step",
    )(layer_input, qk_weight, value_weight, out_cotangent, jnp.transpose(groups, (0, 2, 1)), buckets)
    return pl.pallas_call(
        copy_kernel,
        out_shape=shapes,
        in_specs=[vm] * 4,
        out_specs=(vm,) * 4,
        name="write_results",
    )(*results)


def solution(mesh):
    return jax.shard_map(
        per_device,
        mesh=mesh,
        in_specs=(
            P("seq", "head"),
            P("seq", "head"),
            P("seq", "head"),
            P(None, "seq", None),
            P(None, "seq"),
            P("seq", "head"),
        ),
        out_specs=(P("seq", "head"), P("seq", "head"), P("seq", "head"), P("seq", "head")),
        check_vma=False,
    )
```
